128 devices in a mesh: gx: 32 (over y, z, x_hi), gy: 4 (over x_lo, core).
Axes of the slice: x: 4 (x_hi: 2, x_lo: 2; x = x_hi * 2 + x_lo), y: 4, z: 4, core: 2. Of those that a mesh axis runs over, the one named last changes fastest.
Arguments:
- density: bfloat16 [32, 4, 3, 20, 128, 128], P('gx', 'gy'), may hold values from -0.3 to 0.8
- neighbours: int32 [32, 4, 3, 20], replicated, may hold values from 0 to 383, as said below
- ent_blocks: bfloat16 [12288, 128, 128], P(('gx', 'gy')), may hold values from -0.59765625 to 0.59765625
- ent_owner: int32 [12288], replicated, may hold values from 0 to 127, as said below
- ent_place: int32 [12288], replicated, may hold values from 0 to 59
Outputs:
- purified: float32 [32, 4, 3, 20, 128, 128], P('gx', 'gy')
The draws below stay inside these ranges and needn't reach their ends.
Inputs may be any that keep to these rules, and one draw needn't show every extreme that they name: neighbours[x, y, r, 0] is the row's own index (x * 4 + y) * 3 + r; the other 19 entries of a row are distinct rows of devices (x + a mod 32, y + b mod 4) with a and b in -1, 0, 1. `ent_owner`: among the 96 entries d * 96 to d * 96 + 95 of one device d, no owner is named more than 2 times, and some owner exactly 2 times.
All inputs are finite; a program needn't handle non-finite values.
Results may differ from the reference program's by a relative error of at most 0.0059.
Values may be sent and summed in bfloat16 or wider, within the bound.
No kernel may reach another device: no remote copies, remote signals or barrier semaphores. Data moves between devices by JAX's collectives and lax.ppermute only.
A program may use at most 128 MiB of HBM per device.

```python
import jax
import jax.numpy as jnp
from jax import lax

B = 128
K = 20
R = 3
C = 2
SLAB_X = 32
SLAB_Y = 4
NDEV = 128
E = 96


def draw_density(key, part):
    shape_all = (SLAB_X, SLAB_Y, R, K, B, B)
    orbital_ids = jnp.arange(B, dtype=jnp.int32)
    unit_diag = (orbital_ids[:, None] == orbital_ids[None, :]).astype(jnp.float32)
    slot_ids = jnp.arange(K, dtype=jnp.int32)
    own_slot = (slot_ids == 0).astype(jnp.float32)
    base_part = 0.5 * own_slot[None, None, None, :, None, None] * unit_diag[None, None, None, None, :, :]
    noise_part = 0.05 * jnp.clip(jax.random.normal(key, shape_all, jnp.float32), -6.0, 6.0)
    return (base_part + noise_part).astype(jnp.bfloat16)


def draw_neighbours(key, part):
    total_rows = NDEV * R
    candidates = 9 * R
    global_ids = jnp.arange(total_rows, dtype=jnp.int32)
    home_x = global_ids // (SLAB_Y * R)
    home_y = global_ids // R % SLAB_Y
    home_r = global_ids % R
    row_keys = jax.random.split(key, total_rows)

    def shuffled(row_key):
        return jax.random.permutation(row_key, candidates - 1)
    choices_made = jax.vmap(shuffled)(row_keys)[:, :K - 1].astype(jnp.int32)
    self_slot = 4 * R + home_r
    picked = jnp.where(choices_made >= self_slot[:, None], choices_made + 1, choices_made)
    near_device = picked // R
    near_row = picked % R
    delta_x = near_device // 3 - 1
    delta_y = near_device % 3 - 1
    column_x = (home_x[:, None] + delta_x) % SLAB_X
    column_y = (home_y[:, None] + delta_y) % SLAB_Y
    columns = (column_x * SLAB_Y + column_y) * R + near_row
    joined = jnp.concatenate([global_ids[:, None], columns], axis=1)
    return joined.reshape(SLAB_X, SLAB_Y, R, K).astype(jnp.int32)


def draw_ent_owner(key, part):
    hot_owner = jax.random.randint(jax.random.fold_in(key, 7), (), 0, NDEV)
    source_keys = jax.random.split(jax.random.fold_in(key, 11), NDEV)

    def one_source(source_key):
        first_key, second_key = jax.random.split(source_key)
        others = jax.random.permutation(first_key, (NDEV - 1) * C)[:E - C] + C
        values = jnp.concatenate([jnp.arange(C, dtype=jnp.int32), others.astype(jnp.int32)])
        order = jax.random.permutation(second_key, E)
        values = values[order]
        return (values // C + hot_owner) % NDEV
    return jax.vmap(one_source)(source_keys).reshape(-1).astype(jnp.int32)


def place_ends(entries, own_key, smallest, high):
    extent = entries.shape
    spot = [jax.random.randint(jax.random.fold_in(own_key, axis), (), 0, extent[axis]) for axis in range(len(extent))]
    entries = entries.at[tuple(spot)].set(smallest)
    longest = extent.index(max(extent))
    spot[longest] = (spot[longest] + 1) % extent[longest]
    return entries.at[tuple(spot)].set(high)


def levels(stream_key, dims, cuts, low, high):
    gain, own = 1.0, jax.random.fold_in(stream_key, 6)
    for dim, shards_of in cuts:
        draws = jnp.exp(jax.random.uniform(jax.random.fold_in(own, dim), (shards_of,), jnp.float32, low / len(cuts), high / len(cuts)))
        gain = gain * jnp.repeat(draws, dims[dim] // shards_of).reshape([-1 if axis == dim else 1 for axis in range(len(dims))])
    return gain


def centred(own_key, shape, deviation, most, pieces=(), held_as=jnp.bfloat16):
    values = deviation * jax.random.normal(own_key, shape, jnp.float32)
    if pieces:
        values = values * levels(own_key, shape, pieces, -0.22, 0.18)
    return jnp.clip(values, -most, most).astype(held_as)


def setup_inputs(seed: int = 0) -> dict:
    splits = jax.random.split(jax.random.key(seed), 6)
    density = draw_density(jax.random.fold_in(splits[5], 71), 0)
    neighbours = draw_neighbours(jax.random.fold_in(splits[5], 71), 0)
    ent_blocks = centred(splits[2], (NDEV * E, B, B), 0.1, 0.59765625, ((0, 128),))
    ent_owner = draw_ent_owner(jax.random.fold_in(splits[5], 71), 0)
    ent_place = place_ends(jax.random.randint(splits[4], (NDEV * E,), 0, R * K), jax.random.fold_in(splits[4], 1), 0, (R * K) - 1).astype(jnp.int32)
    return dict(density=density, neighbours=neighbours, ent_blocks=ent_blocks, ent_owner=ent_owner, ent_place=ent_place)


def block_positions(neighbours, here_x, here_y, row_columns):
    wide_count, narrow_count, row_count, slot_count = neighbours.shape
    listing = neighbours.reshape(wide_count * narrow_count * row_count, slot_count)
    inner_lists = jnp.take(listing, row_columns, axis=0)
    matches = inner_lists[:, None, :] == row_columns[None, :, None]
    present = jnp.any(matches, axis=2)
    slot_ids = jnp.arange(slot_count, dtype=jnp.int32)
    inner_slot = jnp.sum(jnp.where(matches, slot_ids[None, None, :], 0), axis=2).astype(jnp.int32)
    inner_x = row_columns // (narrow_count * row_count)
    inner_y = (row_columns // row_count) % narrow_count
    inner_r = row_columns % row_count
    near_x = (inner_x - here_x + 1) % wide_count
    near_y = (inner_y - here_y + 1) % narrow_count
    near_row = (near_x * 3 + near_y) * row_count + inner_r
    position = near_row[:, None] * slot_count + inner_slot
    return jnp.where(present, position, 9 * row_count * slot_count).astype(jnp.int32)


def reference(density, neighbours, ent_blocks, ent_owner, ent_place):
    area = B * B
    flat_blocks = density.reshape(NDEV * R * K, area).astype(jnp.float32)
    owners = ent_owner.reshape(NDEV, E)
    places = ent_place.reshape(NDEV, E)
    entering = ent_blocks.reshape(NDEV, E, area)

    def add_source(total, item):
        owner_list, place_list, block_list = item
        target = (owner_list * (R * K) + place_list).astype(jnp.int32)
        return total.at[target].add(block_list.astype(jnp.float32)), None

    flat_blocks, unused = lax.scan(add_source, flat_blocks, (owners, places, entering))
    admitted = flat_blocks.astype(jnp.bfloat16).reshape(SLAB_X, SLAB_Y, R, K, B, B)
    admitted = lax.optimization_barrier(admitted)

    def one_device(device_id):
        here_x = device_id // SLAB_Y
        here_y = device_id % SLAB_Y
        offsets = jnp.arange(3, dtype=jnp.int32) - 1
        near_xs = ((here_x + offsets) % SLAB_X).astype(jnp.int32)
        near_ys = ((here_y + offsets) % SLAB_Y).astype(jnp.int32)
        table = jnp.take(jnp.take(admitted, near_xs, axis=0), near_ys, axis=1)
        table = table.reshape(9 * R * K, B, B).astype(jnp.float32)
        own_rows = admitted[here_x, here_y]
        own_columns = neighbours[here_x, here_y]

        def one_row(item):
            left_blocks, row_columns = item
            position = block_positions(neighbours, here_x, here_y, row_columns)
            gathered = jnp.take(table, position.reshape(-1), axis=0, mode="fill", fill_value=0.0)
            gathered = gathered.reshape(K, K, B, B)
            square = jnp.einsum("mab,mkbc->kac", left_blocks.astype(jnp.float32), gathered)
            square_b = lax.optimization_barrier(square.astype(jnp.bfloat16))
            cube = jnp.einsum("mab,mkbc->kac", square_b.astype(jnp.float32), gathered)
            return 3.0 * square - 2.0 * cube

        return lax.map(one_row, (own_rows, own_columns))

    result = lax.map(one_device, jnp.arange(NDEV, dtype=jnp.int32))
    return result.reshape(SLAB_X, SLAB_Y, R, K, B, B)
```

```python
import jax
import jax.numpy as jnp
from jax import lax
from jax.experimental import pallas as pl
from jax.experimental.pallas import tpu as pltpu
from jax.sharding import PartitionSpec as P

C = 2


def pack_kernel(slots_ref, ent_ref, out_ref, sem):
    count = ent_ref.shape[0]

    def issue(i, carry):
        pltpu.make_async_copy(ent_ref.at[i], out_ref.at[slots_ref[i]], sem).start()
        return carry

    lax.fori_loop(0, count, issue, 0)
    pltpu.make_async_copy(ent_ref, out_ref.at[pl.ds(0, count)], sem).wait()


def pack(ent_blocks, slots, total):
    return pl.pallas_call(
        pack_kernel,
        out_shape=jax.ShapeDtypeStruct((total,) + ent_blocks.shape[1:], ent_blocks.dtype),
        in_specs=[
            pl.BlockSpec(memory_space=pltpu.SMEM),
            pl.BlockSpec(memory_space=pl.ANY),
        ],
        out_specs=pl.BlockSpec(memory_space=pl.ANY),
        scratch_shapes=[pltpu.SemaphoreType.DMA],
        name="pack",
    )(slots, ent_blocks)


def admit_kernel(first_ref, order_ref, density_ref, received_ref, out_ref):
    def target(t, carry):
        def add(j, total):
            return total + received_ref[order_ref[j]].astype(jnp.float32)

        total = lax.fori_loop(
            first_ref[t], first_ref[t + 1], add, density_ref[t].astype(jnp.float32)
        )
        out_ref[t] = total.astype(out_ref.dtype)
        return carry

    lax.fori_loop(0, density_ref.shape[0], target, 0)


def admit(density, received, first, order):
    return pl.pallas_call(
        admit_kernel,
        out_shape=jax.ShapeDtypeStruct(density.shape, density.dtype),
        in_specs=[
            pl.BlockSpec(memory_space=pltpu.SMEM),
            pl.BlockSpec(memory_space=pltpu.SMEM),
            pl.BlockSpec(memory_space=pltpu.VMEM),
            pl.BlockSpec(memory_space=pltpu.VMEM),
        ],
        out_specs=pl.BlockSpec(memory_space=pltpu.VMEM),
        name="admit",
    )(first, order, density, received)


def purify_kernel(row_count, slot_count, width, piece_starts, pos_ref, *refs):
    pieces = refs[: len(piece_starts)]
    out_ref, table, left, gathered, square, square_b, sems = refs[len(piece_starts):]
    pair = 2 * width
    copies = []
    for i, (piece, start) in enumerate(zip(pieces, piece_starts)):
        copy = pltpu.make_async_copy(piece, table.at[pl.ds(start, piece.shape[0])], sems.at[i])
        copy.start()
        copies.append(copy)
    table[9 * row_count * slot_count] = jnp.zeros((width, width), table.dtype)
    for copy in copies:
        copy.wait()

    def row(r, carry):
        base = r * slot_count * slot_count
        for m in range(slot_count):
            left[:, m * width:(m + 1) * width] = table[r * slot_count + m]
        for k in range(0, slot_count, 2):
            for m in range(slot_count):
                for j in range(2):
                    gathered[
                        m * width:(m + 1) * width, (k + j) * width:(k + j + 1) * width
                    ] = table[pos_ref[base + m * slot_count + k + j]]
            lanes = slice(k * width, k * width + pair)
            product = jnp.dot(
                left[...], gathered[:, lanes], preferred_element_type=jnp.float32
            )
            square[:, lanes] = product
            square_b[:, lanes] = product.astype(jnp.bfloat16)
        for k in range(0, slot_count, 2):
            lanes = slice(k * width, k * width + pair)
            product = jnp.dot(
                square_b[...], gathered[:, lanes], preferred_element_type=jnp.float32
            )
            result = 3.0 * square[:, lanes] - 2.0 * product
            out_ref[r * slot_count + k] = result[:, :width]
            out_ref[r * slot_count + k + 1] = result[:, width:]
        return carry

    lax.fori_loop(0, row_count, row, 0)


def purify(positions, pieces, piece_starts, row_count, slot_count, width):
    import functools

    span = slot_count * width
    return pl.pallas_call(
        functools.partial(purify_kernel, row_count, slot_count, width, piece_starts),
        out_shape=jax.ShapeDtypeStruct((row_count * slot_count, width, width), jnp.float32),
        in_specs=[pl.BlockSpec(memory_space=pltpu.SMEM)]
        + [pl.BlockSpec(memory_space=pl.ANY)] * len(pieces),
        out_specs=pl.BlockSpec(memory_space=pltpu.VMEM),
        scratch_shapes=[
            pltpu.VMEM((9 * row_count * slot_count + 1, width, width), jnp.bfloat16),
            pltpu.VMEM((width, span), jnp.bfloat16),
            pltpu.VMEM((span, span), jnp.bfloat16),
            pltpu.VMEM((width, span), jnp.float32),
            pltpu.VMEM((width, span), jnp.bfloat16),
            pltpu.SemaphoreType.DMA((len(pieces),)),
        ],
        name="purify",
    )(positions, *pieces)


def block_positions(neighbours, here_x, here_y, my_columns):
    wide_count, narrow_count, row_count, slot_count = neighbours.shape
    listing = neighbours.reshape(wide_count * narrow_count * row_count, slot_count)
    inner_lists = jnp.take(listing, my_columns, axis=0)
    matches = inner_lists[:, :, None, :] == my_columns[:, None, :, None]
    present = jnp.any(matches, axis=3)
    slot_ids = jnp.arange(slot_count, dtype=jnp.int32)
    inner_slot = jnp.sum(jnp.where(matches, slot_ids, 0), axis=3)
    inner_x = my_columns // (narrow_count * row_count)
    inner_y = my_columns // row_count % narrow_count
    inner_r = my_columns % row_count
    near_x = jnp.where(inner_x == here_x, 0, jnp.where(inner_x == here_x ^ 1, 1, 2))
    near_y = jnp.where(inner_y == here_y, 0, jnp.where(inner_y == here_y ^ 1, 1, 2))
    near_row = (near_x * 3 + near_y) * row_count + inner_r
    position = near_row[:, :, None] * slot_count + inner_slot
    return jnp.where(present, position, 9 * row_count * slot_count).astype(jnp.int32)


def per_device(density, neighbours, ent_blocks, ent_owner, ent_place):
    wide_count = lax.axis_size("gx")
    narrow_count = lax.axis_size("gy")
    device_count = wide_count * narrow_count
    here_x = lax.axis_index("gx")
    here_y = lax.axis_index("gy")
    self_index = here_x * narrow_count + here_y
    row_count = density.shape[2]
    slot_count = density.shape[3]
    width = density.shape[4]
    blocks = row_count * slot_count
    held = ent_blocks.shape[0]
    owners = ent_owner.reshape(device_count, held)
    places = ent_place.reshape(device_count, held)

    my_owners = lax.dynamic_index_in_dim(owners, self_index, 0, False)
    entry_ids = jnp.arange(held, dtype=jnp.int32)
    same = my_owners[:, None] == my_owners[None, :]
    my_ranks = jnp.sum(same & (entry_ids[None, :] < entry_ids[:, None]), axis=1)
    slots = (my_owners * C + my_ranks).astype(jnp.int32)
    outgoing = pack(ent_blocks, slots, device_count * C)
    received = lax.all_to_all(
        outgoing.reshape(device_count, C, width, width),
        ("gx", "gy"), split_axis=0, concat_axis=0, tiled=True,
    ).reshape(device_count * C, width, width)

    for_me = (owners == self_index).astype(jnp.int32)
    rank = jnp.cumsum(for_me, axis=1) - for_me
    picked = (for_me[:, :, None] == 1) & (
        rank[:, :, None] == jnp.arange(C, dtype=jnp.int32)[None, None, :]
    )
    slot_place = jnp.sum(jnp.where(picked, places[:, :, None], 0), axis=1).reshape(-1)
    slot_used = jnp.any(picked, axis=1).reshape(-1)
    slot_place = jnp.where(slot_used, slot_place, blocks)
    slot_ids = jnp.arange(device_count * C, dtype=jnp.int32)
    ahead = (slot_place[:, None] > slot_place[None, :]) | (
        (slot_place[:, None] == slot_place[None, :]) & (slot_ids[:, None] > slot_ids[None, :])
    )
    sorted_at = jnp.sum(ahead, axis=1)
    order = jnp.sum(
        jnp.where(sorted_at[None, :] == slot_ids[:, None], slot_ids[None, :], 0), axis=1
    ).astype(jnp.int32)
    target_ids = jnp.arange(blocks + 1, dtype=jnp.int32)
    first = jnp.sum(slot_place[None, :] < target_ids[:, None], axis=1).astype(jnp.int32)

    own = admit(density.reshape(blocks, width, width), received, first, order)

    axes = ("gx", "gy")
    devices = [(x, y) for x in range(wide_count) for y in range(narrow_count)]

    def send(array, target):
        pairs = []
        for x, y in devices:
            to_x, to_y = target(x, y)
            pairs.append((x * narrow_count + y, to_x % wide_count * narrow_count + to_y))
        return lax.ppermute(array, axes, pairs)

    def across(x, y):
        return x, narrow_count - 1 - y

    def chip(x, y):
        return x, y ^ 1

    def ring(x, y):
        return x ^ 1, narrow_count - 1 - y

    def onward(x, y):
        return (x + 2 if x % 2 == 0 else x - 2), y

    half = blocks // 2
    own_across = send(own, across)
    ring_across = send(own, ring)
    own_chip = send(own, chip)
    ring_same_a = send(ring_across[:half], across)
    ring_same_b = send(own_across[half:], ring)
    far_across = send(ring_across, onward)
    far_same_a = send(ring_same_a, onward)
    far_same_b = send(ring_same_b, onward)
    ring_chip_a = send(ring_same_a, chip)
    ring_chip_b = send(ring_same_b, chip)
    far_chip_a = send(far_same_a, chip)
    far_chip_b = send(far_same_b, chip)

    pieces = [
        (own, 0), (own_chip, 1), (own_across, 2),
        (ring_same_a, 3), (ring_same_b, 3.5), (ring_chip_a, 4), (ring_chip_b, 4.5), (ring_across, 5),
        (far_same_a, 6), (far_same_b, 6.5), (far_chip_a, 7), (far_chip_b, 7.5), (far_across, 8),
    ]
    my_columns = lax.dynamic_index_in_dim(
        lax.dynamic_index_in_dim(neighbours, here_x, 0, False), here_y, 0, False
    )
    positions = block_positions(neighbours, here_x, here_y, my_columns).reshape(-1)
    purified = purify(
        positions, [piece for piece, _ in pieces],
        [int(start * blocks) for _, start in pieces], row_count, slot_count, width,
    )
    return purified.reshape(density.shape)


def solution(mesh):
    in_specs = (P("gx", "gy", None, None, None, None), P(), P(("gx", "gy"), None, None), P(), P())
    out_specs = P("gx", "gy", None, None, None, None)
    return jax.shard_map(
        per_device, mesh=mesh, in_specs=in_specs, out_specs=out_specs, check_vma=False
    )
```

```python
import functools

import jax
import jax.numpy as jnp
from jax import lax
from jax.experimental import pallas as pl
from jax.experimental.pallas import tpu as pltpu
from jax.sharding import PartitionSpec as P

C = 2


def pack_kernel(slots_ref, ent_ref, out_ref, staged, load_sems, store_sem):
    count = ent_ref.shape[0]
    parts = load_sems.shape[0]
    size = count // parts
    loads = []
    for p in range(parts):
        rows = pl.ds(p * size, size)
        loads.append(pltpu.make_async_copy(ent_ref.at[rows], staged.at[rows], load_sems.at[p]))
        loads[-1].start()

    def issue(i, carry):
        pltpu.make_async_copy(staged.at[i], out_ref.at[slots_ref[i]], store_sem).start()
        return carry

    for p in range(parts):
        loads[p].wait()
        lax.fori_loop(p * size, (p + 1) * size, issue, 0)
    pltpu.make_async_copy(staged, out_ref.at[pl.ds(0, count)], store_sem).wait()


def pack(ent_blocks, slots, total):
    return pl.pallas_call(
        pack_kernel,
        out_shape=jax.ShapeDtypeStruct((total,) + ent_blocks.shape[1:], ent_blocks.dtype),
        in_specs=[
            pl.BlockSpec(memory_space=pltpu.SMEM),
            pl.BlockSpec(memory_space=pl.ANY),
        ],
        out_specs=pl.BlockSpec(memory_space=pl.ANY),
        scratch_shapes=[
            pltpu.VMEM(ent_blocks.shape, ent_blocks.dtype),
            pltpu.SemaphoreType.DMA((4,)),
            pltpu.SemaphoreType.DMA,
        ],
        name="pack",
    )(slots, ent_blocks)


def admit_kernel(first_ref, order_ref, stored_ref, density_ref, received_ref, out_ref):
    def target(t, carry):
        def add(j, total):
            return total + received_ref[order_ref[j]].astype(jnp.float32)

        total = lax.fori_loop(
            first_ref[t], first_ref[t + 1], add, density_ref[t].astype(jnp.float32)
        )
        out_ref[stored_ref[t]] = total.astype(out_ref.dtype)
        return carry

    lax.fori_loop(0, density_ref.shape[0], target, 0)


def admit(density, received, first, order, stored):
    return pl.pallas_call(
        admit_kernel,
        out_shape=jax.ShapeDtypeStruct(density.shape, density.dtype),
        in_specs=[
            pl.BlockSpec(memory_space=pltpu.SMEM),
            pl.BlockSpec(memory_space=pltpu.SMEM),
            pl.BlockSpec(memory_space=pltpu.SMEM),
            pl.BlockSpec(memory_space=pltpu.VMEM),
            pl.BlockSpec(memory_space=pltpu.VMEM),
        ],
        out_specs=pl.BlockSpec(memory_space=pltpu.VMEM),
        name="admit",
    )(first, order, stored, density, received)


def purify_kernel(row_count, slot_count, width, piece_starts, zero_at, pos_ref, stored_ref, *refs):
    pieces = refs[: len(piece_starts)]
    out_ref, table, left, gathered, square, square_b, sems = refs[len(piece_starts):]
    pair = 2 * width
    copies = []
    for i, (piece, start) in enumerate(zip(pieces, piece_starts)):
        copy = pltpu.make_async_copy(piece, table.at[pl.ds(start, piece.shape[0])], sems.at[i])
        copy.start()
        copies.append(copy)
    table[zero_at] = jnp.zeros((width, width), table.dtype)
    for copy in copies:
        copy.wait()

    def row(r, carry):
        base = r * slot_count * slot_count
        for m in range(slot_count):
            left[:, m * width:(m + 1) * width] = table[stored_ref[r * slot_count + m]]
        for k in range(0, slot_count, 2):
            for m in range(slot_count):
                for j in range(2):
                    gathered[
                        m * width:(m + 1) * width, (k + j) * width:(k + j + 1) * width
                    ] = table[pos_ref[base + m * slot_count + k + j]]
            lanes = slice(k * width, k * width + pair)
            product = jnp.dot(
                left[...], gathered[:, lanes], preferred_element_type=jnp.float32
            )
            square[:, lanes] = product
            square_b[:, lanes] = product.astype(jnp.bfloat16)
        for k in range(0, slot_count, 2):
            lanes = slice(k * width, k * width + pair)
            product = jnp.dot(
                square_b[...], gathered[:, lanes], preferred_element_type=jnp.float32
            )
            result = 3.0 * square[:, lanes] - 2.0 * product
            out_ref[r * slot_count + k] = result[:, :width]
            out_ref[r * slot_count + k + 1] = result[:, width:]
        return carry

    lax.fori_loop(0, row_count, row, 0)


def purify(positions, stored, pieces, piece_starts, zero_at, row_count, slot_count, width):
    span = slot_count * width
    return pl.pallas_call(
        functools.partial(purify_kernel, row_count, slot_count, width, piece_starts, zero_at),
        out_shape=jax.ShapeDtypeStruct((row_count * slot_count, width, width), jnp.float32),
        in_specs=[pl.BlockSpec(memory_space=pltpu.SMEM)] * 2
        + [pl.BlockSpec(memory_space=pl.ANY)] * len(pieces),
        out_specs=pl.BlockSpec(memory_space=pltpu.VMEM),
        scratch_shapes=[
            pltpu.VMEM((zero_at + 1, width, width), jnp.bfloat16),
            pltpu.VMEM((width, span), jnp.bfloat16),
            pltpu.VMEM((span, span), jnp.bfloat16),
            pltpu.VMEM((width, span), jnp.float32),
            pltpu.VMEM((width, span), jnp.bfloat16),
            pltpu.SemaphoreType.DMA((len(pieces),)),
        ],
        name="purify",
    )(positions, stored, *pieces)


def block_positions(neighbours, here_x, here_y, my_columns, starts, zero_at):
    wide_count, narrow_count, row_count, slot_count = neighbours.shape
    listing = neighbours.reshape(wide_count * narrow_count * row_count, slot_count)
    inner_lists = jnp.take(listing, my_columns, axis=0)
    inner_x = my_columns // (narrow_count * row_count)
    inner_y = my_columns // row_count % narrow_count
    inner_r = my_columns % row_count
    list_x = inner_lists // (narrow_count * row_count)
    list_y = inner_lists // row_count % narrow_count
    kind = jnp.where(
        list_x == (inner_x ^ 1)[:, :, None], 2, jnp.where(list_y == (inner_y ^ 1)[:, :, None], 1, 0)
    )
    slot_ids = jnp.arange(slot_count, dtype=jnp.int32)
    key = kind * slot_count + slot_ids
    place = jnp.sum((key[:, :, :, None] > key[:, :, None, :]).astype(jnp.int32), axis=3)
    matches = inner_lists[:, :, None, :] == my_columns[:, None, :, None]
    present = jnp.any(matches, axis=3)
    inner_place = jnp.sum(jnp.where(matches, place[:, :, None, :], 0), axis=3)
    near_x = jnp.where(inner_x == here_x, 0, jnp.where(inner_x == here_x ^ 1, 1, 2))
    near_y = jnp.where(inner_y == here_y, 0, jnp.where(inner_y == here_y ^ 1, 1, 2))
    near = near_x * 3 + near_y
    near_start = jnp.zeros_like(near)
    for i, start in enumerate(starts):
        near_start = jnp.where(near == i, start, near_start)
    position = (near_start + inner_r)[:, :, None] + inner_place * row_count
    positions = jnp.where(present, position, zero_at).astype(jnp.int32)
    own_places = place[:, 0] * row_count + jnp.arange(row_count, dtype=jnp.int32)[:, None]
    return positions.reshape(-1), own_places.astype(jnp.int32).reshape(-1)


def per_device(density, neighbours, ent_blocks, ent_owner, ent_place):
    wide_count = lax.axis_size("gx")
    narrow_count = lax.axis_size("gy")
    device_count = wide_count * narrow_count
    here_x = lax.axis_index("gx")
    here_y = lax.axis_index("gy")
    self_index = here_x * narrow_count + here_y
    row_count = density.shape[2]
    slot_count = density.shape[3]
    width = density.shape[4]
    blocks = row_count * slot_count
    held = ent_blocks.shape[0]
    owners = ent_owner.reshape(device_count, held)
    places = ent_place.reshape(device_count, held)

    my_owners = lax.dynamic_index_in_dim(owners, self_index, 0, False)
    entry_ids = jnp.arange(held, dtype=jnp.int32)
    same = my_owners[:, None] == my_owners[None, :]
    my_ranks = jnp.sum(same & (entry_ids[None, :] < entry_ids[:, None]), axis=1)
    slots = (my_owners * C + my_ranks).astype(jnp.int32)
    outgoing = pack(ent_blocks, slots, device_count * C)
    received = lax.all_to_all(
        outgoing.reshape(device_count, C, width, width),
        ("gx", "gy"), split_axis=0, concat_axis=0, tiled=True,
    ).reshape(device_count * C, width, width)

    for_me = (owners == self_index).astype(jnp.int32)
    rank = jnp.cumsum(for_me, axis=1) - for_me
    picked = (for_me[:, :, None] == 1) & (
        rank[:, :, None] == jnp.arange(C, dtype=jnp.int32)[None, None, :]
    )
    slot_place = jnp.sum(jnp.where(picked, places[:, :, None], 0), axis=1).reshape(-1)
    slot_used = jnp.any(picked, axis=1).reshape(-1)
    slot_place = jnp.where(slot_used, slot_place, blocks)
    slot_ids = jnp.arange(device_count * C, dtype=jnp.int32)
    ahead = (slot_place[:, None] > slot_place[None, :]) | (
        (slot_place[:, None] == slot_place[None, :]) & (slot_ids[:, None] > slot_ids[None, :])
    )
    sorted_at = jnp.sum(ahead, axis=1)
    order = jnp.sum(
        jnp.where(sorted_at[None, :] == slot_ids[:, None], slot_ids[None, :], 0), axis=1
    ).astype(jnp.int32)
    target_ids = jnp.arange(blocks + 1, dtype=jnp.int32)
    first = jnp.sum(slot_place[None, :] < target_ids[:, None], axis=1).astype(jnp.int32)

    near_blocks = row_count * min(slot_count, 6 * row_count)
    corner_blocks = row_count * min(slot_count, 4 * row_count)
    sizes = [blocks] * 6 + [near_blocks, near_blocks, corner_blocks]
    starts = [sum(sizes[:i]) for i in range(9)]
    zero_at = sum(sizes)
    my_columns = lax.dynamic_index_in_dim(
        lax.dynamic_index_in_dim(neighbours, here_x, 0, False), here_y, 0, False
    )
    positions, stored = block_positions(neighbours, here_x, here_y, my_columns, starts, zero_at)

    own = admit(density.reshape(blocks, width, width), received, first, order, stored)

    axes = ("gx", "gy")
    devices = [(x, y) for x in range(wide_count) for y in range(narrow_count)]

    def send(array, target):
        pairs = []
        for x, y in devices:
            to_x, to_y = target(x, y)
            pairs.append((x * narrow_count + y, to_x % wide_count * narrow_count + to_y))
        return lax.ppermute(array, axes, pairs)

    def across(x, y):
        return x, narrow_count - 1 - y

    def chip(x, y):
        return x, y ^ 1

    def ring(x, y):
        return x ^ 1, narrow_count - 1 - y

    def onward(x, y):
        return (x + 2 if x % 2 == 0 else x - 2), y

    half = blocks // 2
    ring_across_a = send(own[:half], ring)
    own_across_b = send(own[half:], across)
    own_chip = send(own, chip)
    ring_same_a = send(ring_across_a, across)
    far_across_a = send(ring_across_a, onward)
    ring_same_b = send(own_across_b, ring)
    ring_across_b = send(own[half:], ring)
    own_across_a = send(own[:half], across)
    far_same_a = send(ring_same_a, onward)
    ring_chip_a = send(ring_same_a, chip)
    far_same_b = send(ring_same_b[:near_blocks - half], onward)
    ring_chip_b = send(ring_same_b, chip)
    far_across_b = send(ring_across_b[:corner_blocks - half], onward)
    far_chip_a = send(far_same_a, chip)
    far_chip_b = send(far_same_b, chip)

    pieces = [
        (own, 0, 0), (own_chip, 1, 0), (own_across_a, 2, 0), (own_across_b, 2, half),
        (ring_same_a, 3, 0), (ring_same_b, 3, half), (ring_chip_a, 4, 0), (ring_chip_b, 4, half),
        (ring_across_a, 5, 0), (ring_across_b, 5, half),
        (far_same_a, 6, 0), (far_same_b, 6, half), (far_chip_a, 7, 0), (far_chip_b, 7, half),
        (far_across_a, 8, 0), (far_across_b, 8, half),
    ]
    purified = purify(
        positions, stored, [piece for piece, _, _ in pieces],
        [starts[part] + offset for _, part, offset in pieces],
        zero_at, row_count, slot_count, width,
    )
    return purified.reshape(density.shape)


def solution(mesh):
    in_specs = (P("gx", "gy", None, None, None, None), P(), P(("gx", "gy"), None, None), P(), P())
    out_specs = P("gx", "gy", None, None, None, None)
    return jax.shard_map(
        per_device, mesh=mesh, in_specs=in_specs, out_specs=out_specs, check_vma=False
    )
```

```python
import functools

import jax
import jax.numpy as jnp
from jax import lax
from jax.experimental import pallas as pl
from jax.experimental.pallas import tpu as pltpu
from jax.sharding import PartitionSpec as P

C = 2


def pack_kernel(slots_ref, ent_ref, out_ref, staged, load_sems, store_sem):
    count = ent_ref.shape[0]
    parts = load_sems.shape[0]
    size = count // parts
    loads = []
    for p in range(parts):
        rows = pl.ds(p * size, size)
        loads.append(pltpu.make_async_copy(ent_ref.at[rows], staged.at[rows], load_sems.at[p]))
        loads[-1].start()

    def issue(i, carry):
        pltpu.make_async_copy(staged.at[i], out_ref.at[slots_ref[i]], store_sem).start()
        return carry

    for p in range(parts):
        loads[p].wait()
        lax.fori_loop(p * size, (p + 1) * size, issue, 0)
    pltpu.make_async_copy(staged, out_ref.at[pl.ds(0, count)], store_sem).wait()


def pack(ent_blocks, slots, total):
    return pl.pallas_call(
        pack_kernel,
        out_shape=jax.ShapeDtypeStruct((total,) + ent_blocks.shape[1:], ent_blocks.dtype),
        in_specs=[
            pl.BlockSpec(memory_space=pltpu.SMEM),
            pl.BlockSpec(memory_space=pl.ANY),
        ],
        out_specs=pl.BlockSpec(memory_space=pl.ANY),
        scratch_shapes=[
            pltpu.VMEM(ent_blocks.shape, ent_blocks.dtype),
            pltpu.SemaphoreType.DMA((4,)),
            pltpu.SemaphoreType.DMA,
        ],
        name="pack",
    )(slots, ent_blocks)


def admit_kernel(spans, first_ref, order_ref, source_ref, density_ref, received_ref, own_ref, *part_refs):
    def add(j, total):
        return total + received_ref[order_ref[j]].astype(jnp.float32)

    def place(p, carry):
        t = source_ref[p]
        total = lax.fori_loop(
            first_ref[t], first_ref[t + 1], add, density_ref[t].astype(jnp.float32)
        )
        own_ref[p] = total.astype(own_ref.dtype)
        return carry

    lax.fori_loop(0, own_ref.shape[0], place, 0)
    for (low, high), part_ref in zip(spans, part_refs):
        part_ref[...] = own_ref[low:high]


def admit(density, received, first, order, source, spans):
    shapes = [density.shape[0]] + [high - low for low, high in spans]
    return pl.pallas_call(
        functools.partial(admit_kernel, spans),
        out_shape=[
            jax.ShapeDtypeStruct((n,) + density.shape[1:], density.dtype) for n in shapes
        ],
        in_specs=[pl.BlockSpec(memory_space=pltpu.SMEM)] * 3
        + [pl.BlockSpec(memory_space=pltpu.VMEM)] * 2,
        out_specs=[pl.BlockSpec(memory_space=pltpu.VMEM)] * len(shapes),
        name="admit",
    )(first, order, source, density, received)


def reach(part):
    wide, narrow = divmod(part, 3)
    wides = (0, 1, 2) if wide == 0 else (0, wide)
    narrows = (0, 1, 2) if narrow == 0 else (0, narrow)
    return [w * 3 + n for w in wides for n in narrows]


def purify_kernel(row_count, width, piece_starts, zero_at, pos_ref, slot_ref, *refs):
    pieces = refs[: len(piece_starts)]
    out_ref, table, left, grid, square, square_b, staged, sems, out_sem = refs[len(piece_starts):]
    near = 9 * row_count
    group = row_count * width
    copies = []
    for i, (piece, start) in enumerate(zip(pieces, piece_starts)):
        copy = pltpu.make_async_copy(piece, table.at[pl.ds(start, piece.shape[0])], sems.at[i])
        copy.start()
        copies.append(copy)
    table[zero_at] = jnp.zeros((width, width), table.dtype)
    for copy in copies:
        copy.wait()

    for r in range(row_count):
        for k in range(near):
            left[r * width:(r + 1) * width, k * width:(k + 1) * width] = table[
                pos_ref[r * near + k]
            ]

    def lanes_of(ref, parts):
        return jnp.concatenate([ref[:, q * group:(q + 1) * group] for q in parts], axis=1)

    for part in range(9):
        parts = reach(part)
        for i, q in enumerate(parts):
            for r in range(row_count):
                for k in range(row_count):
                    low = (i * row_count + r) * width
                    grid[part, low:low + width, k * width:(k + 1) * width] = table[
                        pos_ref[(q * row_count + r) * near + part * row_count + k]
                    ]
        product = jnp.dot(
            lanes_of(left, parts), grid[part, :len(parts) * group],
            preferred_element_type=jnp.float32,
        )
        lanes = slice(part * group, (part + 1) * group)
        square[:, lanes] = product
        for r in range(row_count):
            for k in range(row_count):
                listed = pos_ref[r * near + part * row_count + k] != zero_at
                low = part * group + k * width
                square_b[r * width:(r + 1) * width, low:low + width] = jnp.where(
                    listed, product[r * width:(r + 1) * width, k * width:(k + 1) * width], 0.0
                ).astype(jnp.bfloat16)

    for part in range(9):
        parts = reach(part)
        product = jnp.dot(
            lanes_of(square_b, parts), grid[part, :len(parts) * group],
            preferred_element_type=jnp.float32,
        )
        result = 3.0 * square[:, part * group:(part + 1) * group] - 2.0 * product
        for r in range(row_count):
            for k in range(row_count):
                staged[slot_ref[r * near + part * row_count + k]] = result[
                    r * width:(r + 1) * width, k * width:(k + 1) * width
                ]
    copy = pltpu.make_async_copy(staged.at[pl.ds(0, out_ref.shape[0])], out_ref, out_sem)
    copy.start()
    copy.wait()


def purify(positions, out_slots, pieces, piece_starts, zero_at, row_count, slot_count, width):
    span = 9 * row_count * width
    group = row_count * width
    blocks = row_count * slot_count
    return pl.pallas_call(
        functools.partial(purify_kernel, row_count, width, piece_starts, zero_at),
        out_shape=jax.ShapeDtypeStruct((blocks, width, width), jnp.float32),
        in_specs=[pl.BlockSpec(memory_space=pltpu.SMEM)] * 2
        + [pl.BlockSpec(memory_space=pl.ANY)] * len(pieces),
        out_specs=pl.BlockSpec(memory_space=pl.ANY),
        scratch_shapes=[
            pltpu.VMEM((zero_at + 1, width, width), jnp.bfloat16),
            pltpu.VMEM((group, span), jnp.bfloat16),
            pltpu.VMEM((9, span, group), jnp.bfloat16),
            pltpu.VMEM((group, span), jnp.float32),
            pltpu.VMEM((group, span), jnp.bfloat16),
            pltpu.VMEM((blocks + 1, width, width), jnp.float32),
            pltpu.SemaphoreType.DMA((len(pieces),)),
            pltpu.SemaphoreType.DMA,
        ],
        name="purify",
    )(positions, out_slots, *pieces)


def block_positions(neighbours, here_x, here_y, starts, zero_at):
    wide_count, narrow_count, row_count, slot_count = neighbours.shape
    total_rows = wide_count * narrow_count * row_count
    listing = neighbours.reshape(total_rows, slot_count)
    ids = jnp.arange(9 * row_count, dtype=jnp.int32)
    wide, narrow, inner = ids // (3 * row_count), ids // row_count % 3, ids % row_count
    beyond = jnp.where(here_x % 2 == 0, here_x + wide_count - 1, here_x + 1) % wide_count
    near_x = jnp.where(wide == 0, here_x, jnp.where(wide == 1, here_x ^ 1, beyond))
    near_y = jnp.where(
        narrow == 0, here_y, jnp.where(narrow == 1, here_y ^ 1, narrow_count - 1 - here_y)
    )
    rows = (near_x * narrow_count + near_y) * row_count + inner
    lists = jnp.take(listing, rows, axis=0)
    list_x = lists // (narrow_count * row_count)
    list_y = lists // row_count % narrow_count
    kind = jnp.where(
        list_x == (near_x ^ 1)[:, None], 2, jnp.where(list_y == (near_y ^ 1)[:, None], 1, 0)
    )
    slot_ids = jnp.arange(slot_count, dtype=jnp.int32)
    key = kind * slot_count + slot_ids
    place = jnp.sum((key[:, :, None] > key[:, None, :]).astype(jnp.int32), axis=2)
    part = wide * 3 + narrow
    start = jnp.zeros_like(part)
    for i, value in enumerate(starts):
        start = jnp.where(part == i, value, start)
    held_at = (start + inner)[:, None] + place * row_count
    matches = lists[:, None, :] == rows[None, :, None]
    positions = jnp.min(jnp.where(matches, held_at[:, None, :], zero_at), axis=2)
    own_matches = matches[:row_count]
    own_slots = slot_ids + slot_count * jnp.arange(row_count, dtype=jnp.int32)[:, None, None]
    out_slots = jnp.min(jnp.where(own_matches, own_slots, row_count * slot_count), axis=2)
    order = (place[:row_count] * row_count + inner[:row_count, None]).reshape(-1)
    flat_ids = jnp.arange(row_count * slot_count, dtype=jnp.int32)
    source = jnp.sum(jnp.where(order[None, :] == flat_ids[:, None], flat_ids[None, :], 0), axis=1)
    return (
        positions.astype(jnp.int32).reshape(-1),
        out_slots.astype(jnp.int32).reshape(-1),
        source.astype(jnp.int32),
    )


def per_device(density, neighbours, ent_blocks, ent_owner, ent_place):
    wide_count = lax.axis_size("gx")
    narrow_count = lax.axis_size("gy")
    device_count = wide_count * narrow_count
    here_x = lax.axis_index("gx")
    here_y = lax.axis_index("gy")
    self_index = here_x * narrow_count + here_y
    row_count = density.shape[2]
    slot_count = density.shape[3]
    width = density.shape[4]
    blocks = row_count * slot_count
    held = ent_blocks.shape[0]
    owners = ent_owner.reshape(device_count, held)
    places = ent_place.reshape(device_count, held)

    my_owners = lax.dynamic_index_in_dim(owners, self_index, 0, False)
    entry_ids = jnp.arange(held, dtype=jnp.int32)
    same = my_owners[:, None] == my_owners[None, :]
    my_ranks = jnp.sum(same & (entry_ids[None, :] < entry_ids[:, None]), axis=1)
    slots = (my_owners * C + my_ranks).astype(jnp.int32)
    outgoing = pack(ent_blocks, slots, device_count * C)
    received = lax.all_to_all(
        outgoing.reshape(device_count, C, width, width),
        ("gx", "gy"), split_axis=0, concat_axis=0, tiled=True,
    ).reshape(device_count * C, width, width)

    for_me = (owners == self_index).astype(jnp.int32)
    rank = jnp.cumsum(for_me, axis=1) - for_me
    picked = (for_me[:, :, None] == 1) & (
        rank[:, :, None] == jnp.arange(C, dtype=jnp.int32)[None, None, :]
    )
    slot_place = jnp.sum(jnp.where(picked, places[:, :, None], 0), axis=1).reshape(-1)
    slot_used = jnp.any(picked, axis=1).reshape(-1)
    slot_place = jnp.where(slot_used, slot_place, blocks)
    slot_ids = jnp.arange(device_count * C, dtype=jnp.int32)
    ahead = (slot_place[:, None] > slot_place[None, :]) | (
        (slot_place[:, None] == slot_place[None, :]) & (slot_ids[:, None] > slot_ids[None, :])
    )
    sorted_at = jnp.sum(ahead, axis=1)
    order = jnp.sum(
        jnp.where(sorted_at[None, :] == slot_ids[:, None], slot_ids[None, :], 0), axis=1
    ).astype(jnp.int32)
    target_ids = jnp.arange(blocks + 1, dtype=jnp.int32)
    first = jnp.sum(slot_place[None, :] < target_ids[:, None], axis=1).astype(jnp.int32)

    near_blocks = row_count * min(slot_count, 6 * row_count)
    corner_blocks = row_count * min(slot_count, 4 * row_count)
    sizes = [blocks] * 6 + [near_blocks, near_blocks, corner_blocks]
    starts = [sum(sizes[:i]) for i in range(9)]
    zero_at = sum(sizes)
    positions, out_slots, source = block_positions(neighbours, here_x, here_y, starts, zero_at)

    cut = corner_blocks // 2
    spans = ((0, cut), (cut, 2 * cut), (2 * cut, blocks), (0, 2 * cut))
    own, own_1, own_2, own_3, own_12 = admit(
        density.reshape(blocks, width, width), received, first, order, source, spans
    )

    axes = ("gx", "gy")
    devices = [(x, y) for x in range(wide_count) for y in range(narrow_count)]

    def send(array, target):
        pairs = []
        for x, y in devices:
            to_x, to_y = target(x, y)
            pairs.append((x * narrow_count + y, to_x % wide_count * narrow_count + to_y))
        return lax.ppermute(array, axes, pairs)

    def across(x, y):
        return x, narrow_count - 1 - y

    def chip(x, y):
        return x, y ^ 1

    def ring(x, y):
        return x ^ 1, narrow_count - 1 - y

    def onward(x, y):
        return (x + 2 if x % 2 == 0 else x - 2), y

    ring_across_1 = send(own_1, ring)
    own_across_3 = send(own_3, across)
    ring_across_2 = send(own_2, ring)
    own_chip = send(own, chip)
    far_across_1 = send(ring_across_1, onward)
    ring_same_1 = send(ring_across_1, across)
    ring_same_3 = send(own_across_3, ring)
    far_across_2 = send(ring_across_2, onward)
    ring_same_2 = send(ring_across_2, across)
    ring_across_3 = send(own_3, ring)
    own_across_12 = send(own_12, across)
    far_same_1 = send(ring_same_1, onward)
    ring_chip_1 = send(ring_same_1, chip)
    far_same_2 = send(ring_same_2, onward)
    ring_chip_2 = send(ring_same_2, chip)
    far_same_3 = send(ring_same_3[:near_blocks - 2 * cut], onward)
    ring_chip_3 = send(ring_same_3, chip)
    far_chip_1 = send(far_same_1, chip)
    far_chip_2 = send(far_same_2, chip)
    far_chip_3 = send(far_same_3, chip)

    pieces = [
        (own, 0, 0), (own_chip, 1, 0), (own_across_12, 2, 0), (own_across_3, 2, 2 * cut),
        (ring_same_1, 3, 0), (ring_same_2, 3, cut), (ring_same_3, 3, 2 * cut),
        (ring_chip_1, 4, 0), (ring_chip_2, 4, cut), (ring_chip_3, 4, 2 * cut),
        (ring_across_1, 5, 0), (ring_across_2, 5, cut), (ring_across_3, 5, 2 * cut),
        (far_same_1, 6, 0), (far_same_2, 6, cut), (far_same_3, 6, 2 * cut),
        (far_chip_1, 7, 0), (far_chip_2, 7, cut), (far_chip_3, 7, 2 * cut),
        (far_across_1, 8, 0), (far_across_2, 8, cut),
    ]
    purified = purify(
        positions, out_slots, [piece for piece, _, _ in pieces],
        [starts[part] + offset for _, part, offset in pieces],
        zero_at, row_count, slot_count, width,
    )
    return purified.reshape(density.shape)


def solution(mesh):
    in_specs = (P("gx", "gy", None, None, None, None), P(), P(("gx", "gy"), None, None), P(), P())
    out_specs = P("gx", "gy", None, None, None, None)
    return jax.shard_map(
        per_device, mesh=mesh, in_specs=in_specs, out_specs=out_specs, check_vma=False
    )
```

```python
import functools

import jax
import jax.numpy as jnp
from jax import lax
from jax.experimental import pallas as pl
from jax.experimental.pallas import tpu as pltpu
from jax.sharding import PartitionSpec as P

C = 2


def pack_kernel(slots_ref, ent_ref, out_ref, staged, load_sems, store_sem):
    count = ent_ref.shape[0]
    parts = load_sems.shape[0]
    size = count // parts
    loads = []
    for p in range(parts):
        rows = pl.ds(p * size, size)
        loads.append(pltpu.make_async_copy(ent_ref.at[rows], staged.at[rows], load_sems.at[p]))
        loads[-1].start()

    def issue(i, carry):
        pltpu.make_async_copy(staged.at[i], out_ref.at[slots_ref[i]], store_sem).start()
        return carry

    for p in range(parts):
        loads[p].wait()
        lax.fori_loop(p * size, (p + 1) * size, issue, 0)
    pltpu.make_async_copy(staged, out_ref.at[pl.ds(0, count)], store_sem).wait()


def pack(ent_blocks, slots, total):
    return pl.pallas_call(
        pack_kernel,
        out_shape=jax.ShapeDtypeStruct((total,) + ent_blocks.shape[1:], ent_blocks.dtype),
        in_specs=[
            pl.BlockSpec(memory_space=pltpu.SMEM),
            pl.BlockSpec(memory_space=pl.ANY),
        ],
        out_specs=pl.BlockSpec(memory_space=pl.ANY),
        scratch_shapes=[
            pltpu.VMEM(ent_blocks.shape, ent_blocks.dtype),
            pltpu.SemaphoreType.DMA((4,)),
            pltpu.SemaphoreType.DMA,
        ],
        name="pack",
    )(slots, ent_blocks)


def admit_kernel(spans, first_ref, order_ref, source_ref, density_ref, received_ref, *refs):
    part_refs, own, sems = refs[: len(spans)], refs[len(spans)], refs[len(spans) + 1]

    def add(j, total):
        return total + received_ref[order_ref[j]].astype(jnp.float32)

    def place(p, carry):
        t = source_ref[p]
        total = lax.fori_loop(
            first_ref[t], first_ref[t + 1], add, density_ref[t].astype(jnp.float32)
        )
        own[p] = total.astype(own.dtype)
        return carry

    copies = []
    done = 0
    for i, (low, high) in enumerate(spans):
        if high > done:
            lax.fori_loop(done, high, place, 0)
            done = high
        copies.append(pltpu.make_async_copy(own.at[pl.ds(low, high - low)], part_refs[i], sems.at[i]))
        copies[-1].start()
    for copy in copies:
        copy.wait()


def admit(density, received, first, order, source, spans):
    return pl.pallas_call(
        functools.partial(admit_kernel, spans),
        out_shape=[
            jax.ShapeDtypeStruct((high - low,) + density.shape[1:], density.dtype)
            for low, high in spans
        ],
        in_specs=[pl.BlockSpec(memory_space=pltpu.SMEM)] * 3
        + [pl.BlockSpec(memory_space=pltpu.VMEM)] * 2,
        out_specs=[pl.BlockSpec(memory_space=pl.ANY)] * len(spans),
        scratch_shapes=[
            pltpu.VMEM(density.shape, density.dtype),
            pltpu.SemaphoreType.DMA((len(spans),)),
        ],
        name="admit",
    )(first, order, source, density, received)


def reach(part):
    wide, narrow = divmod(part, 3)
    wides = (0, 1, 2) if wide == 0 else (0, wide)
    narrows = (0, 1, 2) if narrow == 0 else (0, narrow)
    return [w * 3 + n for w in wides for n in narrows]


NEAR_PARTS = 6


def near_count(part):
    return len([q for q in reach(part) if q < NEAR_PARTS])


def far_count(part):
    return len(reach(part)) - near_count(part)


def load_pieces(pieces, piece_starts, table, sems):
    copies = []
    for i, (piece, start) in enumerate(zip(pieces, piece_starts)):
        copies.append(
            pltpu.make_async_copy(piece, table.at[pl.ds(start, piece.shape[0])], sems.at[i])
        )
        copies[-1].start()
    return copies


def lanes_of(ref, parts, group):
    return jnp.concatenate([ref[:, q * group:(q + 1) * group] for q in parts], axis=1)


def near_kernel(row_count, width, piece_starts, table_size, pos_ref, *refs):
    pieces = refs[: len(piece_starts)]
    outs = refs[len(piece_starts):]
    grids, (square, left_far, table, left, sems) = outs[:9], outs[9:]
    near = 9 * row_count
    group = row_count * width
    copies = load_pieces(pieces, piece_starts, table, sems)
    table[table_size] = jnp.zeros((width, width), table.dtype)
    for copy in copies:
        copy.wait()

    def block(m, k):
        return table[jnp.minimum(pos_ref[m * near + k], table_size)]

    for r in range(row_count):
        for k in range(near):
            left[r * width:(r + 1) * width, k * width:(k + 1) * width] = block(r, k)
    left_far[...] = left[:, NEAR_PARTS * group:]
    for part in range(9):
        parts = [q for q in reach(part) if q < NEAR_PARTS]
        for i, q in enumerate(parts):
            for r in range(row_count):
                for k in range(row_count):
                    low = (i * row_count + r) * width
                    grids[part][low:low + width, k * width:(k + 1) * width] = block(
                        q * row_count + r, part * row_count + k
                    )
        square[part] = jnp.dot(
            lanes_of(left, parts, group), grids[part][...], preferred_element_type=jnp.float32
        )


def square_near(positions, pieces, piece_starts, table_size, row_count, width):
    group = row_count * width
    span = 9 * group
    return pl.pallas_call(
        functools.partial(near_kernel, row_count, width, piece_starts, table_size),
        out_shape=[
            pltpu.VMEM((near_count(part) * group, group), jnp.bfloat16) for part in range(9)
        ] + [
            pltpu.VMEM((9, group, group), jnp.float32),
            pltpu.VMEM((group, (9 - NEAR_PARTS) * group), jnp.bfloat16),
        ],
        in_specs=[pl.BlockSpec(memory_space=pltpu.SMEM)]
        + [pl.BlockSpec(memory_space=pl.ANY)] * len(pieces),
        out_specs=[pl.BlockSpec(memory_space=pltpu.VMEM)] * 11,
        scratch_shapes=[
            pltpu.VMEM((table_size + 1, width, width), jnp.bfloat16),
            pltpu.VMEM((group, span), jnp.bfloat16),
            pltpu.SemaphoreType.DMA((len(pieces),)),
        ],
        compiler_params=pltpu.CompilerParams(vmem_limit_bytes=20 << 20),
        name="square_near",
    )(positions, *pieces)


def far_kernel(row_count, width, piece_starts, table_start, table_size, pos_ref, slot_ref, *refs):
    pieces = refs[: len(piece_starts)]
    outs = refs[len(piece_starts):]
    near_grids = outs[:9]
    square_in, left, out_ref, table, grid, square, square_b, staged, sems, out_sem = outs[9:]
    near = 9 * row_count
    group = row_count * width
    zero_at = table_start + table_size
    copies = load_pieces(pieces, piece_starts, table, sems)
    table[table_size] = jnp.zeros((width, width), table.dtype)
    for copy in copies:
        copy.wait()

    for part in range(9):
        parts = reach(part)
        base = near_count(part)
        far_base = sum(far_count(q) for q in range(part)) * group
        for i, q in enumerate(parts[base:]):
            for r in range(row_count):
                for k in range(row_count):
                    low = far_base + (i * row_count + r) * width
                    grid[low:low + width, k * width:(k + 1) * width] = table[
                        pos_ref[(q * row_count + r) * near + part * row_count + k] - table_start
                    ]
        product = square_in[part]
        if base < len(parts):
            product = product + jnp.dot(
                lanes_of(left, [q - NEAR_PARTS for q in parts[base:]], group),
                grid[far_base:far_base + far_count(part) * group],
                preferred_element_type=jnp.float32,
            )
        square[part] = product
        for r in range(row_count):
            for k in range(row_count):
                listed = pos_ref[r * near + part * row_count + k] != zero_at
                low = part * group + k * width
                square_b[r * width:(r + 1) * width, low:low + width] = jnp.where(
                    listed, product[r * width:(r + 1) * width, k * width:(k + 1) * width], 0.0
                ).astype(jnp.bfloat16)

    blocks = out_ref.shape[0]
    for part in range(9):
        parts = reach(part)
        base = near_count(part)
        far_base = sum(far_count(q) for q in range(part)) * group
        product = jnp.dot(
            lanes_of(square_b, parts[:base], group), near_grids[part][...],
            preferred_element_type=jnp.float32,
        )
        if base < len(parts):
            product = product + jnp.dot(
                lanes_of(square_b, parts[base:], group),
                grid[far_base:far_base + far_count(part) * group],
                preferred_element_type=jnp.float32,
            )
        result = 3.0 * square[part] - 2.0 * product
        for r in range(row_count):
            for k in range(row_count):
                slot = slot_ref[r * near + part * row_count + k]
                staged[slot] = result[r * width:(r + 1) * width, k * width:(k + 1) * width]

                @pl.when(slot < blocks)
                def _():
                    pltpu.make_async_copy(staged.at[slot], out_ref.at[slot], out_sem).start()

    pltpu.make_async_copy(staged.at[pl.ds(0, blocks)], out_ref, out_sem).wait()


def purify_far(
    positions, out_slots, pieces, piece_starts, carried, table_start, table_size,
    row_count, slot_count, width,
):
    group = row_count * width
    span = 9 * group
    blocks = row_count * slot_count
    return pl.pallas_call(
        functools.partial(
            far_kernel, row_count, width, piece_starts, table_start, table_size
        ),
        out_shape=jax.ShapeDtypeStruct((blocks, width, width), jnp.float32),
        in_specs=[pl.BlockSpec(memory_space=pltpu.SMEM)] * 2
        + [pl.BlockSpec(memory_space=pl.ANY)] * len(pieces)
        + [pl.BlockSpec(memory_space=pltpu.VMEM)] * len(carried),
        out_specs=pl.BlockSpec(memory_space=pl.ANY),
        scratch_shapes=[
            pltpu.VMEM((table_size + 1, width, width), jnp.bfloat16),
            pltpu.VMEM((sum(far_count(part) for part in range(9)) * group, group), jnp.bfloat16),
            pltpu.VMEM((9, group, group), jnp.float32),
            pltpu.VMEM((group, span), jnp.bfloat16),
            pltpu.VMEM((blocks + 1, width, width), jnp.float32),
            pltpu.SemaphoreType.DMA((len(pieces),)),
            pltpu.SemaphoreType.DMA,
        ],
        compiler_params=pltpu.CompilerParams(vmem_limit_bytes=28 << 20),
        name="purify_far",
    )(
        positions, out_slots, *pieces,
        *[pltpu.with_memory_space_constraint(array, pltpu.VMEM) for array in carried],
    )


def block_positions(neighbours, here_x, here_y, starts, zero_at):
    wide_count, narrow_count, row_count, slot_count = neighbours.shape
    total_rows = wide_count * narrow_count * row_count
    listing = neighbours.reshape(total_rows, slot_count)
    ids = jnp.arange(9 * row_count, dtype=jnp.int32)
    wide, narrow, inner = ids // (3 * row_count), ids // row_count % 3, ids % row_count
    beyond = jnp.where(here_x % 2 == 0, here_x + wide_count - 1, here_x + 1) % wide_count
    near_x = jnp.where(wide == 0, here_x, jnp.where(wide == 1, here_x ^ 1, beyond))
    near_y = jnp.where(
        narrow == 0, here_y, jnp.where(narrow == 1, here_y ^ 1, narrow_count - 1 - here_y)
    )
    rows = (near_x * narrow_count + near_y) * row_count + inner
    lists = jnp.take(listing, rows, axis=0)
    list_x = lists // (narrow_count * row_count)
    list_y = lists // row_count % narrow_count
    kind = jnp.where(
        list_x == (near_x ^ 1)[:, None], 2, jnp.where(list_y == (near_y ^ 1)[:, None], 1, 0)
    )
    slot_ids = jnp.arange(slot_count, dtype=jnp.int32)
    key = kind * slot_count + slot_ids
    place = jnp.sum((key[:, :, None] > key[:, None, :]).astype(jnp.int32), axis=2)
    part = wide * 3 + narrow
    start = jnp.zeros_like(part)
    for i, value in enumerate(starts):
        start = jnp.where(part == i, value, start)
    held_at = (start + inner)[:, None] + place * row_count
    matches = lists[:, None, :] == rows[None, :, None]
    positions = jnp.min(jnp.where(matches, held_at[:, None, :], zero_at), axis=2)
    own_matches = matches[:row_count]
    own_slots = slot_ids + slot_count * jnp.arange(row_count, dtype=jnp.int32)[:, None, None]
    out_slots = jnp.min(jnp.where(own_matches, own_slots, row_count * slot_count), axis=2)
    order = (place[:row_count] * row_count + inner[:row_count, None]).reshape(-1)
    flat_ids = jnp.arange(row_count * slot_count, dtype=jnp.int32)
    source = jnp.sum(jnp.where(order[None, :] == flat_ids[:, None], flat_ids[None, :], 0), axis=1)
    return (
        positions.astype(jnp.int32).reshape(-1),
        out_slots.astype(jnp.int32).reshape(-1),
        source.astype(jnp.int32),
    )


def per_device(density, neighbours, ent_blocks, ent_owner, ent_place):
    wide_count = lax.axis_size("gx")
    narrow_count = lax.axis_size("gy")
    device_count = wide_count * narrow_count
    here_x = lax.axis_index("gx")
    here_y = lax.axis_index("gy")
    self_index = here_x * narrow_count + here_y
    row_count = density.shape[2]
    slot_count = density.shape[3]
    width = density.shape[4]
    blocks = row_count * slot_count
    held = ent_blocks.shape[0]
    owners = ent_owner.reshape(device_count, held)
    places = ent_place.reshape(device_count, held)

    my_owners = lax.dynamic_index_in_dim(owners, self_index, 0, False)
    entry_ids = jnp.arange(held, dtype=jnp.int32)
    same = my_owners[:, None] == my_owners[None, :]
    my_ranks = jnp.sum(same & (entry_ids[None, :] < entry_ids[:, None]), axis=1)
    slots = (my_owners * C + my_ranks).astype(jnp.int32)
    outgoing = pack(ent_blocks, slots, device_count * C)
    received = lax.all_to_all(
        outgoing.reshape(device_count, C, width, width),
        ("gx", "gy"), split_axis=0, concat_axis=0, tiled=True,
    ).reshape(device_count * C, width, width)

    for_me = (owners == self_index).astype(jnp.int32)
    rank = jnp.cumsum(for_me, axis=1) - for_me
    picked = (for_me[:, :, None] == 1) & (
        rank[:, :, None] == jnp.arange(C, dtype=jnp.int32)[None, None, :]
    )
    slot_place = jnp.sum(jnp.where(picked, places[:, :, None], 0), axis=1).reshape(-1)
    slot_used = jnp.any(picked, axis=1).reshape(-1)
    slot_place = jnp.where(slot_used, slot_place, blocks)
    slot_ids = jnp.arange(device_count * C, dtype=jnp.int32)
    ahead = (slot_place[:, None] > slot_place[None, :]) | (
        (slot_place[:, None] == slot_place[None, :]) & (slot_ids[:, None] > slot_ids[None, :])
    )
    sorted_at = jnp.sum(ahead, axis=1)
    order = jnp.sum(
        jnp.where(sorted_at[None, :] == slot_ids[:, None], slot_ids[None, :], 0), axis=1
    ).astype(jnp.int32)
    target_ids = jnp.arange(blocks + 1, dtype=jnp.int32)
    first = jnp.sum(slot_place[None, :] < target_ids[:, None], axis=1).astype(jnp.int32)

    near_blocks = row_count * min(slot_count, 6 * row_count)
    corner_blocks = row_count * min(slot_count, 4 * row_count)
    sizes = [blocks] * 6 + [near_blocks, near_blocks, corner_blocks]
    starts = [sum(sizes[:i]) for i in range(9)]
    zero_at = sum(sizes)
    positions, out_slots, source = block_positions(neighbours, here_x, here_y, starts, zero_at)

    cut = corner_blocks // 2
    spans = ((0, cut), (cut, 2 * cut), (0, 2 * cut), (2 * cut, blocks))
    received, first, order, source, positions, out_slots = lax.optimization_barrier(
        (received, first, order, source, positions, out_slots)
    )
    own_1, own_2, own_12, own_3 = admit(
        density.reshape(blocks, width, width), received, first, order, source, spans
    )

    axes = ("gx", "gy")
    devices = [(x, y) for x in range(wide_count) for y in range(narrow_count)]

    def send(array, target):
        pairs = []
        for x, y in devices:
            to_x, to_y = target(x, y)
            pairs.append((x * narrow_count + y, to_x % wide_count * narrow_count + to_y))
        return lax.ppermute(array, axes, pairs)

    def across(x, y):
        return x, narrow_count - 1 - y

    def chip(x, y):
        return x, y ^ 1

    def ring(x, y):
        return x ^ 1, narrow_count - 1 - y

    def onward(x, y):
        return (x + 2 if x % 2 == 0 else x - 2), y

    ring_across_1 = send(own_1, ring)
    own_across_3 = send(own_3, across)
    ring_across_2 = send(own_2, ring)
    own_chip_12 = send(own_12, chip)
    own_chip_3 = send(own_3, chip)
    far_across_1 = send(ring_across_1, onward)
    ring_same_1 = send(ring_across_1, across)
    ring_same_3 = send(own_across_3, ring)
    far_across_2 = send(ring_across_2, onward)
    ring_same_2 = send(ring_across_2, across)
    ring_across_3 = send(own_3, ring)
    own_across_12 = send(own_12, across)
    far_same_1 = send(ring_same_1, onward)
    ring_chip_1 = send(ring_same_1, chip)
    far_same_2 = send(ring_same_2, onward)
    ring_chip_2 = send(ring_same_2, chip)
    far_same_3 = send(ring_same_3[:near_blocks - 2 * cut], onward)
    ring_chip_3 = send(ring_same_3, chip)
    far_chip_1 = send(far_same_1, chip)
    far_chip_2 = send(far_same_2, chip)
    far_chip_3 = send(far_same_3, chip)

    near_pieces = [
        (own_12, 0, 0), (own_3, 0, 2 * cut), (own_chip_12, 1, 0), (own_chip_3, 1, 2 * cut),
        (own_across_12, 2, 0), (own_across_3, 2, 2 * cut),
        (ring_same_1, 3, 0), (ring_same_2, 3, cut), (ring_same_3, 3, 2 * cut),
        (ring_chip_1, 4, 0), (ring_chip_2, 4, cut), (ring_chip_3, 4, 2 * cut),
        (ring_across_1, 5, 0), (ring_across_2, 5, cut), (ring_across_3, 5, 2 * cut),
    ]
    far_pieces = [
        (far_same_1, 6, 0), (far_same_2, 6, cut), (far_same_3, 6, 2 * cut),
        (far_chip_1, 7, 0), (far_chip_2, 7, cut), (far_chip_3, 7, 2 * cut),
        (far_across_1, 8, 0), (far_across_2, 8, cut),
    ]
    far_start = starts[NEAR_PARTS]
    carried = square_near(
        positions, [piece for piece, _, _ in near_pieces],
        [starts[part] + offset for _, part, offset in near_pieces],
        far_start, row_count, width,
    )
    purified = purify_far(
        positions, out_slots, [piece for piece, _, _ in far_pieces],
        [starts[part] + offset - far_start for _, part, offset in far_pieces],
        carried, far_start, zero_at - far_start, row_count, slot_count, width,
    )
    return purified.reshape(density.shape)


def solution(mesh):
    in_specs = (P("gx", "gy", None, None, None, None), P(), P(("gx", "gy"), None, None), P(), P())
    out_specs = P("gx", "gy", None, None, None, None)
    return jax.shard_map(
        per_device, mesh=mesh, in_specs=in_specs, out_specs=out_specs, check_vma=False
    )
```

```python
import functools

import jax
import jax.numpy as jnp
from jax import lax
from jax.experimental import pallas as pl
from jax.experimental.pallas import tpu as pltpu
from jax.sharding import PartitionSpec as P

C = 2


def pack_kernel(slots_ref, ent_ref, out_ref, staged, load_sems, store_sem):
    count = ent_ref.shape[0]
    parts = load_sems.shape[0]
    size = count // parts
    loads = []
    for p in range(parts):
        rows = pl.ds(p * size, size)
        loads.append(pltpu.make_async_copy(ent_ref.at[rows], staged.at[rows], load_sems.at[p]))
        loads[-1].start()

    def issue(i, carry):
        pltpu.make_async_copy(staged.at[i], out_ref.at[slots_ref[i]], store_sem).start()
        return carry

    for p in range(parts):
        loads[p].wait()
        lax.fori_loop(p * size, (p + 1) * size, issue, 0)
    pltpu.make_async_copy(staged, out_ref.at[pl.ds(0, count)], store_sem).wait()


def pack(ent_blocks, slots, total):
    return pl.pallas_call(
        pack_kernel,
        out_shape=jax.ShapeDtypeStruct((total,) + ent_blocks.shape[1:], ent_blocks.dtype),
        in_specs=[
            pl.BlockSpec(memory_space=pltpu.SMEM),
            pl.BlockSpec(memory_space=pl.ANY),
        ],
        out_specs=pl.BlockSpec(memory_space=pl.ANY),
        scratch_shapes=[
            pltpu.VMEM(ent_blocks.shape, ent_blocks.dtype),
            pltpu.SemaphoreType.DMA((4,)),
            pltpu.SemaphoreType.DMA,
        ],
        name="pack",
    )(slots, ent_blocks)


def admit_kernel(spans, first_ref, order_ref, source_ref, density_ref, received_ref, *refs):
    part_refs, own, sems = refs[: len(spans)], refs[len(spans)], refs[len(spans) + 1]

    def add(j, total):
        return total + received_ref[order_ref[j]].astype(jnp.float32)

    def place(p, carry):
        t = source_ref[p]
        total = lax.fori_loop(
            first_ref[t], first_ref[t + 1], add, density_ref[t].astype(jnp.float32)
        )
        own[p] = total.astype(own.dtype)
        return carry

    copies = []
    done = 0
    for i, (low, high) in enumerate(spans):
        if high > done:
            lax.fori_loop(done, high, place, 0)
            done = high
        copy = pltpu.make_async_copy(own.at[pl.ds(low, high - low)], part_refs[i], sems.at[i])
        copy.start()
        copies.append(copy)
    for copy in copies:
        copy.wait()


def admit(density, received, first, order, source, spans):
    return pl.pallas_call(
        functools.partial(admit_kernel, spans),
        out_shape=[
            jax.ShapeDtypeStruct((high - low,) + density.shape[1:], density.dtype)
            for low, high in spans
        ],
        in_specs=[pl.BlockSpec(memory_space=pltpu.SMEM)] * 3
        + [pl.BlockSpec(memory_space=pltpu.VMEM)] * 2,
        out_specs=[pl.BlockSpec(memory_space=pl.ANY)] * len(spans),
        scratch_shapes=[
            pltpu.VMEM(density.shape, density.dtype),
            pltpu.SemaphoreType.DMA((len(spans),)),
        ],
        name="admit",
    )(first, order, source, density, received)


def reach(part):
    wide, narrow = divmod(part, 3)
    wides = (0, 1, 2) if wide == 0 else (0, wide)
    narrows = (0, 1, 2) if narrow == 0 else (0, narrow)
    return [w * 3 + n for w in wides for n in narrows]


FAR_PARTS = (6, 7)


def near_of(part):
    return [q for q in reach(part) if q not in FAR_PARTS]


def far_of(part):
    return [q for q in reach(part) if q in FAR_PARTS]


def load_pieces(pieces, piece_starts, table, sems):
    copies = []
    for i, (piece, start) in enumerate(zip(pieces, piece_starts)):
        copies.append(
            pltpu.make_async_copy(piece, table.at[pl.ds(start, piece.shape[0])], sems.at[i])
        )
        copies[-1].start()
    return copies


def lanes_of(ref, parts, group):
    return jnp.concatenate([ref[:, q * group:(q + 1) * group] for q in parts], axis=1)


def near_kernel(row_count, width, piece_starts, table_size, pos_ref, *refs):
    pieces = refs[: len(piece_starts)]
    outs = refs[len(piece_starts):]
    grids, (square, left_far, table, left, sems) = outs[:9], outs[9:]
    near = 9 * row_count
    group = row_count * width
    copies = load_pieces(pieces, piece_starts, table, sems)
    table[table_size] = jnp.zeros((width, width), table.dtype)
    for copy in copies:
        copy.wait()

    def block(m, k):
        return table[jnp.minimum(pos_ref[m * near + k], table_size)]

    for r in range(row_count):
        for k in range(near):
            left[r * width:(r + 1) * width, k * width:(k + 1) * width] = block(r, k)
    left_far[...] = lanes_of(left, FAR_PARTS, group)
    for part in range(9):
        parts = near_of(part)
        for i, q in enumerate(parts):
            for r in range(row_count):
                for k in range(row_count):
                    low = (i * row_count + r) * width
                    grids[part][low:low + width, k * width:(k + 1) * width] = block(
                        q * row_count + r, part * row_count + k
                    )
        square[part] = jnp.dot(
            lanes_of(left, parts, group), grids[part][...], preferred_element_type=jnp.float32
        )


def square_near(positions, pieces, piece_starts, table_size, row_count, width):
    group = row_count * width
    span = 9 * group
    return pl.pallas_call(
        functools.partial(near_kernel, row_count, width, piece_starts, table_size),
        out_shape=[
            pltpu.VMEM((len(near_of(part)) * group, group), jnp.bfloat16) for part in range(9)
        ] + [
            pltpu.VMEM((9, group, group), jnp.float32),
            pltpu.VMEM((group, len(FAR_PARTS) * group), jnp.bfloat16),
        ],
        in_specs=[pl.BlockSpec(memory_space=pltpu.SMEM)]
        + [pl.BlockSpec(memory_space=pl.ANY)] * len(pieces),
        out_specs=[pl.BlockSpec(memory_space=pltpu.VMEM)] * 11,
        scratch_shapes=[
            pltpu.VMEM((table_size + 1, width, width), jnp.bfloat16),
            pltpu.VMEM((group, span), jnp.bfloat16),
            pltpu.SemaphoreType.DMA((len(pieces),)),
        ],
        compiler_params=pltpu.CompilerParams(vmem_limit_bytes=20 << 20),
        name="square_near",
    )(positions, *pieces)


def far_kernel(row_count, width, piece_starts, table_start, table_size, pos_ref, slot_ref, *refs):
    pieces = refs[: len(piece_starts)]
    outs = refs[len(piece_starts):]
    near_grids = outs[:9]
    square_in, left, out_ref, table, grid, square, square_b, staged, sems, out_sem = outs[9:]
    near = 9 * row_count
    group = row_count * width
    zero_at = table_start + table_size
    copies = load_pieces(pieces, piece_starts, table, sems)
    table[table_size] = jnp.zeros((width, width), table.dtype)
    for copy in copies:
        copy.wait()

    for part in range(9):
        parts = far_of(part)
        far_base = sum(len(far_of(q)) for q in range(part)) * group
        for i, q in enumerate(parts):
            for r in range(row_count):
                for k in range(row_count):
                    low = far_base + (i * row_count + r) * width
                    grid[low:low + width, k * width:(k + 1) * width] = table[
                        pos_ref[(q * row_count + r) * near + part * row_count + k] - table_start
                    ]
        product = square_in[part]
        if parts:
            product = product + jnp.dot(
                lanes_of(left, [FAR_PARTS.index(q) for q in parts], group),
                grid[far_base:far_base + len(parts) * group],
                preferred_element_type=jnp.float32,
            )
        square[part] = product
        for r in range(row_count):
            for k in range(row_count):
                listed = pos_ref[r * near + part * row_count + k] != zero_at
                low = part * group + k * width
                square_b[r * width:(r + 1) * width, low:low + width] = jnp.where(
                    listed, product[r * width:(r + 1) * width, k * width:(k + 1) * width], 0.0
                ).astype(jnp.bfloat16)

    blocks = out_ref.shape[0]
    for part in range(9):
        parts = far_of(part)
        far_base = sum(len(far_of(q)) for q in range(part)) * group
        product = jnp.dot(
            lanes_of(square_b, near_of(part), group), near_grids[part][...],
            preferred_element_type=jnp.float32,
        )
        if parts:
            product = product + jnp.dot(
                lanes_of(square_b, parts, group),
                grid[far_base:far_base + len(parts) * group],
                preferred_element_type=jnp.float32,
            )
        result = 3.0 * square[part] - 2.0 * product
        for r in range(row_count):
            for k in range(row_count):
                slot = slot_ref[r * near + part * row_count + k]
                staged[slot] = result[r * width:(r + 1) * width, k * width:(k + 1) * width]

                @pl.when(slot < blocks)
                def _():
                    pltpu.make_async_copy(staged.at[slot], out_ref.at[slot], out_sem).start()

    pltpu.make_async_copy(staged.at[pl.ds(0, blocks)], out_ref, out_sem).wait()


def purify_far(
    positions, out_slots, pieces, piece_starts, carried, table_start, table_size,
    row_count, slot_count, width,
):
    group = row_count * width
    span = 9 * group
    blocks = row_count * slot_count
    return pl.pallas_call(
        functools.partial(
            far_kernel, row_count, width, piece_starts, table_start, table_size
        ),
        out_shape=jax.ShapeDtypeStruct((blocks, width, width), jnp.float32),
        in_specs=[pl.BlockSpec(memory_space=pltpu.SMEM)] * 2
        + [pl.BlockSpec(memory_space=pl.ANY)] * len(pieces)
        + [pl.BlockSpec(memory_space=pltpu.VMEM)] * len(carried),
        out_specs=pl.BlockSpec(memory_space=pl.ANY),
        scratch_shapes=[
            pltpu.VMEM((table_size + 1, width, width), jnp.bfloat16),
            pltpu.VMEM((sum(len(far_of(part)) for part in range(9)) * group, group), jnp.bfloat16),
            pltpu.VMEM((9, group, group), jnp.float32),
            pltpu.VMEM((group, span), jnp.bfloat16),
            pltpu.VMEM((blocks + 1, width, width), jnp.float32),
            pltpu.SemaphoreType.DMA((len(pieces),)),
            pltpu.SemaphoreType.DMA,
        ],
        compiler_params=pltpu.CompilerParams(vmem_limit_bytes=28 << 20),
        name="purify_far",
    )(
        positions, out_slots, *pieces,
        *[pltpu.with_memory_space_constraint(array, pltpu.VMEM) for array in carried],
    )


def block_positions(neighbours, here_x, here_y, starts, zero_at):
    wide_count, narrow_count, row_count, slot_count = neighbours.shape
    total_rows = wide_count * narrow_count * row_count
    listing = neighbours.reshape(total_rows, slot_count)
    ids = jnp.arange(9 * row_count, dtype=jnp.int32)
    wide, narrow, inner = ids // (3 * row_count), ids // row_count % 3, ids % row_count
    beyond = jnp.where(here_x % 2 == 0, here_x + wide_count - 1, here_x + 1) % wide_count
    near_x = jnp.where(wide == 0, here_x, jnp.where(wide == 1, here_x ^ 1, beyond))
    near_y = jnp.where(
        narrow == 0, here_y, jnp.where(narrow == 1, here_y ^ 1, narrow_count - 1 - here_y)
    )
    rows = (near_x * narrow_count + near_y) * row_count + inner
    lists = jnp.take(listing, rows, axis=0)
    list_x = lists // (narrow_count * row_count)
    list_y = lists // row_count % narrow_count
    aside = list_y == (near_y ^ 1)[:, None]
    kind = jnp.where(
        list_x == (near_x ^ 1)[:, None], jnp.where(aside, 2, 3), jnp.where(aside, 1, 0)
    )
    slot_ids = jnp.arange(slot_count, dtype=jnp.int32)
    key = kind * slot_count + slot_ids
    place = jnp.sum((key[:, :, None] > key[:, None, :]).astype(jnp.int32), axis=2)
    part = wide * 3 + narrow
    start = jnp.zeros_like(part)
    for i, value in enumerate(starts):
        start = jnp.where(part == i, value, start)
    held_at = (start + inner)[:, None] + place * row_count
    matches = lists[:, None, :] == rows[None, :, None]
    positions = jnp.min(jnp.where(matches, held_at[:, None, :], zero_at), axis=2)
    own_matches = matches[:row_count]
    own_slots = slot_ids + slot_count * jnp.arange(row_count, dtype=jnp.int32)[:, None, None]
    out_slots = jnp.min(jnp.where(own_matches, own_slots, row_count * slot_count), axis=2)
    order = (place[:row_count] * row_count + inner[:row_count, None]).reshape(-1)
    flat_ids = jnp.arange(row_count * slot_count, dtype=jnp.int32)
    source = jnp.sum(jnp.where(order[None, :] == flat_ids[:, None], flat_ids[None, :], 0), axis=1)
    return (
        positions.astype(jnp.int32).reshape(-1),
        out_slots.astype(jnp.int32).reshape(-1),
        source.astype(jnp.int32),
    )


def per_device(density, neighbours, ent_blocks, ent_owner, ent_place):
    wide_count = lax.axis_size("gx")
    narrow_count = lax.axis_size("gy")
    device_count = wide_count * narrow_count
    here_x = lax.axis_index("gx")
    here_y = lax.axis_index("gy")
    self_index = here_x * narrow_count + here_y
    row_count = density.shape[2]
    slot_count = density.shape[3]
    width = density.shape[4]
    blocks = row_count * slot_count
    held = ent_blocks.shape[0]
    owners = ent_owner.reshape(device_count, held)
    places = ent_place.reshape(device_count, held)

    my_owners = lax.dynamic_slice(ent_owner, (self_index * held,), (held,))
    entry_ids = jnp.arange(held, dtype=jnp.int32)
    same = my_owners[:, None] == my_owners[None, :]
    my_ranks = jnp.sum(same & (entry_ids[None, :] < entry_ids[:, None]), axis=1)
    slots = (my_owners * C + my_ranks).astype(jnp.int32)
    outgoing = pack(ent_blocks, slots, device_count * C)
    received = lax.all_to_all(
        outgoing.reshape(device_count, C, width, width),
        ("gx", "gy"), split_axis=0, concat_axis=0, tiled=True,
    ).reshape(device_count * C, width, width)

    for_me = (owners == self_index).astype(jnp.int32)
    rank = jnp.cumsum(for_me, axis=1) - for_me
    picked = (for_me[:, :, None] == 1) & (
        rank[:, :, None] == jnp.arange(C, dtype=jnp.int32)[None, None, :]
    )
    slot_place = jnp.sum(jnp.where(picked, places[:, :, None], 0), axis=1).reshape(-1)
    slot_used = jnp.any(picked, axis=1).reshape(-1)
    slot_place = jnp.where(slot_used, slot_place, blocks)
    slot_ids = jnp.arange(device_count * C, dtype=jnp.int32)
    ahead = (slot_place[:, None] > slot_place[None, :]) | (
        (slot_place[:, None] == slot_place[None, :]) & (slot_ids[:, None] > slot_ids[None, :])
    )
    sorted_at = jnp.sum(ahead, axis=1)
    order = jnp.sum(
        jnp.where(sorted_at[None, :] == slot_ids[:, None], slot_ids[None, :], 0), axis=1
    ).astype(jnp.int32)
    target_ids = jnp.arange(blocks + 1, dtype=jnp.int32)
    first = jnp.sum(slot_place[None, :] < target_ids[:, None], axis=1).astype(jnp.int32)

    near_blocks = row_count * min(slot_count, 6 * row_count)
    corner_blocks = row_count * min(slot_count, 4 * row_count)
    layout = [(part, blocks) for part in range(6)]
    layout += [(8, corner_blocks), (6, near_blocks), (7, near_blocks)]
    starts, zero_at = [0] * 9, 0
    for part, size in layout:
        starts[part], zero_at = zero_at, zero_at + size
    far_start = starts[6]
    positions, out_slots, source = block_positions(neighbours, here_x, here_y, starts, zero_at)

    cut = corner_blocks // 3
    tail = blocks - 6 * row_count
    spans = (
        (0, cut), (cut, 2 * cut), (0, 2 * cut), (2 * cut, 3 * cut), (2 * cut, blocks), (tail, blocks)
    )
    received, first, order, source, positions, out_slots = lax.optimization_barrier(
        (received, first, order, source, positions, out_slots)
    )
    own_1, own_2, own_12, own_3, own_34, own_4 = admit(
        density.reshape(blocks, width, width), received, first, order, source, spans
    )

    axes = ("gx", "gy")
    devices = [(x, y) for x in range(wide_count) for y in range(narrow_count)]

    def send(array, target):
        pairs = []
        for x, y in devices:
            to_x, to_y = target(x, y)
            pairs.append((x * narrow_count + y, to_x % wide_count * narrow_count + to_y))
        return lax.ppermute(array, axes, pairs)

    def across(x, y):
        return x, narrow_count - 1 - y

    def chip(x, y):
        return x, y ^ 1

    def ring(x, y):
        return x ^ 1, narrow_count - 1 - y

    def onward(x, y):
        return (x + 2 if x % 2 == 0 else x - 2), y

    ring_across_1 = send(own_1, ring)
    own_across_34 = send(own_34, across)
    ring_across_2 = send(own_2, ring)
    ring_across_3 = send(own_3, ring)
    far_across_1 = send(ring_across_1, onward)
    ring_same_1 = send(ring_across_1, across)
    far_across_2 = send(ring_across_2, onward)
    ring_same_2 = send(ring_across_2, across)
    ring_same_3 = send(own_across_34, ring)
    far_across_3 = send(ring_across_3, onward)
    ring_across_4 = send(own_4, ring)
    own_across_12 = send(own_12, across)
    own_chip_12 = send(own_12, chip)
    own_chip_34 = send(own_34, chip)
    far_same_1 = send(ring_same_1, onward)
    ring_chip_1 = send(ring_same_1, chip)
    far_same_2 = send(ring_same_2, onward)
    ring_chip_2 = send(ring_same_2, chip)
    far_same_3 = send(ring_same_3[:near_blocks - 2 * cut], onward)
    ring_chip_3 = send(ring_same_3, chip)
    far_chip_1 = send(far_same_1, chip)
    far_chip_2 = send(far_same_2, chip)
    far_chip_3 = send(far_same_3, chip)

    near_pieces = [
        (own_12, 0, 0), (own_34, 0, 2 * cut), (own_chip_12, 1, 0), (own_chip_34, 1, 2 * cut),
        (own_across_12, 2, 0), (own_across_34, 2, 2 * cut),
        (ring_same_1, 3, 0), (ring_same_2, 3, cut), (ring_same_3, 3, 2 * cut),
        (ring_chip_1, 4, 0), (ring_chip_2, 4, cut), (ring_chip_3, 4, 2 * cut),
        (ring_across_1, 5, 0), (ring_across_2, 5, cut), (ring_across_3, 5, 2 * cut),
        (ring_across_4, 5, tail),
        (far_across_1, 8, 0), (far_across_2, 8, cut), (far_across_3, 8, 2 * cut),
    ]
    far_pieces = [
        (far_same_1, 6, 0), (far_same_2, 6, cut), (far_same_3, 6, 2 * cut),
        (far_chip_1, 7, 0), (far_chip_2, 7, cut), (far_chip_3, 7, 2 * cut),
    ]
    carried = square_near(
        positions, [piece for piece, _, _ in near_pieces],
        [starts[part] + offset for _, part, offset in near_pieces],
        far_start, row_count, width,
    )
    purified = purify_far(
        positions, out_slots, [piece for piece, _, _ in far_pieces],
        [starts[part] + offset - far_start for _, part, offset in far_pieces],
        carried, far_start, zero_at - far_start, row_count, slot_count, width,
    )
    return purified.reshape(density.shape)


def solution(mesh):
    in_specs = (P("gx", "gy", None, None, None, None), P(), P(("gx", "gy"), None, None), P(), P())
    out_specs = P("gx", "gy", None, None, None, None)
    return jax.shard_map(
        per_device, mesh=mesh, in_specs=in_specs, out_specs=out_specs, check_vma=False
    )
```

```python
import functools

import jax
import jax.numpy as jnp
from jax import lax
from jax.experimental import pallas as pl
from jax.experimental.pallas import tpu as pltpu
from jax.sharding import PartitionSpec as P

C = 2


def pack_kernel(slots_ref, ent_ref, out_ref, staged, load_sems, store_sem):
    count = ent_ref.shape[0]
    parts = load_sems.shape[0]
    size = count // parts
    loads = []
    for p in range(parts):
        rows = pl.ds(p * size, size)
        loads.append(pltpu.make_async_copy(ent_ref.at[rows], staged.at[rows], load_sems.at[p]))
        loads[-1].start()

    def issue(i, carry):
        pltpu.make_async_copy(staged.at[i], out_ref.at[slots_ref[i]], store_sem).start()
        return carry

    for p in range(parts):
        loads[p].wait()
        lax.fori_loop(p * size, (p + 1) * size, issue, 0)
    pltpu.make_async_copy(staged, out_ref.at[pl.ds(0, count)], store_sem).wait()


def pack(ent_blocks, slots, total):
    return pl.pallas_call(
        pack_kernel,
        out_shape=jax.ShapeDtypeStruct((total,) + ent_blocks.shape[1:], ent_blocks.dtype),
        in_specs=[
            pl.BlockSpec(memory_space=pltpu.SMEM),
            pl.BlockSpec(memory_space=pl.ANY),
        ],
        out_specs=pl.BlockSpec(memory_space=pl.ANY),
        scratch_shapes=[
            pltpu.VMEM(ent_blocks.shape, ent_blocks.dtype),
            pltpu.SemaphoreType.DMA((4,)),
            pltpu.SemaphoreType.DMA,
        ],
        name="pack",
    )(slots, ent_blocks)


def admit_kernel(spans, first_ref, order_ref, target_ref, source_ref, density_ref, received_ref, *refs):
    part_refs = refs[: len(spans)]
    density, received, total, own, load_sem, chunk_sems, sems = refs[len(spans):]
    chunks = chunk_sems.shape[0]
    size = received.shape[0] // chunks
    density_load = pltpu.make_async_copy(density_ref, density, load_sem)
    density_load.start()
    loads = []
    for c in range(chunks):
        rows = pl.ds(c * size, size)
        load = pltpu.make_async_copy(received_ref.at[rows], received.at[rows], chunk_sems.at[c])
        load.start()
        loads.append(load)
    density_load.wait()

    def begin(p, carry):
        total[p] = density[source_ref[p]].astype(jnp.float32)
        return carry

    lax.fori_loop(0, own.shape[0], begin, 0)

    def add(j, carry):
        p = target_ref[j]
        total[p] = total[p] + received[order_ref[j]].astype(jnp.float32)
        return carry

    for c in range(chunks):
        loads[c].wait()
        lax.fori_loop(first_ref[c], first_ref[c + 1], add, 0)

    def finish(p, carry):
        own[p] = total[p].astype(own.dtype)
        return carry

    copies = []
    done = 0
    for i, (low, high) in enumerate(spans):
        if high > done:
            lax.fori_loop(done, high, finish, 0)
            done = high
        copy = pltpu.make_async_copy(own.at[pl.ds(low, high - low)], part_refs[i], sems.at[i])
        copy.start()
        copies.append(copy)
    for copy in copies:
        copy.wait()


RECEIVE_CHUNKS = 4


def admit(density, received, first, order, target, source, spans):
    return pl.pallas_call(
        functools.partial(admit_kernel, spans),
        out_shape=[
            jax.ShapeDtypeStruct((high - low,) + density.shape[1:], density.dtype)
            for low, high in spans
        ],
        in_specs=[pl.BlockSpec(memory_space=pltpu.SMEM)] * 4
        + [pl.BlockSpec(memory_space=pl.ANY)] * 2,
        out_specs=[pl.BlockSpec(memory_space=pl.ANY)] * len(spans),
        scratch_shapes=[
            pltpu.VMEM(density.shape, density.dtype),
            pltpu.VMEM(received.shape, received.dtype),
            pltpu.VMEM(density.shape, jnp.float32),
            pltpu.VMEM(density.shape, density.dtype),
            pltpu.SemaphoreType.DMA,
            pltpu.SemaphoreType.DMA((RECEIVE_CHUNKS,)),
            pltpu.SemaphoreType.DMA((len(spans),)),
        ],
        name="admit",
    )(first, order, target, source, density, received)


def reach(part):
    wide, narrow = divmod(part, 3)
    wides = (0, 1, 2) if wide == 0 else (0, wide)
    narrows = (0, 1, 2) if narrow == 0 else (0, narrow)
    return [w * 3 + n for w in wides for n in narrows]


FAR_PARTS = (6, 7, 8)


def near_of(part):
    return [q for q in reach(part) if q not in FAR_PARTS]


def middle_of(part):
    return [q for q in reach(part) if q // 3 == 1]


def inner_of(part):
    return [q for q in reach(part) if q // 3 == 0]


def masked(product, pos_ref, row_count, width, part, zero_at):
    near = 9 * row_count
    rows = []
    for r in range(row_count):
        row = []
        for k in range(row_count):
            listed = pos_ref[r * near + part * row_count + k] != zero_at
            block = product[r * width:(r + 1) * width, k * width:(k + 1) * width]
            row.append(jnp.where(listed, block, 0.0).astype(jnp.bfloat16))
        rows.append(jnp.concatenate(row, axis=1))
    return jnp.concatenate(rows, axis=0)


def far_of(part):
    return [q for q in reach(part) if q in FAR_PARTS]


def load_pieces(pieces, piece_starts, table, sems):
    copies = []
    for i, (piece, start) in enumerate(zip(pieces, piece_starts)):
        copies.append(
            pltpu.make_async_copy(piece, table.at[pl.ds(start, piece.shape[0])], sems.at[i])
        )
        copies[-1].start()
    return copies


def lanes_of(ref, parts, group):
    return jnp.concatenate([ref[:, q * group:(q + 1) * group] for q in parts], axis=1)


def near_kernel(row_count, width, piece_starts, table_size, zero_at, pos_ref, *refs):
    pieces = refs[: len(piece_starts)]
    outs = refs[len(piece_starts):]
    inner_grids, (square, cube, left_far, table, left, square_b, sems) = outs[:9], outs[9:16]
    outer_grids = outs[16:]
    near = 9 * row_count
    group = row_count * width
    copies = load_pieces(pieces, piece_starts, table, sems)
    table[table_size] = jnp.zeros((width, width), table.dtype)
    for copy in copies:
        copy.wait()

    def block(m, k):
        return table[jnp.minimum(pos_ref[m * near + k], table_size)]

    for r in range(row_count):
        for k in range(near):
            left[r * width:(r + 1) * width, k * width:(k + 1) * width] = block(r, k)
    left_far[...] = lanes_of(left, FAR_PARTS, group)
    for part in range(9):
        parts = near_of(part)
        for i, q in enumerate(parts):
            count = len(inner_of(part))
            ref, at = (inner_grids[part], i) if i < count else (outer_grids[part], i - count)
            for r in range(row_count):
                for k in range(row_count):
                    low = (at * row_count + r) * width
                    ref[low:low + width, k * width:(k + 1) * width] = block(
                        q * row_count + r, part * row_count + k
                    )
        product = jnp.dot(
            lanes_of(left, inner_of(part), group), inner_grids[part][...],
            preferred_element_type=jnp.float32,
        )
        if middle_of(part):
            product = product + jnp.dot(
                lanes_of(left, middle_of(part), group), outer_grids[part][...],
                preferred_element_type=jnp.float32,
            )
        square[part] = product
        if part // 3 == 1:
            lanes = slice((part - 3) * group, (part - 2) * group)
            square_b[:, lanes] = masked(product, pos_ref, row_count, width, part, zero_at)
    for part in range(6):
        product = jnp.dot(
            lanes_of(square_b, [q - 3 for q in middle_of(part)], group), outer_grids[part][...],
            preferred_element_type=jnp.float32,
        )
        if part < 3:
            cube[part] = product
        else:
            square[part] = 3.0 * square[part] - 2.0 * product


def square_near(positions, pieces, piece_starts, table_size, zero_at, row_count, width):
    group = row_count * width
    span = 9 * group
    return pl.pallas_call(
        functools.partial(near_kernel, row_count, width, piece_starts, table_size, zero_at),
        out_shape=[
            pltpu.VMEM((len(inner_of(part)) * group, group), jnp.bfloat16) for part in range(9)
        ] + [
            pltpu.VMEM((9, group, group), jnp.float32),
            pltpu.VMEM((3, group, group), jnp.float32),
            pltpu.VMEM((group, len(FAR_PARTS) * group), jnp.bfloat16),
        ],
        in_specs=[pl.BlockSpec(memory_space=pltpu.SMEM)]
        + [pl.BlockSpec(memory_space=pl.ANY)] * len(pieces),
        out_specs=[pl.BlockSpec(memory_space=pltpu.VMEM)] * 12,
        scratch_shapes=[
            pltpu.VMEM((table_size + 1, width, width), jnp.bfloat16),
            pltpu.VMEM((group, span), jnp.bfloat16),
            pltpu.VMEM((group, 3 * group), jnp.bfloat16),
            pltpu.SemaphoreType.DMA((len(pieces),)),
        ] + [
            pltpu.VMEM((len(middle_of(part)) * group, group), jnp.bfloat16) for part in range(6)
        ],
        compiler_params=pltpu.CompilerParams(vmem_limit_bytes=24 << 20),
        name="square_near",
    )(positions, *pieces)


def far_kernel(row_count, width, piece_starts, table_start, table_size, pos_ref, slot_ref, *refs):
    pieces = refs[: len(piece_starts)]
    outs = refs[len(piece_starts):]
    inner_grids = outs[:9]
    square_in, cube_in, left, out_ref, table, grid, square, square_b, staged, sems, out_sem = outs[9:]
    near = 9 * row_count
    group = row_count * width
    zero_at = table_start + table_size
    copies = load_pieces(pieces, piece_starts, table, sems)
    table[table_size] = jnp.zeros((width, width), table.dtype)
    for copy in copies:
        copy.wait()

    outer = [0, 1, 2, 6, 7, 8]
    for index, part in enumerate(outer):
        parts = far_of(part)
        far_base = sum(len(far_of(q)) for q in range(part)) * group
        for i, q in enumerate(parts):
            for r in range(row_count):
                for k in range(row_count):
                    low = far_base + (i * row_count + r) * width
                    grid[low:low + width, k * width:(k + 1) * width] = table[
                        pos_ref[(q * row_count + r) * near + part * row_count + k] - table_start
                    ]
        product = square_in[part] + jnp.dot(
            lanes_of(left, [FAR_PARTS.index(q) for q in parts], group),
            grid[far_base:far_base + len(parts) * group],
            preferred_element_type=jnp.float32,
        )
        square[index] = product
        square_b[:, index * group:(index + 1) * group] = masked(
            product, pos_ref, row_count, width, part, zero_at
        )

    blocks = out_ref.shape[0]
    for part in range(9):
        parts = far_of(part)
        far_base = sum(len(far_of(q)) for q in range(part)) * group
        product = jnp.dot(
            lanes_of(square_b, [outer.index(q) for q in inner_of(part)], group),
            inner_grids[part][...], preferred_element_type=jnp.float32,
        )
        if parts:
            product = product + jnp.dot(
                lanes_of(square_b, [outer.index(q) for q in parts], group),
                grid[far_base:far_base + len(parts) * group],
                preferred_element_type=jnp.float32,
            )
            if part < 3:
                product = product + cube_in[part]
            result = 3.0 * square[outer.index(part)] - 2.0 * product
        else:
            result = square_in[part] - 2.0 * product
        for r in range(row_count):
            for k in range(row_count):
                slot = slot_ref[r * near + part * row_count + k]
                staged[slot] = result[r * width:(r + 1) * width, k * width:(k + 1) * width]

                @pl.when(slot < blocks)
                def _():
                    pltpu.make_async_copy(staged.at[slot], out_ref.at[slot], out_sem).start()

    pltpu.make_async_copy(staged.at[pl.ds(0, blocks)], out_ref, out_sem).wait()


def purify_far(
    positions, out_slots, pieces, piece_starts, carried, table_start, table_size,
    row_count, slot_count, width,
):
    group = row_count * width
    blocks = row_count * slot_count
    return pl.pallas_call(
        functools.partial(
            far_kernel, row_count, width, piece_starts, table_start, table_size
        ),
        out_shape=jax.ShapeDtypeStruct((blocks, width, width), jnp.float32),
        in_specs=[pl.BlockSpec(memory_space=pltpu.SMEM)] * 2
        + [pl.BlockSpec(memory_space=pl.ANY)] * len(pieces)
        + [pl.BlockSpec(memory_space=pltpu.VMEM)] * len(carried),
        out_specs=pl.BlockSpec(memory_space=pl.ANY),
        scratch_shapes=[
            pltpu.VMEM((table_size + 1, width, width), jnp.bfloat16),
            pltpu.VMEM((sum(len(far_of(part)) for part in range(9)) * group, group), jnp.bfloat16),
            pltpu.VMEM((6, group, group), jnp.float32),
            pltpu.VMEM((group, 6 * group), jnp.bfloat16),
            pltpu.VMEM((blocks + 1, width, width), jnp.float32),
            pltpu.SemaphoreType.DMA((len(pieces),)),
            pltpu.SemaphoreType.DMA,
        ],
        compiler_params=pltpu.CompilerParams(vmem_limit_bytes=28 << 20),
        name="purify_far",
    )(
        positions, out_slots, *pieces,
        *[pltpu.with_memory_space_constraint(array, pltpu.VMEM) for array in carried],
    )


def block_positions(neighbours, here_x, here_y, starts, zero_at):
    wide_count, narrow_count, row_count, slot_count = neighbours.shape
    total_rows = wide_count * narrow_count * row_count
    listing = neighbours.reshape(total_rows, slot_count)
    ids = jnp.arange(9 * row_count, dtype=jnp.int32)
    wide, narrow, inner = ids // (3 * row_count), ids // row_count % 3, ids % row_count
    beyond = jnp.where(here_x % 2 == 0, here_x + wide_count - 1, here_x + 1) % wide_count
    near_x = jnp.where(wide == 0, here_x, jnp.where(wide == 1, here_x ^ 1, beyond))
    near_y = jnp.where(
        narrow == 0, here_y, jnp.where(narrow == 1, here_y ^ 1, narrow_count - 1 - here_y)
    )
    rows = (near_x * narrow_count + near_y) * row_count + inner
    lists = jnp.take(listing, rows, axis=0)
    list_x = lists // (narrow_count * row_count)
    list_y = lists // row_count % narrow_count
    aside = list_y == (near_y ^ 1)[:, None]
    kind = jnp.where(
        list_x == (near_x ^ 1)[:, None], jnp.where(aside, 2, 3), jnp.where(aside, 1, 0)
    )
    slot_ids = jnp.arange(slot_count, dtype=jnp.int32)
    key = kind * slot_count + slot_ids
    place = jnp.sum((key[:, :, None] > key[:, None, :]).astype(jnp.int32), axis=2)
    part = wide * 3 + narrow
    start = jnp.zeros_like(part)
    for i, value in enumerate(starts):
        start = jnp.where(part == i, value, start)
    held_at = (start + inner)[:, None] + place * row_count
    matches = lists[:, None, :] == rows[None, :, None]
    positions = jnp.min(jnp.where(matches, held_at[:, None, :], zero_at), axis=2)
    own_matches = matches[:row_count]
    own_slots = slot_ids + slot_count * jnp.arange(row_count, dtype=jnp.int32)[:, None, None]
    out_slots = jnp.min(jnp.where(own_matches, own_slots, row_count * slot_count), axis=2)
    order = (place[:row_count] * row_count + inner[:row_count, None]).reshape(-1)
    flat_ids = jnp.arange(row_count * slot_count, dtype=jnp.int32)
    source = jnp.sum(jnp.where(order[None, :] == flat_ids[:, None], flat_ids[None, :], 0), axis=1)
    return (
        positions.astype(jnp.int32).reshape(-1),
        out_slots.astype(jnp.int32).reshape(-1),
        source.astype(jnp.int32),
    )


def per_device(density, neighbours, ent_blocks, ent_owner, ent_place):
    wide_count = lax.axis_size("gx")
    narrow_count = lax.axis_size("gy")
    device_count = wide_count * narrow_count
    here_x = lax.axis_index("gx")
    here_y = lax.axis_index("gy")
    self_index = here_x * narrow_count + here_y
    row_count = density.shape[2]
    slot_count = density.shape[3]
    width = density.shape[4]
    blocks = row_count * slot_count
    held = ent_blocks.shape[0]
    owners = ent_owner.reshape(device_count, held)
    places = ent_place.reshape(device_count, held)

    my_owners = lax.dynamic_index_in_dim(owners, self_index, 0, False)
    entry_ids = jnp.arange(held, dtype=jnp.int32)
    same = my_owners[:, None] == my_owners[None, :]
    my_ranks = jnp.sum(same & (entry_ids[None, :] < entry_ids[:, None]), axis=1)
    slots = (my_owners * C + my_ranks).astype(jnp.int32)
    outgoing = pack(ent_blocks, slots, device_count * C)
    received = lax.all_to_all(
        outgoing.reshape(device_count, C, width, width),
        ("gx", "gy"), split_axis=0, concat_axis=0, tiled=True,
    ).reshape(device_count * C, width, width)

    for_me = (owners == self_index).astype(jnp.int32)
    rank = jnp.cumsum(for_me, axis=1) - for_me
    picked = (for_me[:, :, None] == 1) & (
        rank[:, :, None] == jnp.arange(C, dtype=jnp.int32)[None, None, :]
    )
    slot_place = jnp.sum(jnp.where(picked, places[:, :, None], 0), axis=1).reshape(-1)
    slot_used = jnp.any(picked, axis=1).reshape(-1)
    slot_ids = jnp.arange(device_count * C, dtype=jnp.int32)
    used = slot_used.astype(jnp.int32)
    ahead = jnp.sum(
        jnp.where(slot_ids[None, :] < slot_ids[:, None], used[None, :], 0), axis=1
    )
    chosen = slot_used[None, :] & (ahead[None, :] == slot_ids[:, None])
    order = jnp.sum(jnp.where(chosen, slot_ids[None, :], 0), axis=1).astype(jnp.int32)
    bounds = jnp.arange(RECEIVE_CHUNKS + 1, dtype=jnp.int32) * (device_count * C // RECEIVE_CHUNKS)
    first = jnp.sum(
        jnp.where(slot_ids[None, :] < bounds[:, None], used[None, :], 0), axis=1
    ).astype(jnp.int32)

    near_blocks = row_count * min(slot_count, 6 * row_count)
    corner_blocks = row_count * min(slot_count, 4 * row_count)
    layout = [(part, blocks) for part in range(6)]
    layout += [(6, near_blocks), (7, near_blocks), (8, corner_blocks)]
    starts, zero_at = [0] * 9, 0
    for part, size in layout:
        starts[part], zero_at = zero_at, zero_at + size
    far_start = starts[6]
    positions, out_slots, source = block_positions(neighbours, here_x, here_y, starts, zero_at)
    targets = jnp.arange(blocks, dtype=jnp.int32)
    slot_target = jnp.sum(
        jnp.where(source[None, :] == slot_place[:, None], targets[None, :], 0), axis=1
    )
    target = jnp.sum(jnp.where(chosen, slot_target[None, :], 0), axis=1).astype(jnp.int32)

    cut = corner_blocks // 3
    tail = blocks - 6 * row_count
    spans = (
        (0, cut), (cut, 2 * cut), (0, 2 * cut), (2 * cut, 3 * cut), (2 * cut, tail), (tail, blocks)
    )
    received, first, order, target, source, positions, out_slots = lax.optimization_barrier(
        (received, first, order, target, source, positions, out_slots)
    )
    own_1, own_2, own_12, own_3, own_34a, own_34b = admit(
        density.reshape(blocks, width, width), received, first, order, target, source, spans
    )

    axes = ("gx", "gy")
    devices = [(x, y) for x in range(wide_count) for y in range(narrow_count)]

    def send(array, target):
        pairs = []
        for x, y in devices:
            to_x, to_y = target(x, y)
            pairs.append((x * narrow_count + y, to_x % wide_count * narrow_count + to_y))
        return lax.ppermute(array, axes, pairs)

    def across(x, y):
        return x, narrow_count - 1 - y

    def chip(x, y):
        return x, y ^ 1

    def ring(x, y):
        return x ^ 1, narrow_count - 1 - y

    def onward(x, y):
        return (x + 2 if x % 2 == 0 else x - 2), y

    ring_across_1 = send(own_1, ring)
    own_across_a = send(own_34a, across)
    own_across_b = send(own_34b, across)
    ring_across_2 = send(own_2, ring)
    ring_across_3 = send(own_3, ring)
    far_across_1 = send(ring_across_1, onward)
    ring_same_1 = send(ring_across_1, across)
    far_across_2 = send(ring_across_2, onward)
    ring_same_2 = send(ring_across_2, across)
    ring_same_a = send(own_across_a, ring)
    ring_same_b = send(own_across_b, ring)
    far_across_3 = send(ring_across_3, onward)
    ring_across_4 = send(own_34b, ring)
    own_across_12 = send(own_12, across)
    own_chip_12 = send(own_12, chip)
    own_chip_a = send(own_34a, chip)
    own_chip_b = send(own_34b, chip)
    far_same_1 = send(ring_same_1, onward)
    ring_chip_1 = send(ring_same_1, chip)
    far_same_2 = send(ring_same_2, onward)
    ring_chip_2 = send(ring_same_2, chip)
    far_same_a = send(ring_same_a, onward)
    ring_chip_a = send(ring_same_a, chip)
    far_same_b = send(ring_same_b[:near_blocks - tail], onward)
    ring_chip_b = send(ring_same_b, chip)
    far_chip_1 = send(far_same_1, chip)
    far_chip_2 = send(far_same_2, chip)
    far_chip_a = send(far_same_a, chip)
    far_chip_b = send(far_same_b, chip)

    near_pieces = [
        (own_12, 0, 0), (own_34a, 0, 2 * cut), (own_34b, 0, tail),
        (own_chip_12, 1, 0), (own_chip_a, 1, 2 * cut), (own_chip_b, 1, tail),
        (own_across_12, 2, 0), (own_across_a, 2, 2 * cut), (own_across_b, 2, tail),
        (ring_same_1, 3, 0), (ring_same_2, 3, cut), (ring_same_a, 3, 2 * cut), (ring_same_b, 3, tail),
        (ring_chip_1, 4, 0), (ring_chip_2, 4, cut), (ring_chip_a, 4, 2 * cut), (ring_chip_b, 4, tail),
        (ring_across_1, 5, 0), (ring_across_2, 5, cut), (ring_across_3, 5, 2 * cut),
        (ring_across_4, 5, tail),
    ]
    far_pieces = [
        (far_same_1, 6, 0), (far_same_2, 6, cut), (far_same_a, 6, 2 * cut), (far_same_b, 6, tail),
        (far_chip_1, 7, 0), (far_chip_2, 7, cut), (far_chip_a, 7, 2 * cut), (far_chip_b, 7, tail),
        (far_across_1, 8, 0), (far_across_2, 8, cut), (far_across_3, 8, 2 * cut),
    ]
    carried = square_near(
        positions, [piece for piece, _, _ in near_pieces],
        [starts[part] + offset for _, part, offset in near_pieces],
        far_start, zero_at, row_count, width,
    )
    purified = purify_far(
        positions, out_slots, [piece for piece, _, _ in far_pieces],
        [starts[part] + offset - far_start for _, part, offset in far_pieces],
        carried, far_start, zero_at - far_start, row_count, slot_count, width,
    )
    return purified.reshape(density.shape)


def solution(mesh):
    in_specs = (P("gx", "gy", None, None, None, None), P(), P(("gx", "gy"), None, None), P(), P())
    out_specs = P("gx", "gy", None, None, None, None)
    return jax.shard_map(
        per_device, mesh=mesh, in_specs=in_specs, out_specs=out_specs, check_vma=False
    )
```

```python
import functools

import jax
import jax.numpy as jnp
from jax import lax
from jax.experimental import pallas as pl
from jax.experimental.pallas import tpu as pltpu
from jax.sharding import PartitionSpec as P

C = 2


def pack_kernel(base_ref, owner_ref, ent_ref, out_ref, staged, seen, load_sems, store_sem):
    count = ent_ref.shape[0]
    parts = load_sems.shape[0]
    size = count // parts
    loads = []
    for p in range(parts):
        rows = pl.ds(p * size, size)
        loads.append(pltpu.make_async_copy(ent_ref.at[rows], staged.at[rows], load_sems.at[p]))
        loads[-1].start()

    def clear(i, carry):
        seen[i] = 0
        return carry

    def issue(i, carry):
        owner = owner_ref[base_ref[0] + i]
        rank = seen[owner]
        seen[owner] = rank + 1
        slot = owner * C + rank
        pltpu.make_async_copy(staged.at[i], out_ref.at[slot], store_sem).start()
        return carry

    lax.fori_loop(0, seen.shape[0], clear, 0, unroll=8)
    for p in range(parts):
        loads[p].wait()
        lax.fori_loop(p * size, (p + 1) * size, issue, 0)
    pltpu.make_async_copy(staged, out_ref.at[pl.ds(0, count)], store_sem).wait()


def pack(ent_blocks, ent_owner, base, device_count):
    return pl.pallas_call(
        pack_kernel,
        out_shape=jax.ShapeDtypeStruct(
            (device_count * C,) + ent_blocks.shape[1:], ent_blocks.dtype
        ),
        in_specs=[
            pl.BlockSpec(memory_space=pltpu.SMEM),
            pl.BlockSpec(memory_space=pltpu.SMEM),
            pl.BlockSpec(memory_space=pl.ANY),
        ],
        out_specs=pl.BlockSpec(memory_space=pl.ANY),
        scratch_shapes=[
            pltpu.VMEM(ent_blocks.shape, ent_blocks.dtype),
            pltpu.SMEM((device_count,), jnp.int32),
            pltpu.SemaphoreType.DMA((4,)),
            pltpu.SemaphoreType.DMA,
        ],
        name="pack",
    )(base, ent_owner, ent_blocks)


def admit_kernel(spans, first_ref, order_ref, source_ref, density_ref, received_ref, *refs):
    part_refs, own, sems = refs[: len(spans)], refs[len(spans)], refs[len(spans) + 1]

    def add(j, total):
        return total + received_ref[order_ref[j]].astype(jnp.float32)

    def place(p, carry):
        t = source_ref[p]
        total = lax.fori_loop(
            first_ref[t], first_ref[t + 1], add, density_ref[t].astype(jnp.float32)
        )
        own[p] = total.astype(own.dtype)
        return carry

    copies = []
    done = spans[0][0]
    for i, (low, high) in enumerate(spans):
        if high > done:
            lax.fori_loop(done, high, place, 0)
            done = high
        copies.append(pltpu.make_async_copy(own.at[pl.ds(low, high - low)], part_refs[i], sems.at[i]))
        copies[-1].start()
    for copy in copies:
        copy.wait()


def admit(density, received, first, order, source, spans):
    return pl.pallas_call(
        functools.partial(admit_kernel, spans),
        out_shape=[
            jax.ShapeDtypeStruct((high - low,) + density.shape[1:], density.dtype)
            for low, high in spans
        ],
        in_specs=[pl.BlockSpec(memory_space=pltpu.SMEM)] * 3
        + [pl.BlockSpec(memory_space=pltpu.VMEM)] * 2,
        out_specs=[pl.BlockSpec(memory_space=pl.ANY)] * len(spans),
        scratch_shapes=[
            pltpu.VMEM(density.shape, density.dtype),
            pltpu.SemaphoreType.DMA((len(spans),)),
        ],
        name="admit",
    )(first, order, source, density, received)


def reach(part):
    wide, narrow = divmod(part, 3)
    wides = (0, 1, 2) if wide == 0 else (0, wide)
    narrows = (0, 1, 2) if narrow == 0 else (0, narrow)
    return [w * 3 + n for w in wides for n in narrows]


NEAR_PARTS = 6


def near_count(part):
    return len([q for q in reach(part) if q < NEAR_PARTS])


def far_count(part):
    return len(reach(part)) - near_count(part)


def load_pieces(pieces, piece_starts, table, sems):
    copies = []
    for i, (piece, start) in enumerate(zip(pieces, piece_starts)):
        copies.append(
            pltpu.make_async_copy(piece, table.at[pl.ds(start, piece.shape[0])], sems.at[i])
        )
        copies[-1].start()
    return copies


def lanes_of(ref, parts, group):
    return jnp.concatenate([ref[:, q * group:(q + 1) * group] for q in parts], axis=1)


def near_kernel(row_count, width, piece_starts, table_size, pos_ref, *refs):
    pieces = refs[: len(piece_starts)]
    outs = refs[len(piece_starts):]
    grids, (square, left_far, table, left, sems) = outs[:9], outs[9:]
    near = 9 * row_count
    group = row_count * width
    copies = load_pieces(pieces, piece_starts, table, sems)
    table[table_size] = jnp.zeros((width, width), table.dtype)
    for copy in copies:
        copy.wait()

    def block(m, k):
        return table[jnp.minimum(pos_ref[m * near + k], table_size)]

    for r in range(row_count):
        for k in range(near):
            left[r * width:(r + 1) * width, k * width:(k + 1) * width] = block(r, k)
    left_far[...] = left[:, NEAR_PARTS * group:]
    for part in range(9):
        parts = [q for q in reach(part) if q < NEAR_PARTS]
        for i, q in enumerate(parts):
            for r in range(row_count):
                for k in range(row_count):
                    low = (i * row_count + r) * width
                    grids[part][low:low + width, k * width:(k + 1) * width] = block(
                        q * row_count + r, part * row_count + k
                    )
        square[part] = jnp.dot(
            lanes_of(left, parts, group), grids[part][...], preferred_element_type=jnp.float32
        )


def square_near(positions, pieces, piece_starts, table_size, row_count, width):
    group = row_count * width
    span = 9 * group
    return pl.pallas_call(
        functools.partial(near_kernel, row_count, width, piece_starts, table_size),
        out_shape=[
            pltpu.VMEM((near_count(part) * group, group), jnp.bfloat16) for part in range(9)
        ] + [
            pltpu.VMEM((9, group, group), jnp.float32),
            pltpu.VMEM((group, (9 - NEAR_PARTS) * group), jnp.bfloat16),
        ],
        in_specs=[pl.BlockSpec(memory_space=pltpu.SMEM)]
        + [pl.BlockSpec(memory_space=pl.ANY)] * len(pieces),
        out_specs=[pl.BlockSpec(memory_space=pltpu.VMEM)] * 11,
        scratch_shapes=[
            pltpu.VMEM((table_size + 1, width, width), jnp.bfloat16),
            pltpu.VMEM((group, span), jnp.bfloat16),
            pltpu.SemaphoreType.DMA((len(pieces),)),
        ],
        compiler_params=pltpu.CompilerParams(vmem_limit_bytes=20 << 20),
        name="square_near",
    )(positions, *pieces)


def far_kernel(row_count, width, piece_starts, table_start, table_size, pos_ref, slot_ref, *refs):
    pieces = refs[: len(piece_starts)]
    outs = refs[len(piece_starts):]
    near_grids = outs[:9]
    square_in, left, out_ref, table, grid, square, square_b, staged, sems, out_sem = outs[9:]
    near = 9 * row_count
    group = row_count * width
    zero_at = table_start + table_size
    copies = load_pieces(pieces, piece_starts, table, sems)
    table[table_size] = jnp.zeros((width, width), table.dtype)
    for copy in copies:
        copy.wait()

    for part in range(9):
        parts = reach(part)
        base = near_count(part)
        far_base = sum(far_count(q) for q in range(part)) * group
        for i, q in enumerate(parts[base:]):
            for r in range(row_count):
                for k in range(row_count):
                    low = far_base + (i * row_count + r) * width
                    grid[low:low + width, k * width:(k + 1) * width] = table[
                        pos_ref[(q * row_count + r) * near + part * row_count + k] - table_start
                    ]
        product = square_in[part]
        if base < len(parts):
            product = product + jnp.dot(
                lanes_of(left, [q - NEAR_PARTS for q in parts[base:]], group),
                grid[far_base:far_base + far_count(part) * group],
                preferred_element_type=jnp.float32,
            )
        square[part] = product
        for r in range(row_count):
            for k in range(row_count):
                listed = pos_ref[r * near + part * row_count + k] != zero_at
                low = part * group + k * width
                square_b[r * width:(r + 1) * width, low:low + width] = jnp.where(
                    listed, product[r * width:(r + 1) * width, k * width:(k + 1) * width], 0.0
                ).astype(jnp.bfloat16)

    blocks = out_ref.shape[0]
    for part in range(9):
        parts = reach(part)
        base = near_count(part)
        far_base = sum(far_count(q) for q in range(part)) * group
        product = jnp.dot(
            lanes_of(square_b, parts[:base], group), near_grids[part][...],
            preferred_element_type=jnp.float32,
        )
        if base < len(parts):
            product = product + jnp.dot(
                lanes_of(square_b, parts[base:], group),
                grid[far_base:far_base + far_count(part) * group],
                preferred_element_type=jnp.float32,
            )
        result = 3.0 * square[part] - 2.0 * product
        for r in range(row_count):
            for k in range(row_count):
                slot = slot_ref[r * near + part * row_count + k]
                staged[slot] = result[r * width:(r + 1) * width, k * width:(k + 1) * width]

                @pl.when(slot < blocks)
                def _():
                    pltpu.make_async_copy(staged.at[slot], out_ref.at[slot], out_sem).start()

    pltpu.make_async_copy(staged.at[pl.ds(0, blocks)], out_ref, out_sem).wait()


def purify_far(
    positions, out_slots, pieces, piece_starts, carried, table_start, table_size,
    row_count, slot_count, width,
):
    group = row_count * width
    span = 9 * group
    blocks = row_count * slot_count
    return pl.pallas_call(
        functools.partial(
            far_kernel, row_count, width, piece_starts, table_start, table_size
        ),
        out_shape=jax.ShapeDtypeStruct((blocks, width, width), jnp.float32),
        in_specs=[pl.BlockSpec(memory_space=pltpu.SMEM)] * 2
        + [pl.BlockSpec(memory_space=pl.ANY)] * len(pieces)
        + [pl.BlockSpec(memory_space=pltpu.VMEM)] * len(carried),
        out_specs=pl.BlockSpec(memory_space=pl.ANY),
        scratch_shapes=[
            pltpu.VMEM((table_size + 1, width, width), jnp.bfloat16),
            pltpu.VMEM((sum(far_count(part) for part in range(9)) * group, group), jnp.bfloat16),
            pltpu.VMEM((9, group, group), jnp.float32),
            pltpu.VMEM((group, span), jnp.bfloat16),
            pltpu.VMEM((blocks + 1, width, width), jnp.float32),
            pltpu.SemaphoreType.DMA((len(pieces),)),
            pltpu.SemaphoreType.DMA,
        ],
        compiler_params=pltpu.CompilerParams(vmem_limit_bytes=28 << 20),
        name="purify_far",
    )(
        positions, out_slots, *pieces,
        *[pltpu.with_memory_space_constraint(array, pltpu.VMEM) for array in carried],
    )


def block_positions(neighbours, here_x, here_y, starts, zero_at):
    wide_count, narrow_count, row_count, slot_count = neighbours.shape
    total_rows = wide_count * narrow_count * row_count
    listing = neighbours.reshape(total_rows, slot_count)
    ids = jnp.arange(9 * row_count, dtype=jnp.int32)
    wide, narrow, inner = ids // (3 * row_count), ids // row_count % 3, ids % row_count
    beyond = jnp.where(here_x % 2 == 0, here_x + wide_count - 1, here_x + 1) % wide_count
    near_x = jnp.where(wide == 0, here_x, jnp.where(wide == 1, here_x ^ 1, beyond))
    near_y = jnp.where(
        narrow == 0, here_y, jnp.where(narrow == 1, here_y ^ 1, narrow_count - 1 - here_y)
    )
    rows = (near_x * narrow_count + near_y) * row_count + inner
    lists = jnp.take(listing, rows, axis=0)
    list_x = lists // (narrow_count * row_count)
    list_y = lists // row_count % narrow_count
    aside = list_y == (near_y ^ 1)[:, None]
    kind = jnp.where(
        list_x == (near_x ^ 1)[:, None], jnp.where(aside, 2, 3), jnp.where(aside, 1, 0)
    )
    slot_ids = jnp.arange(slot_count, dtype=jnp.int32)
    key = kind * slot_count + slot_ids
    place = jnp.sum((key[:, :, None] > key[:, None, :]).astype(jnp.int32), axis=2)
    part = wide * 3 + narrow
    start = jnp.zeros_like(part)
    for i, value in enumerate(starts):
        start = jnp.where(part == i, value, start)
    held_at = (start + inner)[:, None] + place * row_count
    matches = lists[:, None, :] == rows[None, :, None]
    positions = jnp.min(jnp.where(matches, held_at[:, None, :], zero_at), axis=2)
    own_matches = matches[:row_count]
    own_slots = slot_ids + slot_count * jnp.arange(row_count, dtype=jnp.int32)[:, None, None]
    out_slots = jnp.min(jnp.where(own_matches, own_slots, row_count * slot_count), axis=2)
    order = (place[:row_count] * row_count + inner[:row_count, None]).reshape(-1)
    flat_ids = jnp.arange(row_count * slot_count, dtype=jnp.int32)
    source = jnp.sum(jnp.where(order[None, :] == flat_ids[:, None], flat_ids[None, :], 0), axis=1)
    return (
        positions.astype(jnp.int32).reshape(-1),
        out_slots.astype(jnp.int32).reshape(-1),
        source.astype(jnp.int32),
    )


def per_device(density, neighbours, ent_blocks, ent_owner, ent_place):
    wide_count = lax.axis_size("gx")
    narrow_count = lax.axis_size("gy")
    device_count = wide_count * narrow_count
    here_x = lax.axis_index("gx")
    here_y = lax.axis_index("gy")
    self_index = here_x * narrow_count + here_y
    row_count = density.shape[2]
    slot_count = density.shape[3]
    width = density.shape[4]
    blocks = row_count * slot_count
    held = ent_blocks.shape[0]
    owners = ent_owner.reshape(device_count, held)
    places = ent_place.reshape(device_count, held)

    base = (self_index * held).astype(jnp.int32).reshape(1)
    outgoing = pack(ent_blocks, ent_owner, base, device_count)
    received = lax.all_to_all(
        outgoing.reshape(device_count, C, width, width),
        ("gx", "gy"), split_axis=0, concat_axis=0, tiled=True,
    ).reshape(device_count * C, width, width)

    for_me = (owners == self_index).astype(jnp.int32)
    rank = jnp.cumsum(for_me, axis=1) - for_me
    picked = (for_me[:, :, None] == 1) & (
        rank[:, :, None] == jnp.arange(C, dtype=jnp.int32)[None, None, :]
    )
    slot_place = jnp.sum(jnp.where(picked, places[:, :, None], 0), axis=1).reshape(-1)
    slot_used = jnp.any(picked, axis=1).reshape(-1)
    slot_place = jnp.where(slot_used, slot_place, blocks)
    slot_ids = jnp.arange(device_count * C, dtype=jnp.int32)
    ahead = (slot_place[:, None] > slot_place[None, :]) | (
        (slot_place[:, None] == slot_place[None, :]) & (slot_ids[:, None] > slot_ids[None, :])
    )
    sorted_at = jnp.sum(ahead, axis=1)
    order = jnp.sum(
        jnp.where(sorted_at[None, :] == slot_ids[:, None], slot_ids[None, :], 0), axis=1
    ).astype(jnp.int32)
    target_ids = jnp.arange(blocks + 1, dtype=jnp.int32)
    first = jnp.sum(slot_place[None, :] < target_ids[:, None], axis=1).astype(jnp.int32)

    near_blocks = row_count * min(slot_count, 6 * row_count)
    corner_blocks = row_count * min(slot_count, 4 * row_count)
    sizes = [blocks] * 6 + [near_blocks, near_blocks, corner_blocks]
    starts = [sum(sizes[:i]) for i in range(9)]
    zero_at = sum(sizes)
    positions, out_slots, source = block_positions(neighbours, here_x, here_y, starts, zero_at)

    cut = corner_blocks // 2
    tail = blocks - 6 * row_count
    received, first, order, source, positions, out_slots = lax.optimization_barrier(
        (received, first, order, source, positions, out_slots)
    )
    flat_density = density.reshape(blocks, width, width)
    (own_1,) = admit(flat_density, received, first, order, source, ((0, cut),))
    own_2, own_3, own_t = admit(
        flat_density, received, first, order, source,
        ((cut, 2 * cut), (2 * cut, blocks), (tail, blocks)),
    )

    axes = ("gx", "gy")
    devices = [(x, y) for x in range(wide_count) for y in range(narrow_count)]

    def send(array, target):
        pairs = []
        for x, y in devices:
            to_x, to_y = target(x, y)
            pairs.append((x * narrow_count + y, to_x % wide_count * narrow_count + to_y))
        return lax.ppermute(array, axes, pairs)

    def across(x, y):
        return x, narrow_count - 1 - y

    def chip(x, y):
        return x, y ^ 1

    def ring(x, y):
        return x ^ 1, narrow_count - 1 - y

    def onward(x, y):
        return (x + 2 if x % 2 == 0 else x - 2), y

    ring_across_1 = send(own_1, ring)
    own_across_1 = send(own_1, across)
    ring_across_2 = send(own_2, ring)
    own_across_3 = send(own_3, across)
    far_across_1 = send(ring_across_1, onward)
    ring_same_1 = send(ring_across_1, across)
    own_chip_1 = send(own_1, chip)
    far_across_2 = send(ring_across_2, onward)
    ring_same_2 = send(ring_across_2, across)
    ring_same_3 = send(own_across_3, ring)
    ring_across_t = send(own_t, ring)
    own_across_2 = send(own_2, across)
    own_chip_2 = send(own_2, chip)
    own_chip_3 = send(own_3, chip)
    far_same_1 = send(ring_same_1, onward)
    ring_chip_1 = send(ring_same_1, chip)
    far_same_3 = send(ring_same_3[:near_blocks - 2 * cut], onward)
    ring_chip_3 = send(ring_same_3, chip)
    far_same_2 = send(ring_same_2, onward)
    ring_chip_2 = send(ring_same_2, chip)
    far_chip_1 = send(far_same_1, chip)
    far_chip_3 = send(far_same_3, chip)
    far_chip_2 = send(far_same_2, chip)

    near_pieces = [
        (own_1, 0, 0), (own_2, 0, cut), (own_3, 0, 2 * cut),
        (own_chip_1, 1, 0), (own_chip_2, 1, cut), (own_chip_3, 1, 2 * cut),
        (own_across_1, 2, 0), (own_across_2, 2, cut), (own_across_3, 2, 2 * cut),
        (ring_same_1, 3, 0), (ring_same_2, 3, cut), (ring_same_3, 3, 2 * cut),
        (ring_chip_1, 4, 0), (ring_chip_2, 4, cut), (ring_chip_3, 4, 2 * cut),
        (ring_across_1, 5, 0), (ring_across_2, 5, cut), (ring_across_t, 5, tail),
    ]
    far_pieces = [
        (far_same_1, 6, 0), (far_same_2, 6, cut), (far_same_3, 6, 2 * cut),
        (far_chip_1, 7, 0), (far_chip_2, 7, cut), (far_chip_3, 7, 2 * cut),
        (far_across_1, 8, 0), (far_across_2, 8, cut),
    ]
    far_start = starts[NEAR_PARTS]
    carried = square_near(
        positions, [piece for piece, _, _ in near_pieces],
        [starts[part] + offset for _, part, offset in near_pieces],
        far_start, row_count, width,
    )
    purified = purify_far(
        positions, out_slots, [piece for piece, _, _ in far_pieces],
        [starts[part] + offset - far_start for _, part, offset in far_pieces],
        carried, far_start, zero_at - far_start, row_count, slot_count, width,
    )
    return purified.reshape(density.shape)


def solution(mesh):
    in_specs = (P("gx", "gy", None, None, None, None), P(), P(("gx", "gy"), None, None), P(), P())
    out_specs = P("gx", "gy", None, None, None, None)
    return jax.shard_map(
        per_device, mesh=mesh, in_specs=in_specs, out_specs=out_specs, check_vma=False
    )
```

```python
import functools

import jax
import jax.numpy as jnp
from jax import lax
from jax.experimental import pallas as pl
from jax.experimental.pallas import tpu as pltpu
from jax.sharding import PartitionSpec as P

C = 2


def pack_kernel(base_ref, owner_ref, ent_ref, out_ref, staged, seen, load_sems, store_sem):
    count = ent_ref.shape[0]
    parts = load_sems.shape[0]
    size = count // parts
    loads = []
    for p in range(parts):
        rows = pl.ds(p * size, size)
        loads.append(pltpu.make_async_copy(ent_ref.at[rows], staged.at[rows], load_sems.at[p]))
        loads[-1].start()

    def clear(i, carry):
        seen[i] = 0
        return carry

    def issue(i, carry):
        owner = owner_ref[base_ref[0] + i]
        rank = seen[owner]
        seen[owner] = rank + 1
        slot = owner * C + rank
        pltpu.make_async_copy(staged.at[i], out_ref.at[slot], store_sem).start()
        return carry

    lax.fori_loop(0, seen.shape[0], clear, 0, unroll=8)
    for p in range(parts):
        loads[p].wait()
        lax.fori_loop(p * size, (p + 1) * size, issue, 0)
    pltpu.make_async_copy(staged, out_ref.at[pl.ds(0, count)], store_sem).wait()


def pack(ent_blocks, ent_owner, base, device_count):
    return pl.pallas_call(
        pack_kernel,
        out_shape=jax.ShapeDtypeStruct(
            (device_count * C,) + ent_blocks.shape[1:], ent_blocks.dtype
        ),
        in_specs=[
            pl.BlockSpec(memory_space=pltpu.SMEM),
            pl.BlockSpec(memory_space=pltpu.SMEM),
            pl.BlockSpec(memory_space=pl.ANY),
        ],
        out_specs=pl.BlockSpec(memory_space=pl.ANY),
        scratch_shapes=[
            pltpu.VMEM(ent_blocks.shape, ent_blocks.dtype),
            pltpu.SMEM((device_count,), jnp.int32),
            pltpu.SemaphoreType.DMA((4,)),
            pltpu.SemaphoreType.DMA,
        ],
        name="pack",
    )(base, ent_owner, ent_blocks)


def admit_kernel(spans, first_ref, order_ref, source_ref, density_ref, received_ref, *refs):
    part_refs, own, sems = refs[: len(spans)], refs[len(spans)], refs[len(spans) + 1]

    def add(j, total):
        return total + received_ref[order_ref[j]].astype(jnp.float32)

    def place(p, carry):
        t = source_ref[p]
        total = lax.fori_loop(
            first_ref[t], first_ref[t + 1], add, density_ref[t].astype(jnp.float32)
        )
        own[p] = total.astype(own.dtype)
        return carry

    copies = []
    done = 0
    for i, (low, high) in enumerate(spans):
        if high > done:
            lax.fori_loop(max(low, done), high, place, 0)
            done = high
        copies.append(pltpu.make_async_copy(own.at[pl.ds(low, high - low)], part_refs[i], sems.at[i]))
        copies[-1].start()
    for copy in copies:
        copy.wait()


def admit(density, received, first, order, source, spans):
    return pl.pallas_call(
        functools.partial(admit_kernel, spans),
        out_shape=[
            jax.ShapeDtypeStruct((high - low,) + density.shape[1:], density.dtype)
            for low, high in spans
        ],
        in_specs=[pl.BlockSpec(memory_space=pltpu.SMEM)] * 3
        + [pl.BlockSpec(memory_space=pltpu.VMEM)] * 2,
        out_specs=[pl.BlockSpec(memory_space=pl.ANY)] * len(spans),
        scratch_shapes=[
            pltpu.VMEM(density.shape, density.dtype),
            pltpu.SemaphoreType.DMA((len(spans),)),
        ],
        name="admit",
    )(first, order, source, density, received)


def reach(part):
    wide, narrow = divmod(part, 3)
    wides = (0, 1, 2) if wide == 0 else (0, wide)
    narrows = (0, 1, 2) if narrow == 0 else (0, narrow)
    return [w * 3 + n for w in wides for n in narrows]


NEAR_PARTS = 6


def near_count(part):
    return len([q for q in reach(part) if q < NEAR_PARTS])


def far_count(part):
    return len(reach(part)) - near_count(part)


def load_pieces(pieces, piece_starts, table, sems):
    copies = []
    for i, (piece, start) in enumerate(zip(pieces, piece_starts)):
        copies.append(
            pltpu.make_async_copy(piece, table.at[pl.ds(start, piece.shape[0])], sems.at[i])
        )
        copies[-1].start()
    return copies


def lanes_of(ref, parts, group):
    return jnp.concatenate([ref[:, q * group:(q + 1) * group] for q in parts], axis=1)


def near_kernel(row_count, width, piece_starts, table_size, pos_ref, *refs):
    pieces = refs[: len(piece_starts)]
    outs = refs[len(piece_starts):]
    grids, (square, left_far, table, left, sems) = outs[:9], outs[9:]
    near = 9 * row_count
    group = row_count * width
    copies = load_pieces(pieces, piece_starts, table, sems)
    table[table_size] = jnp.zeros((width, width), table.dtype)
    for copy in copies:
        copy.wait()

    def block(m, k):
        return table[jnp.minimum(pos_ref[m * near + k], table_size)]

    for r in range(row_count):
        for k in range(near):
            left[r * width:(r + 1) * width, k * width:(k + 1) * width] = block(r, k)
    left_far[...] = left[:, NEAR_PARTS * group:]
    for part in range(9):
        parts = [q for q in reach(part) if q < NEAR_PARTS]
        for i, q in enumerate(parts):
            for r in range(row_count):
                for k in range(row_count):
                    low = (i * row_count + r) * width
                    grids[part][low:low + width, k * width:(k + 1) * width] = block(
                        q * row_count + r, part * row_count + k
                    )
        square[part] = jnp.dot(
            lanes_of(left, parts, group), grids[part][...], preferred_element_type=jnp.float32
        )


def square_near(positions, pieces, piece_starts, table_size, row_count, width):
    group = row_count * width
    span = 9 * group
    return pl.pallas_call(
        functools.partial(near_kernel, row_count, width, piece_starts, table_size),
        out_shape=[
            pltpu.VMEM((near_count(part) * group, group), jnp.bfloat16) for part in range(9)
        ] + [
            pltpu.VMEM((9, group, group), jnp.float32),
            pltpu.VMEM((group, (9 - NEAR_PARTS) * group), jnp.bfloat16),
        ],
        in_specs=[pl.BlockSpec(memory_space=pltpu.SMEM)]
        + [pl.BlockSpec(memory_space=pl.ANY)] * len(pieces),
        out_specs=[pl.BlockSpec(memory_space=pltpu.VMEM)] * 11,
        scratch_shapes=[
            pltpu.VMEM((table_size + 1, width, width), jnp.bfloat16),
            pltpu.VMEM((group, span), jnp.bfloat16),
            pltpu.SemaphoreType.DMA((len(pieces),)),
        ],
        compiler_params=pltpu.CompilerParams(vmem_limit_bytes=20 << 20),
        name="square_near",
    )(positions, *pieces)


def far_kernel(row_count, width, piece_starts, table_start, table_size, pos_ref, slot_ref, *refs):
    pieces = refs[: len(piece_starts)]
    outs = refs[len(piece_starts):]
    near_grids = outs[:9]
    square_in, left, out_ref, table, grid, square, square_b, staged, sems, out_sem = outs[9:]
    near = 9 * row_count
    group = row_count * width
    zero_at = table_start + table_size
    copies = load_pieces(pieces, piece_starts, table, sems)
    table[table_size] = jnp.zeros((width, width), table.dtype)
    for copy in copies:
        copy.wait()

    for part in range(9):
        parts = reach(part)
        base = near_count(part)
        far_base = sum(far_count(q) for q in range(part)) * group
        for i, q in enumerate(parts[base:]):
            for r in range(row_count):
                for k in range(row_count):
                    low = far_base + (i * row_count + r) * width
                    grid[low:low + width, k * width:(k + 1) * width] = table[
                        pos_ref[(q * row_count + r) * near + part * row_count + k] - table_start
                    ]
        product = square_in[part]
        if base < len(parts):
            product = product + jnp.dot(
                lanes_of(left, [q - NEAR_PARTS for q in parts[base:]], group),
                grid[far_base:far_base + far_count(part) * group],
                preferred_element_type=jnp.float32,
            )
        square[part] = product
        for r in range(row_count):
            for k in range(row_count):
                listed = pos_ref[r * near + part * row_count + k] != zero_at
                low = part * group + k * width
                square_b[r * width:(r + 1) * width, low:low + width] = jnp.where(
                    listed, product[r * width:(r + 1) * width, k * width:(k + 1) * width], 0.0
                ).astype(jnp.bfloat16)

    blocks = out_ref.shape[0]
    for part in range(9):
        parts = reach(part)
        base = near_count(part)
        far_base = sum(far_count(q) for q in range(part)) * group
        product = jnp.dot(
            lanes_of(square_b, parts[:base], group), near_grids[part][...],
            preferred_element_type=jnp.float32,
        )
        if base < len(parts):
            product = product + jnp.dot(
                lanes_of(square_b, parts[base:], group),
                grid[far_base:far_base + far_count(part) * group],
                preferred_element_type=jnp.float32,
            )
        result = 3.0 * square[part] - 2.0 * product
        for r in range(row_count):
            for k in range(row_count):
                slot = slot_ref[r * near + part * row_count + k]
                staged[slot] = result[r * width:(r + 1) * width, k * width:(k + 1) * width]

                @pl.when(slot < blocks)
                def _():
                    pltpu.make_async_copy(staged.at[slot], out_ref.at[slot], out_sem).start()

    pltpu.make_async_copy(staged.at[pl.ds(0, blocks)], out_ref, out_sem).wait()


def purify_far(
    positions, out_slots, pieces, piece_starts, carried, table_start, table_size,
    row_count, slot_count, width,
):
    group = row_count * width
    span = 9 * group
    blocks = row_count * slot_count
    return pl.pallas_call(
        functools.partial(
            far_kernel, row_count, width, piece_starts, table_start, table_size
        ),
        out_shape=jax.ShapeDtypeStruct((blocks, width, width), jnp.float32),
        in_specs=[pl.BlockSpec(memory_space=pltpu.SMEM)] * 2
        + [pl.BlockSpec(memory_space=pl.ANY)] * len(pieces)
        + [pl.BlockSpec(memory_space=pltpu.VMEM)] * len(carried),
        out_specs=pl.BlockSpec(memory_space=pl.ANY),
        scratch_shapes=[
            pltpu.VMEM((table_size + 1, width, width), jnp.bfloat16),
            pltpu.VMEM((sum(far_count(part) for part in range(9)) * group, group), jnp.bfloat16),
            pltpu.VMEM((9, group, group), jnp.float32),
            pltpu.VMEM((group, span), jnp.bfloat16),
            pltpu.VMEM((blocks + 1, width, width), jnp.float32),
            pltpu.SemaphoreType.DMA((len(pieces),)),
            pltpu.SemaphoreType.DMA,
        ],
        compiler_params=pltpu.CompilerParams(vmem_limit_bytes=28 << 20),
        name="purify_far",
    )(
        positions, out_slots, *pieces,
        *[pltpu.with_memory_space_constraint(array, pltpu.VMEM) for array in carried],
    )


def block_positions(neighbours, here_x, here_y, starts, zero_at):
    wide_count, narrow_count, row_count, slot_count = neighbours.shape
    total_rows = wide_count * narrow_count * row_count
    listing = neighbours.reshape(total_rows, slot_count)
    ids = jnp.arange(9 * row_count, dtype=jnp.int32)
    wide, narrow, inner = ids // (3 * row_count), ids // row_count % 3, ids % row_count
    beyond = jnp.where(here_x % 2 == 0, here_x + wide_count - 1, here_x + 1) % wide_count
    near_x = jnp.where(wide == 0, here_x, jnp.where(wide == 1, here_x ^ 1, beyond))
    near_y = jnp.where(
        narrow == 0, here_y, jnp.where(narrow == 1, here_y ^ 1, narrow_count - 1 - here_y)
    )
    rows = (near_x * narrow_count + near_y) * row_count + inner
    lists = jnp.take(listing, rows, axis=0)
    list_x = lists // (narrow_count * row_count)
    list_y = lists // row_count % narrow_count
    aside = list_y == (near_y ^ 1)[:, None]
    kind = jnp.where(
        list_x == (near_x ^ 1)[:, None], jnp.where(aside, 2, 3), jnp.where(aside, 1, 0)
    )
    slot_ids = jnp.arange(slot_count, dtype=jnp.int32)
    key = kind * slot_count + slot_ids
    place = jnp.sum((key[:, :, None] > key[:, None, :]).astype(jnp.int32), axis=2)
    part = wide * 3 + narrow
    start = jnp.zeros_like(part)
    for i, value in enumerate(starts):
        start = jnp.where(part == i, value, start)
    held_at = (start + inner)[:, None] + place * row_count
    matches = lists[:, None, :] == rows[None, :, None]
    positions = jnp.min(jnp.where(matches, held_at[:, None, :], zero_at), axis=2)
    own_matches = matches[:row_count]
    own_slots = slot_ids + slot_count * jnp.arange(row_count, dtype=jnp.int32)[:, None, None]
    out_slots = jnp.min(jnp.where(own_matches, own_slots, row_count * slot_count), axis=2)
    order = (place[:row_count] * row_count + inner[:row_count, None]).reshape(-1)
    flat_ids = jnp.arange(row_count * slot_count, dtype=jnp.int32)
    source = jnp.sum(jnp.where(order[None, :] == flat_ids[:, None], flat_ids[None, :], 0), axis=1)
    return (
        positions.astype(jnp.int32).reshape(-1),
        out_slots.astype(jnp.int32).reshape(-1),
        source.astype(jnp.int32),
    )


def per_device(density, neighbours, ent_blocks, ent_owner, ent_place):
    wide_count = lax.axis_size("gx")
    narrow_count = lax.axis_size("gy")
    device_count = wide_count * narrow_count
    here_x = lax.axis_index("gx")
    here_y = lax.axis_index("gy")
    self_index = here_x * narrow_count + here_y
    row_count = density.shape[2]
    slot_count = density.shape[3]
    width = density.shape[4]
    blocks = row_count * slot_count
    held = ent_blocks.shape[0]
    owners = ent_owner.reshape(device_count, held)
    places = ent_place.reshape(device_count, held)

    base = (self_index * held).astype(jnp.int32).reshape(1)
    outgoing = pack(ent_blocks, ent_owner, base, device_count)
    received = lax.all_to_all(
        outgoing.reshape(device_count, C, width, width),
        ("gx", "gy"), split_axis=0, concat_axis=0, tiled=True,
    ).reshape(device_count * C, width, width)

    for_me = (owners == self_index).astype(jnp.int32)
    rank = jnp.cumsum(for_me, axis=1) - for_me
    picked = (for_me[:, :, None] == 1) & (
        rank[:, :, None] == jnp.arange(C, dtype=jnp.int32)[None, None, :]
    )
    slot_place = jnp.sum(jnp.where(picked, places[:, :, None], 0), axis=1).reshape(-1)
    slot_used = jnp.any(picked, axis=1).reshape(-1)
    slot_place = jnp.where(slot_used, slot_place, blocks)
    slot_ids = jnp.arange(device_count * C, dtype=jnp.int32)
    ahead = (slot_place[:, None] > slot_place[None, :]) | (
        (slot_place[:, None] == slot_place[None, :]) & (slot_ids[:, None] > slot_ids[None, :])
    )
    sorted_at = jnp.sum(ahead, axis=1)
    order = jnp.sum(
        jnp.where(sorted_at[None, :] == slot_ids[:, None], slot_ids[None, :], 0), axis=1
    ).astype(jnp.int32)
    target_ids = jnp.arange(blocks + 1, dtype=jnp.int32)
    first = jnp.sum(slot_place[None, :] < target_ids[:, None], axis=1).astype(jnp.int32)

    near_blocks = row_count * min(slot_count, 6 * row_count)
    corner_blocks = row_count * min(slot_count, 4 * row_count)
    sizes = [blocks] * 6 + [near_blocks, near_blocks, corner_blocks]
    starts = [sum(sizes[:i]) for i in range(9)]
    zero_at = sum(sizes)
    positions, out_slots, source = block_positions(neighbours, here_x, here_y, starts, zero_at)

    cut = corner_blocks // 2
    tail = blocks - 6 * row_count
    received, first, order, source, positions, out_slots = lax.optimization_barrier(
        (received, first, order, source, positions, out_slots)
    )
    flat_density = density.reshape(blocks, width, width)
    own_1, own_3, own_t = admit(
        flat_density, received, first, order, source,
        ((0, cut), (2 * cut, blocks), (tail, blocks)),
    )
    (own_2,) = admit(flat_density, received, first, order, source, ((cut, 2 * cut),))

    axes = ("gx", "gy")
    devices = [(x, y) for x in range(wide_count) for y in range(narrow_count)]

    def send(array, target):
        pairs = []
        for x, y in devices:
            to_x, to_y = target(x, y)
            pairs.append((x * narrow_count + y, to_x % wide_count * narrow_count + to_y))
        return lax.ppermute(array, axes, pairs)

    def across(x, y):
        return x, narrow_count - 1 - y

    def chip(x, y):
        return x, y ^ 1

    def ring(x, y):
        return x ^ 1, narrow_count - 1 - y

    def onward(x, y):
        return (x + 2 if x % 2 == 0 else x - 2), y

    ring_across_1 = send(own_1, ring)
    own_across_1 = send(own_1, across)
    ring_across_2 = send(own_2, ring)
    own_across_3 = send(own_3, across)
    far_across_1 = send(ring_across_1, onward)
    ring_same_1 = send(ring_across_1, across)
    own_chip_1 = send(own_1, chip)
    far_across_2 = send(ring_across_2, onward)
    ring_same_2 = send(ring_across_2, across)
    ring_same_3 = send(own_across_3, ring)
    ring_across_t = send(own_t, ring)
    own_across_2 = send(own_2, across)
    own_chip_2 = send(own_2, chip)
    own_chip_3 = send(own_3, chip)
    far_same_1 = send(ring_same_1, onward)
    ring_chip_1 = send(ring_same_1, chip)
    far_same_3 = send(ring_same_3[:near_blocks - 2 * cut], onward)
    ring_chip_3 = send(ring_same_3, chip)
    far_same_2 = send(ring_same_2, onward)
    ring_chip_2 = send(ring_same_2, chip)
    far_chip_1 = send(far_same_1, chip)
    far_chip_3 = send(far_same_3, chip)
    far_chip_2 = send(far_same_2, chip)

    near_pieces = [
        (own_1, 0, 0), (own_2, 0, cut), (own_3, 0, 2 * cut),
        (own_chip_1, 1, 0), (own_chip_2, 1, cut), (own_chip_3, 1, 2 * cut),
        (own_across_1, 2, 0), (own_across_2, 2, cut), (own_across_3, 2, 2 * cut),
        (ring_same_1, 3, 0), (ring_same_2, 3, cut), (ring_same_3, 3, 2 * cut),
        (ring_chip_1, 4, 0), (ring_chip_2, 4, cut), (ring_chip_3, 4, 2 * cut),
        (ring_across_1, 5, 0), (ring_across_2, 5, cut), (ring_across_t, 5, tail),
    ]
    far_pieces = [
        (far_same_1, 6, 0), (far_same_2, 6, cut), (far_same_3, 6, 2 * cut),
        (far_chip_1, 7, 0), (far_chip_2, 7, cut), (far_chip_3, 7, 2 * cut),
        (far_across_1, 8, 0), (far_across_2, 8, cut),
    ]
    far_start = starts[NEAR_PARTS]
    carried = square_near(
        positions, [piece for piece, _, _ in near_pieces],
        [starts[part] + offset for _, part, offset in near_pieces],
        far_start, row_count, width,
    )
    purified = purify_far(
        positions, out_slots, [piece for piece, _, _ in far_pieces],
        [starts[part] + offset - far_start for _, part, offset in far_pieces],
        carried, far_start, zero_at - far_start, row_count, slot_count, width,
    )
    return purified.reshape(density.shape)


def solution(mesh):
    in_specs = (P("gx", "gy", None, None, None, None), P(), P(("gx", "gy"), None, None), P(), P())
    out_specs = P("gx", "gy", None, None, None, None)
    return jax.shard_map(
        per_device, mesh=mesh, in_specs=in_specs, out_specs=out_specs, check_vma=False
    )
```

```python
import functools

import jax
import jax.numpy as jnp
from jax import lax
from jax.experimental import pallas as pl
from jax.experimental.pallas import tpu as pltpu
from jax.sharding import PartitionSpec as P

C = 2


def pack_kernel(
    base_ref, owner_ref, ent_ref, out_ref, staged, seen, slots, load_sems, store_sem
):
    count = ent_ref.shape[0]
    parts = load_sems.shape[0]
    size = count // parts
    loads = []
    for p in range(parts):
        rows = pl.ds(p * size, size)
        loads.append(pltpu.make_async_copy(ent_ref.at[rows], staged.at[rows], load_sems.at[p]))
        loads[-1].start()

    def clear(i, carry):
        seen[i] = 0
        return carry

    def count_rank(i, carry):
        owner = owner_ref[base_ref[0] + i]
        rank = seen[owner]
        seen[owner] = rank + 1
        slots[i] = owner * C + rank
        return carry

    def issue(i, carry):
        pltpu.make_async_copy(staged.at[i], out_ref.at[slots[i]], store_sem).start()
        return carry

    lax.fori_loop(0, seen.shape[0], clear, 0, unroll=8)
    lax.fori_loop(0, count, count_rank, 0, unroll=4)
    for p in range(parts):
        loads[p].wait()
        lax.fori_loop(p * size, (p + 1) * size, issue, 0, unroll=4)
    pltpu.make_async_copy(staged, out_ref.at[pl.ds(0, count)], store_sem).wait()


def pack(ent_blocks, ent_owner, base, device_count):
    return pl.pallas_call(
        pack_kernel,
        out_shape=jax.ShapeDtypeStruct(
            (device_count * C,) + ent_blocks.shape[1:], ent_blocks.dtype
        ),
        in_specs=[
            pl.BlockSpec(memory_space=pltpu.SMEM),
            pl.BlockSpec(memory_space=pltpu.SMEM),
            pl.BlockSpec(memory_space=pl.ANY),
        ],
        out_specs=pl.BlockSpec(memory_space=pl.ANY),
        scratch_shapes=[
            pltpu.VMEM(ent_blocks.shape, ent_blocks.dtype),
            pltpu.SMEM((device_count,), jnp.int32),
            pltpu.SMEM((ent_blocks.shape[0],), jnp.int32),
            pltpu.SemaphoreType.DMA((4,)),
            pltpu.SemaphoreType.DMA,
        ],
        name="pack",
    )(base, ent_owner, ent_blocks)


def admit_kernel(spans, first_ref, order_ref, source_ref, density_ref, received_ref, *refs):
    part_refs, own, sems = refs[: len(spans)], refs[len(spans)], refs[len(spans) + 1]

    def add(j, total):
        return total + received_ref[order_ref[j]].astype(jnp.float32)

    def place(p, carry):
        t = source_ref[p]
        total = lax.fori_loop(
            first_ref[t], first_ref[t + 1], add, density_ref[t].astype(jnp.float32)
        )
        own[p] = total.astype(own.dtype)
        return carry

    copies = []
    done = 0
    for i, (low, high) in enumerate(spans):
        if high > done:
            lax.fori_loop(max(low, done), high, place, 0)
            done = high
        copies.append(pltpu.make_async_copy(own.at[pl.ds(low, high - low)], part_refs[i], sems.at[i]))
        copies[-1].start()
    for copy in copies:
        copy.wait()


def admit(density, received, first, order, source, spans):
    return pl.pallas_call(
        functools.partial(admit_kernel, spans),
        out_shape=[
            jax.ShapeDtypeStruct((high - low,) + density.shape[1:], density.dtype)
            for low, high in spans
        ],
        in_specs=[pl.BlockSpec(memory_space=pltpu.SMEM)] * 3
        + [pl.BlockSpec(memory_space=pltpu.VMEM)] * 2,
        out_specs=[pl.BlockSpec(memory_space=pl.ANY)] * len(spans),
        scratch_shapes=[
            pltpu.VMEM(density.shape, density.dtype),
            pltpu.SemaphoreType.DMA((len(spans),)),
        ],
        name="admit",
    )(first, order, source, density, received)


def reach(part):
    wide, narrow = divmod(part, 3)
    wides = (0, 1, 2) if wide == 0 else (0, wide)
    narrows = (0, 1, 2) if narrow == 0 else (0, narrow)
    return [w * 3 + n for w in wides for n in narrows]


NEAR_PARTS = 6


def near_count(part):
    return len([q for q in reach(part) if q < NEAR_PARTS])


def inner_count(part):
    return len([q for q in reach(part) if q < 3])


def far_count(part):
    return len(reach(part)) - near_count(part)


def load_pieces(pieces, piece_starts, table, sems):
    copies = []
    for i, (piece, start) in enumerate(zip(pieces, piece_starts)):
        copies.append(
            pltpu.make_async_copy(piece, table.at[pl.ds(start, piece.shape[0])], sems.at[i])
        )
        copies[-1].start()
    return copies


def lanes_of(ref, parts, group):
    return jnp.concatenate([ref[:, q * group:(q + 1) * group] for q in parts], axis=1)


def near_kernel(row_count, width, piece_starts, table_size, pos_ref, *refs):
    pieces = refs[: len(piece_starts)]
    outs = refs[len(piece_starts):]
    grids, (square, left_far, table, left, sems) = outs[:9], outs[9:]
    near = 9 * row_count
    group = row_count * width
    copies = load_pieces(pieces, piece_starts, table, sems)
    table[table_size] = jnp.zeros((width, width), table.dtype)
    for copy in copies:
        copy.wait()

    def block(m, k):
        return table[jnp.minimum(pos_ref[m * near + k], table_size)]

    for r in range(row_count):
        for k in range(near):
            left[r * width:(r + 1) * width, k * width:(k + 1) * width] = block(r, k)
    left_far[...] = left[:, NEAR_PARTS * group:]
    for part in range(9):
        parts = [q for q in reach(part) if q < NEAR_PARTS]
        for i, q in enumerate(parts):
            for r in range(row_count):
                for k in range(row_count):
                    low = (i * row_count + r) * width
                    grids[part][low:low + width, k * width:(k + 1) * width] = block(
                        q * row_count + r, part * row_count + k
                    )
        square[part] = jnp.dot(
            lanes_of(left, parts, group), grids[part][...], preferred_element_type=jnp.float32
        )


def square_near(positions, pieces, piece_starts, table_size, row_count, width):
    group = row_count * width
    span = 9 * group
    return pl.pallas_call(
        functools.partial(near_kernel, row_count, width, piece_starts, table_size),
        out_shape=[
            pltpu.VMEM((near_count(part) * group, group), jnp.bfloat16) for part in range(9)
        ] + [
            pltpu.VMEM((9, group, group), jnp.float32),
            pltpu.VMEM((group, (9 - NEAR_PARTS) * group), jnp.bfloat16),
        ],
        in_specs=[pl.BlockSpec(memory_space=pltpu.SMEM)]
        + [pl.BlockSpec(memory_space=pl.ANY)] * len(pieces),
        out_specs=[pl.BlockSpec(memory_space=pltpu.VMEM)] * 11,
        scratch_shapes=[
            pltpu.VMEM((table_size + 1, width, width), jnp.bfloat16),
            pltpu.VMEM((group, span), jnp.bfloat16),
            pltpu.SemaphoreType.DMA((len(pieces),)),
        ],
        compiler_params=pltpu.CompilerParams(vmem_limit_bytes=20 << 20),
        name="square_near",
    )(positions, *pieces)


def far_kernel(row_count, width, piece_starts, table_start, table_size, pos_ref, slot_ref, *refs):
    pieces = refs[: len(piece_starts)]
    outs = refs[len(piece_starts):]
    near_grids = outs[:9]
    square_in, left, out_ref, table, grid, square, square_b, early, staged, sems, out_sem = outs[9:]
    near = 9 * row_count
    group = row_count * width
    zero_at = table_start + table_size
    copies = load_pieces(pieces, piece_starts, table, sems)
    table[table_size] = jnp.zeros((width, width), table.dtype)
    middle = (3, 4, 5)

    def mask(part, product):
        for r in range(row_count):
            for k in range(row_count):
                listed = pos_ref[r * near + part * row_count + k] != zero_at
                low = part * group + k * width
                square_b[r * width:(r + 1) * width, low:low + width] = jnp.where(
                    listed, product[r * width:(r + 1) * width, k * width:(k + 1) * width], 0.0
                ).astype(jnp.bfloat16)

    for part in middle:
        mask(part, square_in[part])
    for part in range(NEAR_PARTS):
        early[part] = jnp.dot(
            lanes_of(square_b, [q for q in reach(part) if q in middle], group),
            near_grids[part][inner_count(part) * group:],
            preferred_element_type=jnp.float32,
        )
    for copy in copies:
        copy.wait()

    for part in range(9):
        parts = reach(part)
        base = near_count(part)
        far_base = sum(far_count(q) for q in range(part)) * group
        for i, q in enumerate(parts[base:]):
            for r in range(row_count):
                for k in range(row_count):
                    low = far_base + (i * row_count + r) * width
                    grid[low:low + width, k * width:(k + 1) * width] = table[
                        pos_ref[(q * row_count + r) * near + part * row_count + k] - table_start
                    ]
        product = square_in[part]
        if base < len(parts):
            product = product + jnp.dot(
                lanes_of(left, [q - NEAR_PARTS for q in parts[base:]], group),
                grid[far_base:far_base + far_count(part) * group],
                preferred_element_type=jnp.float32,
            )
        square[part] = product
        if part not in middle:
            mask(part, product)

    blocks = out_ref.shape[0]
    for part in range(9):
        parts = reach(part)
        base = near_count(part)
        far_base = sum(far_count(q) for q in range(part)) * group
        inner = inner_count(part)
        product = jnp.dot(
            lanes_of(square_b, parts[:inner], group), near_grids[part][:inner * group],
            preferred_element_type=jnp.float32,
        )
        if part < NEAR_PARTS:
            product = product + early[part]
        if base < len(parts):
            product = product + jnp.dot(
                lanes_of(square_b, parts[base:], group),
                grid[far_base:far_base + far_count(part) * group],
                preferred_element_type=jnp.float32,
            )
        result = 3.0 * square[part] - 2.0 * product
        for r in range(row_count):
            for k in range(row_count):
                slot = slot_ref[r * near + part * row_count + k]
                staged[slot] = result[r * width:(r + 1) * width, k * width:(k + 1) * width]

                @pl.when(slot < blocks)
                def _():
                    pltpu.make_async_copy(staged.at[slot], out_ref.at[slot], out_sem).start()

    pltpu.make_async_copy(staged.at[pl.ds(0, blocks)], out_ref, out_sem).wait()


def purify_far(
    positions, out_slots, pieces, piece_starts, carried, table_start, table_size,
    row_count, slot_count, width,
):
    group = row_count * width
    span = 9 * group
    blocks = row_count * slot_count
    return pl.pallas_call(
        functools.partial(
            far_kernel, row_count, width, piece_starts, table_start, table_size
        ),
        out_shape=jax.ShapeDtypeStruct((blocks, width, width), jnp.float32),
        in_specs=[pl.BlockSpec(memory_space=pltpu.SMEM)] * 2
        + [pl.BlockSpec(memory_space=pl.ANY)] * len(pieces)
        + [pl.BlockSpec(memory_space=pltpu.VMEM)] * len(carried),
        out_specs=pl.BlockSpec(memory_space=pl.ANY),
        scratch_shapes=[
            pltpu.VMEM((table_size + 1, width, width), jnp.bfloat16),
            pltpu.VMEM((sum(far_count(part) for part in range(9)) * group, group), jnp.bfloat16),
            pltpu.VMEM((9, group, group), jnp.float32),
            pltpu.VMEM((group, span), jnp.bfloat16),
            pltpu.VMEM((NEAR_PARTS, group, group), jnp.float32),
            pltpu.VMEM((blocks + 1, width, width), jnp.float32),
            pltpu.SemaphoreType.DMA((len(pieces),)),
            pltpu.SemaphoreType.DMA,
        ],
        compiler_params=pltpu.CompilerParams(vmem_limit_bytes=28 << 20),
        name="purify_far",
    )(
        positions, out_slots, *pieces,
        *[pltpu.with_memory_space_constraint(array, pltpu.VMEM) for array in carried],
    )


def block_positions(neighbours, here_x, here_y, starts, zero_at):
    wide_count, narrow_count, row_count, slot_count = neighbours.shape
    total_rows = wide_count * narrow_count * row_count
    listing = neighbours.reshape(total_rows, slot_count)
    ids = jnp.arange(9 * row_count, dtype=jnp.int32)
    wide, narrow, inner = ids // (3 * row_count), ids // row_count % 3, ids % row_count
    beyond = jnp.where(here_x % 2 == 0, here_x + wide_count - 1, here_x + 1) % wide_count
    near_x = jnp.where(wide == 0, here_x, jnp.where(wide == 1, here_x ^ 1, beyond))
    near_y = jnp.where(
        narrow == 0, here_y, jnp.where(narrow == 1, here_y ^ 1, narrow_count - 1 - here_y)
    )
    rows = (near_x * narrow_count + near_y) * row_count + inner
    lists = jnp.take(listing, rows, axis=0)
    list_x = lists // (narrow_count * row_count)
    list_y = lists // row_count % narrow_count
    aside = list_y == (near_y ^ 1)[:, None]
    kind = jnp.where(
        list_x == (near_x ^ 1)[:, None], jnp.where(aside, 2, 3), jnp.where(aside, 1, 0)
    )
    slot_ids = jnp.arange(slot_count, dtype=jnp.int32)
    key = kind * slot_count + slot_ids
    place = jnp.sum((key[:, :, None] > key[:, None, :]).astype(jnp.int32), axis=2)
    part = wide * 3 + narrow
    start = jnp.zeros_like(part)
    for i, value in enumerate(starts):
        start = jnp.where(part == i, value, start)
    held_at = (start + inner)[:, None] + place * row_count
    matches = lists[:, None, :] == rows[None, :, None]
    positions = jnp.min(jnp.where(matches, held_at[:, None, :], zero_at), axis=2)
    own_matches = matches[:row_count]
    own_slots = slot_ids + slot_count * jnp.arange(row_count, dtype=jnp.int32)[:, None, None]
    out_slots = jnp.min(jnp.where(own_matches, own_slots, row_count * slot_count), axis=2)
    order = (place[:row_count] * row_count + inner[:row_count, None]).reshape(-1)
    flat_ids = jnp.arange(row_count * slot_count, dtype=jnp.int32)
    source = jnp.sum(jnp.where(order[None, :] == flat_ids[:, None], flat_ids[None, :], 0), axis=1)
    return (
        positions.astype(jnp.int32).reshape(-1),
        out_slots.astype(jnp.int32).reshape(-1),
        source.astype(jnp.int32),
    )


def per_device(density, neighbours, ent_blocks, ent_owner, ent_place):
    wide_count = lax.axis_size("gx")
    narrow_count = lax.axis_size("gy")
    device_count = wide_count * narrow_count
    here_x = lax.axis_index("gx")
    here_y = lax.axis_index("gy")
    self_index = here_x * narrow_count + here_y
    row_count = density.shape[2]
    slot_count = density.shape[3]
    width = density.shape[4]
    blocks = row_count * slot_count
    held = ent_blocks.shape[0]
    owners = ent_owner.reshape(device_count, held)
    places = ent_place.reshape(device_count, held)

    base = (self_index * held).astype(jnp.int32).reshape(1)
    outgoing = pack(ent_blocks, ent_owner, base, device_count)
    received = lax.all_to_all(
        outgoing.reshape(device_count, C, width, width),
        ("gx", "gy"), split_axis=0, concat_axis=0, tiled=True,
    ).reshape(device_count * C, width, width)

    for_me = (owners == self_index).astype(jnp.int32)
    rank = jnp.cumsum(for_me, axis=1) - for_me
    picked = (for_me[:, :, None] == 1) & (
        rank[:, :, None] == jnp.arange(C, dtype=jnp.int32)[None, None, :]
    )
    slot_place = jnp.sum(jnp.where(picked, places[:, :, None], 0), axis=1).reshape(-1)
    slot_used = jnp.any(picked, axis=1).reshape(-1)
    slot_place = jnp.where(slot_used, slot_place, blocks)
    slot_ids = jnp.arange(device_count * C, dtype=jnp.int32)
    ahead = (slot_place[:, None] > slot_place[None, :]) | (
        (slot_place[:, None] == slot_place[None, :]) & (slot_ids[:, None] > slot_ids[None, :])
    )
    sorted_at = jnp.sum(ahead, axis=1)
    order = jnp.sum(
        jnp.where(sorted_at[None, :] == slot_ids[:, None], slot_ids[None, :], 0), axis=1
    ).astype(jnp.int32)
    target_ids = jnp.arange(blocks + 1, dtype=jnp.int32)
    first = jnp.sum(slot_place[None, :] < target_ids[:, None], axis=1).astype(jnp.int32)

    near_blocks = row_count * min(slot_count, 6 * row_count)
    corner_blocks = row_count * min(slot_count, 4 * row_count)
    sizes = [blocks] * 6 + [near_blocks, near_blocks, corner_blocks]
    starts = [sum(sizes[:i]) for i in range(9)]
    zero_at = sum(sizes)
    positions, out_slots, source = block_positions(neighbours, here_x, here_y, starts, zero_at)

    cut = corner_blocks // 2
    tail = blocks - 6 * row_count
    received, first, order, source, positions, out_slots = lax.optimization_barrier(
        (received, first, order, source, positions, out_slots)
    )
    flat_density = density.reshape(blocks, width, width)
    own_1, own_3, own_t = admit(
        flat_density, received, first, order, source,
        ((0, cut), (2 * cut, blocks), (tail, blocks)),
    )
    (own_2,) = admit(flat_density, received, first, order, source, ((cut, 2 * cut),))

    axes = ("gx", "gy")
    devices = [(x, y) for x in range(wide_count) for y in range(narrow_count)]

    def send(array, target):
        pairs = []
        for x, y in devices:
            to_x, to_y = target(x, y)
            pairs.append((x * narrow_count + y, to_x % wide_count * narrow_count + to_y))
        return lax.ppermute(array, axes, pairs)

    def across(x, y):
        return x, narrow_count - 1 - y

    def chip(x, y):
        return x, y ^ 1

    def ring(x, y):
        return x ^ 1, narrow_count - 1 - y

    def onward(x, y):
        return (x + 2 if x % 2 == 0 else x - 2), y

    ring_across_1 = send(own_1, ring)
    own_across_1 = send(own_1, across)
    ring_across_2 = send(own_2, ring)
    own_across_3 = send(own_3, across)
    far_across_1 = send(ring_across_1, onward)
    ring_same_1 = send(ring_across_1, across)
    own_chip_1 = send(own_1, chip)
    far_across_2 = send(ring_across_2[:cut // 2], onward)
    ring_same_2 = send(ring_across_2, across)
    ring_same_3 = send(own_across_3, ring)
    ring_across_t = send(own_t, ring)
    own_across_2 = send(own_2, across)
    own_chip_2 = send(own_2, chip)
    own_chip_3 = send(own_3, chip)
    far_same_1 = send(ring_same_1, onward)
    ring_chip_1 = send(ring_same_1, chip)
    far_same_3 = send(ring_same_3[:near_blocks - 2 * cut], onward)
    ring_chip_3 = send(ring_same_3, chip)
    far_same_2 = send(ring_same_2, onward)
    ring_chip_2 = send(ring_same_2, chip)
    far_across_3 = send(ring_across_2[cut // 2:], onward)
    far_chip_1 = send(far_same_1, chip)
    far_chip_3 = send(far_same_3, chip)
    far_chip_2 = send(far_same_2, chip)

    near_pieces = [
        (own_1, 0, 0), (own_2, 0, cut), (own_3, 0, 2 * cut),
        (own_chip_1, 1, 0), (own_chip_2, 1, cut), (own_chip_3, 1, 2 * cut),
        (own_across_1, 2, 0), (own_across_2, 2, cut), (own_across_3, 2, 2 * cut),
        (ring_same_1, 3, 0), (ring_same_2, 3, cut), (ring_same_3, 3, 2 * cut),
        (ring_chip_1, 4, 0), (ring_chip_2, 4, cut), (ring_chip_3, 4, 2 * cut),
        (ring_across_1, 5, 0), (ring_across_2, 5, cut), (ring_across_t, 5, tail),
    ]
    far_pieces = [
        (far_same_1, 6, 0), (far_same_2, 6, cut), (far_same_3, 6, 2 * cut),
        (far_chip_1, 7, 0), (far_chip_2, 7, cut), (far_chip_3, 7, 2 * cut),
        (far_across_1, 8, 0), (far_across_2, 8, cut), (far_across_3, 8, cut + cut // 2),
    ]
    far_start = starts[NEAR_PARTS]
    carried = square_near(
        positions, [piece for piece, _, _ in near_pieces],
        [starts[part] + offset for _, part, offset in near_pieces],
        far_start, row_count, width,
    )
    purified = purify_far(
        positions, out_slots, [piece for piece, _, _ in far_pieces],
        [starts[part] + offset - far_start for _, part, offset in far_pieces],
        carried, far_start, zero_at - far_start, row_count, slot_count, width,
    )
    return purified.reshape(density.shape)


def solution(mesh):
    in_specs = (P("gx", "gy", None, None, None, None), P(), P(("gx", "gy"), None, None), P(), P())
    out_specs = P("gx", "gy", None, None, None, None)
    return jax.shard_map(
        per_device, mesh=mesh, in_specs=in_specs, out_specs=out_specs, check_vma=False
    )
```

```python
import functools

import jax
import jax.numpy as jnp
from jax import lax
from jax.experimental import pallas as pl
from jax.experimental.pallas import tpu as pltpu
from jax.sharding import PartitionSpec as P

C = 2


def pack_kernel(base_ref, owner_ref, ent_ref, out_ref, staged, seen, load_sems, store_sem):
    count = ent_ref.shape[0]
    parts = load_sems.shape[0]
    size = count // parts
    loads = []
    for p in range(parts):
        rows = pl.ds(p * size, size)
        loads.append(pltpu.make_async_copy(ent_ref.at[rows], staged.at[rows], load_sems.at[p]))
        loads[-1].start()

    def clear(i, carry):
        seen[i] = 0
        return carry

    def issue(i, carry):
        owner = owner_ref[base_ref[0] + i]
        rank = seen[owner]
        seen[owner] = rank + 1
        slot = owner * C + rank
        pltpu.make_async_copy(staged.at[i], out_ref.at[slot], store_sem).start()
        return carry

    lax.fori_loop(0, seen.shape[0], clear, 0, unroll=8)
    for p in range(parts):
        loads[p].wait()
        lax.fori_loop(p * size, (p + 1) * size, issue, 0)
    pltpu.make_async_copy(staged, out_ref.at[pl.ds(0, count)], store_sem).wait()


def pack(ent_blocks, ent_owner, base, device_count):
    return pl.pallas_call(
        pack_kernel,
        out_shape=jax.ShapeDtypeStruct(
            (device_count * C,) + ent_blocks.shape[1:], ent_blocks.dtype
        ),
        in_specs=[
            pl.BlockSpec(memory_space=pltpu.SMEM),
            pl.BlockSpec(memory_space=pltpu.SMEM),
            pl.BlockSpec(memory_space=pl.ANY),
        ],
        out_specs=pl.BlockSpec(memory_space=pl.ANY),
        scratch_shapes=[
            pltpu.VMEM(ent_blocks.shape, ent_blocks.dtype),
            pltpu.SMEM((device_count,), jnp.int32),
            pltpu.SemaphoreType.DMA((4,)),
            pltpu.SemaphoreType.DMA,
        ],
        name="pack",
    )(base, ent_owner, ent_blocks)


def admit_kernel(spans, first_ref, order_ref, source_ref, density_ref, received_ref, *refs):
    part_refs, own, sems = refs[: len(spans)], refs[len(spans)], refs[len(spans) + 1]

    def add(j, total):
        return total + received_ref[order_ref[j]].astype(jnp.float32)

    def place(p, carry):
        t = source_ref[p]
        total = lax.fori_loop(
            first_ref[t], first_ref[t + 1], add, density_ref[t].astype(jnp.float32)
        )
        own[p] = total.astype(own.dtype)
        return carry

    copies = []
    done = 0
    for i, (low, high) in enumerate(spans):
        if high > done:
            lax.fori_loop(max(low, done), high, place, 0)
            done = high
        copies.append(pltpu.make_async_copy(own.at[pl.ds(low, high - low)], part_refs[i], sems.at[i]))
        copies[-1].start()
    for copy in copies:
        copy.wait()


def admit(density, received, first, order, source, spans):
    return pl.pallas_call(
        functools.partial(admit_kernel, spans),
        out_shape=[
            jax.ShapeDtypeStruct((high - low,) + density.shape[1:], density.dtype)
            for low, high in spans
        ],
        in_specs=[pl.BlockSpec(memory_space=pltpu.SMEM)] * 3
        + [pl.BlockSpec(memory_space=pltpu.VMEM)] * 2,
        out_specs=[pl.BlockSpec(memory_space=pl.ANY)] * len(spans),
        scratch_shapes=[
            pltpu.VMEM(density.shape, density.dtype),
            pltpu.SemaphoreType.DMA((len(spans),)),
        ],
        name="admit",
    )(first, order, source, density, received)


def reach(part):
    wide, narrow = divmod(part, 3)
    wides = (0, 1, 2) if wide == 0 else (0, wide)
    narrows = (0, 1, 2) if narrow == 0 else (0, narrow)
    return [w * 3 + n for w in wides for n in narrows]


NEAR_PARTS = 6


def near_count(part):
    return len([q for q in reach(part) if q < NEAR_PARTS])


def far_count(part):
    return len(reach(part)) - near_count(part)


def load_pieces(pieces, piece_starts, table, sems):
    copies = {}
    for i, (piece, (part, start)) in enumerate(zip(pieces, piece_starts)):
        copy = pltpu.make_async_copy(piece, table.at[pl.ds(start, piece.shape[0])], sems.at[i])
        copy.start()
        copies.setdefault(part, []).append(copy)
    return copies


def lanes_of(ref, parts, group):
    return jnp.concatenate([ref[:, q * group:(q + 1) * group] for q in parts], axis=1)


def near_kernel(row_count, width, piece_starts, table_size, pos_ref, *refs):
    pieces = refs[: len(piece_starts)]
    outs = refs[len(piece_starts):]
    grids, (square, left_far, table, left, sems) = outs[:9], outs[9:]
    near = 9 * row_count
    group = row_count * width
    copies = load_pieces(pieces, piece_starts, table, sems)
    table[table_size] = jnp.zeros((width, width), table.dtype)

    def block(m, k):
        return table[jnp.minimum(pos_ref[m * near + k], table_size)]

    for q in range(NEAR_PARTS):
        for copy in copies[q]:
            copy.wait()
        if q == 0:
            for r in range(row_count):
                for k in range(near):
                    left[r * width:(r + 1) * width, k * width:(k + 1) * width] = block(r, k)
            left_far[...] = left[:, NEAR_PARTS * group:]
        for part in range(9):
            if q not in reach(part):
                continue
            i = reach(part).index(q)
            for r in range(row_count):
                for k in range(row_count):
                    low = (i * row_count + r) * width
                    grids[part][low:low + width, k * width:(k + 1) * width] = block(
                        q * row_count + r, part * row_count + k
                    )
    for part in range(9):
        parts = [q for q in reach(part) if q < NEAR_PARTS]
        square[part] = jnp.dot(
            lanes_of(left, parts, group), grids[part][...], preferred_element_type=jnp.float32
        )


def square_near(positions, pieces, piece_starts, table_size, row_count, width):
    group = row_count * width
    span = 9 * group
    return pl.pallas_call(
        functools.partial(near_kernel, row_count, width, piece_starts, table_size),
        out_shape=[
            pltpu.VMEM((near_count(part) * group, group), jnp.bfloat16) for part in range(9)
        ] + [
            pltpu.VMEM((9, group, group), jnp.float32),
            pltpu.VMEM((group, (9 - NEAR_PARTS) * group), jnp.bfloat16),
        ],
        in_specs=[pl.BlockSpec(memory_space=pltpu.SMEM)]
        + [pl.BlockSpec(memory_space=pl.ANY)] * len(pieces),
        out_specs=[pl.BlockSpec(memory_space=pltpu.VMEM)] * 11,
        scratch_shapes=[
            pltpu.VMEM((table_size + 1, width, width), jnp.bfloat16),
            pltpu.VMEM((group, span), jnp.bfloat16),
            pltpu.SemaphoreType.DMA((len(pieces),)),
        ],
        compiler_params=pltpu.CompilerParams(vmem_limit_bytes=20 << 20),
        name="square_near",
    )(positions, *pieces)


def far_kernel(row_count, width, piece_starts, table_start, table_size, pos_ref, slot_ref, *refs):
    pieces = refs[: len(piece_starts)]
    outs = refs[len(piece_starts):]
    near_grids = outs[:9]
    square_in, left, out_ref, table, grid, square, square_b, staged, sems, out_sem = outs[9:]
    near = 9 * row_count
    group = row_count * width
    zero_at = table_start + table_size
    copies = load_pieces(pieces, piece_starts, table, sems)
    table[table_size] = jnp.zeros((width, width), table.dtype)
    for q in (8, 6, 7):
        for copy in copies[q]:
            copy.wait()
        for part in range(9):
            if q not in reach(part):
                continue
            i = reach(part).index(q) - near_count(part)
            far_base = sum(far_count(p) for p in range(part)) * group
            for r in range(row_count):
                for k in range(row_count):
                    low = far_base + (i * row_count + r) * width
                    grid[low:low + width, k * width:(k + 1) * width] = table[
                        pos_ref[(q * row_count + r) * near + part * row_count + k] - table_start
                    ]

    for part in range(9):
        parts = reach(part)
        base = near_count(part)
        far_base = sum(far_count(q) for q in range(part)) * group
        product = square_in[part]
        if base < len(parts):
            product = product + jnp.dot(
                lanes_of(left, [q - NEAR_PARTS for q in parts[base:]], group),
                grid[far_base:far_base + far_count(part) * group],
                preferred_element_type=jnp.float32,
            )
        square[part] = product
        for r in range(row_count):
            for k in range(row_count):
                listed = pos_ref[r * near + part * row_count + k] != zero_at
                low = part * group + k * width
                square_b[r * width:(r + 1) * width, low:low + width] = jnp.where(
                    listed, product[r * width:(r + 1) * width, k * width:(k + 1) * width], 0.0
                ).astype(jnp.bfloat16)

    blocks = out_ref.shape[0]
    for part in range(9):
        parts = reach(part)
        base = near_count(part)
        far_base = sum(far_count(q) for q in range(part)) * group
        product = jnp.dot(
            lanes_of(square_b, parts[:base], group), near_grids[part][...],
            preferred_element_type=jnp.float32,
        )
        if base < len(parts):
            product = product + jnp.dot(
                lanes_of(square_b, parts[base:], group),
                grid[far_base:far_base + far_count(part) * group],
                preferred_element_type=jnp.float32,
            )
        result = 3.0 * square[part] - 2.0 * product
        for r in range(row_count):
            for k in range(row_count):
                slot = slot_ref[r * near + part * row_count + k]
                staged[slot] = result[r * width:(r + 1) * width, k * width:(k + 1) * width]

                @pl.when(slot < blocks)
                def _():
                    pltpu.make_async_copy(staged.at[slot], out_ref.at[slot], out_sem).start()

    pltpu.make_async_copy(staged.at[pl.ds(0, blocks)], out_ref, out_sem).wait()


def purify_far(
    positions, out_slots, pieces, piece_starts, carried, table_start, table_size,
    row_count, slot_count, width,
):
    group = row_count * width
    span = 9 * group
    blocks = row_count * slot_count
    return pl.pallas_call(
        functools.partial(
            far_kernel, row_count, width, piece_starts, table_start, table_size
        ),
        out_shape=jax.ShapeDtypeStruct((blocks, width, width), jnp.float32),
        in_specs=[pl.BlockSpec(memory_space=pltpu.SMEM)] * 2
        + [pl.BlockSpec(memory_space=pl.ANY)] * len(pieces)
        + [pl.BlockSpec(memory_space=pltpu.VMEM)] * len(carried),
        out_specs=pl.BlockSpec(memory_space=pl.ANY),
        scratch_shapes=[
            pltpu.VMEM((table_size + 1, width, width), jnp.bfloat16),
            pltpu.VMEM((sum(far_count(part) for part in range(9)) * group, group), jnp.bfloat16),
            pltpu.VMEM((9, group, group), jnp.float32),
            pltpu.VMEM((group, span), jnp.bfloat16),
            pltpu.VMEM((blocks + 1, width, width), jnp.float32),
            pltpu.SemaphoreType.DMA((len(pieces),)),
            pltpu.SemaphoreType.DMA,
        ],
        compiler_params=pltpu.CompilerParams(vmem_limit_bytes=28 << 20),
        name="purify_far",
    )(
        positions, out_slots, *pieces,
        *[pltpu.with_memory_space_constraint(array, pltpu.VMEM) for array in carried],
    )


def block_positions(neighbours, here_x, here_y, starts, zero_at):
    wide_count, narrow_count, row_count, slot_count = neighbours.shape
    total_rows = wide_count * narrow_count * row_count
    listing = neighbours.reshape(total_rows, slot_count)
    ids = jnp.arange(9 * row_count, dtype=jnp.int32)
    wide, narrow, inner = ids // (3 * row_count), ids // row_count % 3, ids % row_count
    beyond = jnp.where(here_x % 2 == 0, here_x + wide_count - 1, here_x + 1) % wide_count
    near_x = jnp.where(wide == 0, here_x, jnp.where(wide == 1, here_x ^ 1, beyond))
    near_y = jnp.where(
        narrow == 0, here_y, jnp.where(narrow == 1, here_y ^ 1, narrow_count - 1 - here_y)
    )
    rows = (near_x * narrow_count + near_y) * row_count + inner
    lists = jnp.take(listing, rows, axis=0)
    list_x = lists // (narrow_count * row_count)
    list_y = lists // row_count % narrow_count
    aside = list_y == (near_y ^ 1)[:, None]
    kind = jnp.where(
        list_x == (near_x ^ 1)[:, None], jnp.where(aside, 2, 3), jnp.where(aside, 1, 0)
    )
    slot_ids = jnp.arange(slot_count, dtype=jnp.int32)
    key = kind * slot_count + slot_ids
    place = jnp.sum((key[:, :, None] > key[:, None, :]).astype(jnp.int32), axis=2)
    part = wide * 3 + narrow
    start = jnp.zeros_like(part)
    for i, value in enumerate(starts):
        start = jnp.where(part == i, value, start)
    held_at = (start + inner)[:, None] + place * row_count
    matches = lists[:, None, :] == rows[None, :, None]
    positions = jnp.min(jnp.where(matches, held_at[:, None, :], zero_at), axis=2)
    own_matches = matches[:row_count]
    own_slots = slot_ids + slot_count * jnp.arange(row_count, dtype=jnp.int32)[:, None, None]
    out_slots = jnp.min(jnp.where(own_matches, own_slots, row_count * slot_count), axis=2)
    order = (place[:row_count] * row_count + inner[:row_count, None]).reshape(-1)
    flat_ids = jnp.arange(row_count * slot_count, dtype=jnp.int32)
    source = jnp.sum(jnp.where(order[None, :] == flat_ids[:, None], flat_ids[None, :], 0), axis=1)
    return (
        positions.astype(jnp.int32).reshape(-1),
        out_slots.astype(jnp.int32).reshape(-1),
        source.astype(jnp.int32),
    )


def per_device(density, neighbours, ent_blocks, ent_owner, ent_place):
    wide_count = lax.axis_size("gx")
    narrow_count = lax.axis_size("gy")
    device_count = wide_count * narrow_count
    here_x = lax.axis_index("gx")
    here_y = lax.axis_index("gy")
    self_index = here_x * narrow_count + here_y
    row_count = density.shape[2]
    slot_count = density.shape[3]
    width = density.shape[4]
    blocks = row_count * slot_count
    held = ent_blocks.shape[0]
    owners = ent_owner.reshape(device_count, held)
    places = ent_place.reshape(device_count, held)

    base = (self_index * held).astype(jnp.int32).reshape(1)
    outgoing = pack(ent_blocks, ent_owner, base, device_count)
    received = lax.all_to_all(
        outgoing.reshape(device_count, C, width, width),
        ("gx", "gy"), split_axis=0, concat_axis=0, tiled=True,
    ).reshape(device_count * C, width, width)

    for_me = (owners == self_index).astype(jnp.int32)
    rank = jnp.cumsum(for_me, axis=1) - for_me
    picked = (for_me[:, :, None] == 1) & (
        rank[:, :, None] == jnp.arange(C, dtype=jnp.int32)[None, None, :]
    )
    slot_place = jnp.sum(jnp.where(picked, places[:, :, None], 0), axis=1).reshape(-1)
    slot_used = jnp.any(picked, axis=1).reshape(-1)
    slot_place = jnp.where(slot_used, slot_place, blocks)
    slot_ids = jnp.arange(device_count * C, dtype=jnp.int32)
    ahead = (slot_place[:, None] > slot_place[None, :]) | (
        (slot_place[:, None] == slot_place[None, :]) & (slot_ids[:, None] > slot_ids[None, :])
    )
    sorted_at = jnp.sum(ahead, axis=1)
    order = jnp.sum(
        jnp.where(sorted_at[None, :] == slot_ids[:, None], slot_ids[None, :], 0), axis=1
    ).astype(jnp.int32)
    target_ids = jnp.arange(blocks + 1, dtype=jnp.int32)
    first = jnp.sum(slot_place[None, :] < target_ids[:, None], axis=1).astype(jnp.int32)

    near_blocks = row_count * min(slot_count, 6 * row_count)
    corner_blocks = row_count * min(slot_count, 4 * row_count)
    sizes = [blocks] * 6 + [near_blocks, near_blocks, corner_blocks]
    starts = [sum(sizes[:i]) for i in range(9)]
    zero_at = sum(sizes)
    positions, out_slots, source = block_positions(neighbours, here_x, here_y, starts, zero_at)

    cut = corner_blocks // 2
    tail = blocks - 6 * row_count
    received, first, order, source, positions, out_slots = lax.optimization_barrier(
        (received, first, order, source, positions, out_slots)
    )
    flat_density = density.reshape(blocks, width, width)
    own_1, own_3, own_t = admit(
        flat_density, received, first, order, source,
        ((0, cut), (2 * cut, blocks), (tail, blocks)),
    )
    (own_2,) = admit(flat_density, received, first, order, source, ((cut, 2 * cut),))

    axes = ("gx", "gy")
    devices = [(x, y) for x in range(wide_count) for y in range(narrow_count)]

    def send(array, target):
        pairs = []
        for x, y in devices:
            to_x, to_y = target(x, y)
            pairs.append((x * narrow_count + y, to_x % wide_count * narrow_count + to_y))
        return lax.ppermute(array, axes, pairs)

    def across(x, y):
        return x, narrow_count - 1 - y

    def chip(x, y):
        return x, y ^ 1

    def ring(x, y):
        return x ^ 1, narrow_count - 1 - y

    def onward(x, y):
        return (x + 2 if x % 2 == 0 else x - 2), y

    ring_across_1 = send(own_1, ring)
    own_across_1 = send(own_1, across)
    ring_across_2 = send(own_2, ring)
    own_across_3 = send(own_3, across)
    far_across_1 = send(ring_across_1, onward)
    ring_same_1 = send(ring_across_1, across)
    own_chip_1 = send(own_1, chip)
    far_across_2 = send(ring_across_2[:cut // 2], onward)
    ring_same_2 = send(ring_across_2, across)
    ring_same_3 = send(own_across_3, ring)
    ring_across_t = send(own_t, ring)
    own_across_2 = send(own_2, across)
    own_chip_2 = send(own_2, chip)
    own_chip_3 = send(own_3, chip)
    far_same_1 = send(ring_same_1, onward)
    ring_chip_1 = send(ring_same_1, chip)
    far_same_3 = send(ring_same_3[:near_blocks - 2 * cut], onward)
    ring_chip_3 = send(ring_same_3, chip)
    far_same_2 = send(ring_same_2, onward)
    ring_chip_2 = send(ring_same_2, chip)
    far_across_3 = send(far_same_2[cut // 2:], across)
    far_chip_1 = send(far_same_1, chip)
    far_chip_3 = send(far_same_3, chip)
    far_chip_2 = send(far_same_2, chip)

    near_pieces = [
        (own_1, 0, 0), (own_2, 0, cut), (own_3, 0, 2 * cut),
        (own_chip_1, 1, 0), (own_chip_2, 1, cut), (own_chip_3, 1, 2 * cut),
        (own_across_1, 2, 0), (own_across_2, 2, cut), (own_across_3, 2, 2 * cut),
        (ring_same_1, 3, 0), (ring_same_2, 3, cut), (ring_same_3, 3, 2 * cut),
        (ring_chip_1, 4, 0), (ring_chip_2, 4, cut), (ring_chip_3, 4, 2 * cut),
        (ring_across_1, 5, 0), (ring_across_2, 5, cut), (ring_across_t, 5, tail),
    ]
    far_pieces = [
        (far_across_1, 8, 0), (far_across_2, 8, cut), (far_across_3, 8, cut + cut // 2),
        (far_same_1, 6, 0), (far_same_2, 6, cut), (far_same_3, 6, 2 * cut),
        (far_chip_1, 7, 0), (far_chip_2, 7, cut), (far_chip_3, 7, 2 * cut),
    ]
    far_start = starts[NEAR_PARTS]
    carried = square_near(
        positions, [piece for piece, _, _ in near_pieces],
        [(part, starts[part] + offset) for _, part, offset in near_pieces],
        far_start, row_count, width,
    )
    purified = purify_far(
        positions, out_slots, [piece for piece, _, _ in far_pieces],
        [(part, starts[part] + offset - far_start) for _, part, offset in far_pieces],
        carried, far_start, zero_at - far_start, row_count, slot_count, width,
    )
    return purified.reshape(density.shape)


def solution(mesh):
    in_specs = (P("gx", "gy", None, None, None, None), P(), P(("gx", "gy"), None, None), P(), P())
    out_specs = P("gx", "gy", None, None, None, None)
    return jax.shard_map(
        per_device, mesh=mesh, in_specs=in_specs, out_specs=out_specs, check_vma=False
    )
```

```python
import functools

import jax
import jax.numpy as jnp
from jax import lax
from jax.experimental import pallas as pl
from jax.experimental.pallas import tpu as pltpu
from jax.sharding import PartitionSpec as P

C = 2


def pack_kernel(base_ref, owner_ref, ent_ref, out_ref, staged, seen, load_sems, store_sem):
    count = ent_ref.shape[0]
    parts = load_sems.shape[0]
    size = count // parts
    loads = []
    for p in range(parts):
        rows = pl.ds(p * size, size)
        loads.append(pltpu.make_async_copy(ent_ref.at[rows], staged.at[rows], load_sems.at[p]))
        loads[-1].start()

    def clear(i, carry):
        seen[i] = 0
        return carry

    def issue(i, carry):
        owner = owner_ref[base_ref[0] + i]
        rank = seen[owner]
        seen[owner] = rank + 1
        slot = owner * C + rank
        pltpu.make_async_copy(staged.at[i], out_ref.at[slot], store_sem).start()
        return carry

    lax.fori_loop(0, seen.shape[0], clear, 0, unroll=8)
    for p in range(parts):
        loads[p].wait()
        lax.fori_loop(p * size, (p + 1) * size, issue, 0)
    pltpu.make_async_copy(staged, out_ref.at[pl.ds(0, count)], store_sem).wait()


def pack(ent_blocks, ent_owner, base, device_count):
    return pl.pallas_call(
        pack_kernel,
        out_shape=jax.ShapeDtypeStruct(
            (device_count * C,) + ent_blocks.shape[1:], ent_blocks.dtype
        ),
        in_specs=[
            pl.BlockSpec(memory_space=pltpu.SMEM),
            pl.BlockSpec(memory_space=pltpu.SMEM),
            pl.BlockSpec(memory_space=pl.ANY),
        ],
        out_specs=pl.BlockSpec(memory_space=pl.ANY),
        scratch_shapes=[
            pltpu.VMEM(ent_blocks.shape, ent_blocks.dtype),
            pltpu.SMEM((device_count,), jnp.int32),
            pltpu.SemaphoreType.DMA((4,)),
            pltpu.SemaphoreType.DMA,
        ],
        name="pack",
    )(base, ent_owner, ent_blocks)


def admit_kernel(spans, first_ref, order_ref, source_ref, density_ref, received_ref, *refs):
    part_refs, own, sems = refs[: len(spans)], refs[len(spans)], refs[len(spans) + 1]

    def add(j, total):
        return total + received_ref[order_ref[j]].astype(jnp.float32)

    def place(p, carry):
        t = source_ref[p]
        total = lax.fori_loop(
            first_ref[t], first_ref[t + 1], add, density_ref[t].astype(jnp.float32)
        )
        own[p] = total.astype(own.dtype)
        return carry

    copies = []
    done = 0
    for i, (low, high) in enumerate(spans):
        if high > done:
            lax.fori_loop(max(low, done), high, place, 0)
            done = high
        copies.append(pltpu.make_async_copy(own.at[pl.ds(low, high - low)], part_refs[i], sems.at[i]))
        copies[-1].start()
    for copy in copies:
        copy.wait()


def admit(density, received, first, order, source, spans):
    return pl.pallas_call(
        functools.partial(admit_kernel, spans),
        out_shape=[
            jax.ShapeDtypeStruct((high - low,) + density.shape[1:], density.dtype)
            for low, high in spans
        ],
        in_specs=[pl.BlockSpec(memory_space=pltpu.SMEM)] * 3
        + [pl.BlockSpec(memory_space=pltpu.VMEM)] * 2,
        out_specs=[pl.BlockSpec(memory_space=pl.ANY)] * len(spans),
        scratch_shapes=[
            pltpu.VMEM(density.shape, density.dtype),
            pltpu.SemaphoreType.DMA((len(spans),)),
        ],
        name="admit",
    )(first, order, source, density, received)


def reach(part):
    wide, narrow = divmod(part, 3)
    wides = (0, 1, 2) if wide == 0 else (0, wide)
    narrows = (0, 1, 2) if narrow == 0 else (0, narrow)
    return [w * 3 + n for w in wides for n in narrows]


NEAR_PARTS = 6


def near_count(part):
    return len([q for q in reach(part) if q < NEAR_PARTS])


def far_count(part):
    return len(reach(part)) - near_count(part)


def load_pieces(pieces, piece_starts, table, sems, order):
    copies = {part: [] for part in order}
    for i, (piece, (part, start)) in enumerate(zip(pieces, piece_starts)):
        place = table.at[pl.ds(start, piece.shape[0])]
        copies[part].append(pltpu.make_async_copy(piece, place, sems.at[i]))
    for part in order:
        for copy in copies[part]:
            copy.start()
    return copies


def wait_for(copies, parts):
    for part in parts:
        for copy in copies.pop(part, ()):
            copy.wait()


def lanes_of(ref, parts, group):
    return jnp.concatenate([ref[:, q * group:(q + 1) * group] for q in parts], axis=1)


def near_kernel(row_count, width, piece_starts, table_size, pos_ref, *refs):
    pieces = refs[: len(piece_starts)]
    outs = refs[len(piece_starts):]
    grids, (square, left_far, table, left, sems) = outs[:9], outs[9:]
    near = 9 * row_count
    group = row_count * width
    copies = load_pieces(pieces, piece_starts, table, sems, (0, 1, 3, 4, 2, 5))
    table[table_size] = jnp.zeros((width, width), table.dtype)
    wait_for(copies, (0,))

    def block(m, k):
        return table[jnp.minimum(pos_ref[m * near + k], table_size)]

    for r in range(row_count):
        for k in range(near):
            left[r * width:(r + 1) * width, k * width:(k + 1) * width] = block(r, k)
    left_far[...] = left[:, NEAR_PARTS * group:]
    for part in (7, 4, 1, 8, 6, 5, 2, 3, 0):
        parts = [q for q in reach(part) if q < NEAR_PARTS]
        wait_for(copies, parts)
        for i, q in enumerate(parts):
            for r in range(row_count):
                for k in range(row_count):
                    low = (i * row_count + r) * width
                    grids[part][low:low + width, k * width:(k + 1) * width] = block(
                        q * row_count + r, part * row_count + k
                    )
        square[part] = jnp.dot(
            lanes_of(left, parts, group), grids[part][...], preferred_element_type=jnp.float32
        )


def square_near(positions, pieces, piece_starts, table_size, row_count, width):
    group = row_count * width
    span = 9 * group
    return pl.pallas_call(
        functools.partial(near_kernel, row_count, width, piece_starts, table_size),
        out_shape=[
            pltpu.VMEM((near_count(part) * group, group), jnp.bfloat16) for part in range(9)
        ] + [
            pltpu.VMEM((9, group, group), jnp.float32),
            pltpu.VMEM((group, (9 - NEAR_PARTS) * group), jnp.bfloat16),
        ],
        in_specs=[pl.BlockSpec(memory_space=pltpu.SMEM)]
        + [pl.BlockSpec(memory_space=pl.ANY)] * len(pieces),
        out_specs=[pl.BlockSpec(memory_space=pltpu.VMEM)] * 11,
        scratch_shapes=[
            pltpu.VMEM((table_size + 1, width, width), jnp.bfloat16),
            pltpu.VMEM((group, span), jnp.bfloat16),
            pltpu.SemaphoreType.DMA((len(pieces),)),
        ],
        compiler_params=pltpu.CompilerParams(vmem_limit_bytes=20 << 20),
        name="square_near",
    )(positions, *pieces)


def far_kernel(row_count, width, piece_starts, table_start, table_size, pos_ref, slot_ref, *refs):
    pieces = refs[: len(piece_starts)]
    outs = refs[len(piece_starts):]
    near_grids = outs[:9]
    square_in, left, out_ref, table, grid, square, square_b, staged, sems, out_sem = outs[9:]
    near = 9 * row_count
    group = row_count * width
    zero_at = table_start + table_size
    copies = load_pieces(pieces, piece_starts, table, sems, (8, 6, 7))
    table[table_size] = jnp.zeros((width, width), table.dtype)

    for part in (3, 4, 5, 2, 8, 1, 7, 0, 6):
        parts = reach(part)
        base = near_count(part)
        wait_for(copies, parts[base:])
        far_base = sum(far_count(q) for q in range(part)) * group
        for i, q in enumerate(parts[base:]):
            for r in range(row_count):
                for k in range(row_count):
                    low = far_base + (i * row_count + r) * width
                    grid[low:low + width, k * width:(k + 1) * width] = table[
                        pos_ref[(q * row_count + r) * near + part * row_count + k] - table_start
                    ]
        product = square_in[part]
        if base < len(parts):
            product = product + jnp.dot(
                lanes_of(left, [q - NEAR_PARTS for q in parts[base:]], group),
                grid[far_base:far_base + far_count(part) * group],
                preferred_element_type=jnp.float32,
            )
        square[part] = product
        for r in range(row_count):
            for k in range(row_count):
                listed = pos_ref[r * near + part * row_count + k] != zero_at
                low = part * group + k * width
                square_b[r * width:(r + 1) * width, low:low + width] = jnp.where(
                    listed, product[r * width:(r + 1) * width, k * width:(k + 1) * width], 0.0
                ).astype(jnp.bfloat16)

    blocks = out_ref.shape[0]
    for part in range(9):
        parts = reach(part)
        base = near_count(part)
        far_base = sum(far_count(q) for q in range(part)) * group
        product = jnp.dot(
            lanes_of(square_b, parts[:base], group), near_grids[part][...],
            preferred_element_type=jnp.float32,
        )
        if base < len(parts):
            product = product + jnp.dot(
                lanes_of(square_b, parts[base:], group),
                grid[far_base:far_base + far_count(part) * group],
                preferred_element_type=jnp.float32,
            )
        result = 3.0 * square[part] - 2.0 * product
        for r in range(row_count):
            for k in range(row_count):
                slot = slot_ref[r * near + part * row_count + k]
                staged[slot] = result[r * width:(r + 1) * width, k * width:(k + 1) * width]

                @pl.when(slot < blocks)
                def _():
                    pltpu.make_async_copy(staged.at[slot], out_ref.at[slot], out_sem).start()

    pltpu.make_async_copy(staged.at[pl.ds(0, blocks)], out_ref, out_sem).wait()


def purify_far(
    positions, out_slots, pieces, piece_starts, carried, table_start, table_size,
    row_count, slot_count, width,
):
    group = row_count * width
    span = 9 * group
    blocks = row_count * slot_count
    return pl.pallas_call(
        functools.partial(
            far_kernel, row_count, width, piece_starts, table_start, table_size
        ),
        out_shape=jax.ShapeDtypeStruct((blocks, width, width), jnp.float32),
        in_specs=[pl.BlockSpec(memory_space=pltpu.SMEM)] * 2
        + [pl.BlockSpec(memory_space=pl.ANY)] * len(pieces)
        + [pl.BlockSpec(memory_space=pltpu.VMEM)] * len(carried),
        out_specs=pl.BlockSpec(memory_space=pl.ANY),
        scratch_shapes=[
            pltpu.VMEM((table_size + 1, width, width), jnp.bfloat16),
            pltpu.VMEM((sum(far_count(part) for part in range(9)) * group, group), jnp.bfloat16),
            pltpu.VMEM((9, group, group), jnp.float32),
            pltpu.VMEM((group, span), jnp.bfloat16),
            pltpu.VMEM((blocks + 1, width, width), jnp.float32),
            pltpu.SemaphoreType.DMA((len(pieces),)),
            pltpu.SemaphoreType.DMA,
        ],
        compiler_params=pltpu.CompilerParams(vmem_limit_bytes=28 << 20),
        name="purify_far",
    )(
        positions, out_slots, *pieces,
        *[pltpu.with_memory_space_constraint(array, pltpu.VMEM) for array in carried],
    )


def block_positions(neighbours, here_x, here_y, starts, zero_at):
    wide_count, narrow_count, row_count, slot_count = neighbours.shape
    total_rows = wide_count * narrow_count * row_count
    listing = neighbours.reshape(total_rows, slot_count)
    ids = jnp.arange(9 * row_count, dtype=jnp.int32)
    wide, narrow, inner = ids // (3 * row_count), ids // row_count % 3, ids % row_count
    beyond = jnp.where(here_x % 2 == 0, here_x + wide_count - 1, here_x + 1) % wide_count
    near_x = jnp.where(wide == 0, here_x, jnp.where(wide == 1, here_x ^ 1, beyond))
    near_y = jnp.where(
        narrow == 0, here_y, jnp.where(narrow == 1, here_y ^ 1, narrow_count - 1 - here_y)
    )
    rows = (near_x * narrow_count + near_y) * row_count + inner
    lists = jnp.take(listing, rows, axis=0)
    list_x = lists // (narrow_count * row_count)
    list_y = lists // row_count % narrow_count
    aside = list_y == (near_y ^ 1)[:, None]
    kind = jnp.where(
        list_x == (near_x ^ 1)[:, None], jnp.where(aside, 2, 3), jnp.where(aside, 1, 0)
    )
    slot_ids = jnp.arange(slot_count, dtype=jnp.int32)
    key = kind * slot_count + slot_ids
    place = jnp.sum((key[:, :, None] > key[:, None, :]).astype(jnp.int32), axis=2)
    part = wide * 3 + narrow
    start = jnp.zeros_like(part)
    for i, value in enumerate(starts):
        start = jnp.where(part == i, value, start)
    held_at = (start + inner)[:, None] + place * row_count
    matches = lists[:, None, :] == rows[None, :, None]
    positions = jnp.min(jnp.where(matches, held_at[:, None, :], zero_at), axis=2)
    own_matches = matches[:row_count]
    own_slots = slot_ids + slot_count * jnp.arange(row_count, dtype=jnp.int32)[:, None, None]
    out_slots = jnp.min(jnp.where(own_matches, own_slots, row_count * slot_count), axis=2)
    order = (place[:row_count] * row_count + inner[:row_count, None]).reshape(-1)
    flat_ids = jnp.arange(row_count * slot_count, dtype=jnp.int32)
    source = jnp.sum(jnp.where(order[None, :] == flat_ids[:, None], flat_ids[None, :], 0), axis=1)
    return (
        positions.astype(jnp.int32).reshape(-1),
        out_slots.astype(jnp.int32).reshape(-1),
        source.astype(jnp.int32),
    )


def per_device(density, neighbours, ent_blocks, ent_owner, ent_place):
    wide_count = lax.axis_size("gx")
    narrow_count = lax.axis_size("gy")
    device_count = wide_count * narrow_count
    here_x = lax.axis_index("gx")
    here_y = lax.axis_index("gy")
    self_index = here_x * narrow_count + here_y
    row_count = density.shape[2]
    slot_count = density.shape[3]
    width = density.shape[4]
    blocks = row_count * slot_count
    held = ent_blocks.shape[0]
    owners = ent_owner.reshape(device_count, held)
    places = ent_place.reshape(device_count, held)

    base = (self_index * held).astype(jnp.int32).reshape(1)
    outgoing = pack(ent_blocks, ent_owner, base, device_count)
    received = lax.all_to_all(
        outgoing.reshape(device_count, C, width, width),
        ("gx", "gy"), split_axis=0, concat_axis=0, tiled=True,
    ).reshape(device_count * C, width, width)

    for_me = (owners == self_index).astype(jnp.int32)
    rank = jnp.cumsum(for_me, axis=1) - for_me
    picked = (for_me[:, :, None] == 1) & (
        rank[:, :, None] == jnp.arange(C, dtype=jnp.int32)[None, None, :]
    )
    slot_place = jnp.sum(jnp.where(picked, places[:, :, None], 0), axis=1).reshape(-1)
    slot_used = jnp.any(picked, axis=1).reshape(-1)
    slot_place = jnp.where(slot_used, slot_place, blocks)
    slot_ids = jnp.arange(device_count * C, dtype=jnp.int32)
    ahead = (slot_place[:, None] > slot_place[None, :]) | (
        (slot_place[:, None] == slot_place[None, :]) & (slot_ids[:, None] > slot_ids[None, :])
    )
    sorted_at = jnp.sum(ahead, axis=1)
    order = jnp.sum(
        jnp.where(sorted_at[None, :] == slot_ids[:, None], slot_ids[None, :], 0), axis=1
    ).astype(jnp.int32)
    target_ids = jnp.arange(blocks + 1, dtype=jnp.int32)
    first = jnp.sum(slot_place[None, :] < target_ids[:, None], axis=1).astype(jnp.int32)

    near_blocks = row_count * min(slot_count, 6 * row_count)
    corner_blocks = row_count * min(slot_count, 4 * row_count)
    sizes = [blocks] * 6 + [near_blocks, near_blocks, corner_blocks]
    starts = [sum(sizes[:i]) for i in range(9)]
    zero_at = sum(sizes)
    positions, out_slots, source = block_positions(neighbours, here_x, here_y, starts, zero_at)

    cut = corner_blocks // 2
    tail = blocks - 6 * row_count
    received, first, order, source, positions, out_slots = lax.optimization_barrier(
        (received, first, order, source, positions, out_slots)
    )
    flat_density = density.reshape(blocks, width, width)
    own_1, own_3, own_t = admit(
        flat_density, received, first, order, source,
        ((0, cut), (2 * cut, blocks), (tail, blocks)),
    )
    (own_2,) = admit(flat_density, received, first, order, source, ((cut, 2 * cut),))

    axes = ("gx", "gy")
    devices = [(x, y) for x in range(wide_count) for y in range(narrow_count)]

    def send(array, target):
        pairs = []
        for x, y in devices:
            to_x, to_y = target(x, y)
            pairs.append((x * narrow_count + y, to_x % wide_count * narrow_count + to_y))
        return lax.ppermute(array, axes, pairs)

    def across(x, y):
        return x, narrow_count - 1 - y

    def chip(x, y):
        return x, y ^ 1

    def ring(x, y):
        return x ^ 1, narrow_count - 1 - y

    def onward(x, y):
        return (x + 2 if x % 2 == 0 else x - 2), y

    ring_across_1 = send(own_1, ring)
    own_across_1 = send(own_1, across)
    ring_across_2 = send(own_2, ring)
    own_across_3 = send(own_3, across)
    far_across_1 = send(ring_across_1, onward)
    ring_same_1 = send(ring_across_1, across)
    own_chip_1 = send(own_1, chip)
    far_across_2 = send(ring_across_2[:cut // 2], onward)
    ring_same_2 = send(ring_across_2, across)
    ring_same_3 = send(own_across_3, ring)
    ring_across_t = send(own_t, ring)
    own_across_2 = send(own_2, across)
    own_chip_2 = send(own_2, chip)
    own_chip_3 = send(own_3, chip)
    far_same_1 = send(ring_same_1, onward)
    ring_chip_1 = send(ring_same_1, chip)
    far_same_3 = send(ring_same_3[:near_blocks - 2 * cut], onward)
    ring_chip_3 = send(ring_same_3, chip)
    far_same_2 = send(ring_same_2, onward)
    ring_chip_2 = send(ring_same_2, chip)
    far_across_3 = send(far_same_2[cut // 2:], across)
    far_chip_1 = send(far_same_1, chip)
    far_chip_3 = send(far_same_3, chip)
    far_chip_2 = send(far_same_2, chip)

    near_pieces = [
        (own_1, 0, 0), (own_2, 0, cut), (own_3, 0, 2 * cut),
        (own_chip_1, 1, 0), (own_chip_2, 1, cut), (own_chip_3, 1, 2 * cut),
        (own_across_1, 2, 0), (own_across_2, 2, cut), (own_across_3, 2, 2 * cut),
        (ring_same_1, 3, 0), (ring_same_2, 3, cut), (ring_same_3, 3, 2 * cut),
        (ring_chip_1, 4, 0), (ring_chip_2, 4, cut), (ring_chip_3, 4, 2 * cut),
        (ring_across_1, 5, 0), (ring_across_2, 5, cut), (ring_across_t, 5, tail),
    ]
    far_pieces = [
        (far_same_1, 6, 0), (far_same_2, 6, cut), (far_same_3, 6, 2 * cut),
        (far_chip_1, 7, 0), (far_chip_2, 7, cut), (far_chip_3, 7, 2 * cut),
        (far_across_1, 8, 0), (far_across_2, 8, cut), (far_across_3, 8, cut + cut // 2),
    ]
    far_start = starts[NEAR_PARTS]
    carried = square_near(
        positions, [piece for piece, _, _ in near_pieces],
        [(part, starts[part] + offset) for _, part, offset in near_pieces],
        far_start, row_count, width,
    )
    purified = purify_far(
        positions, out_slots, [piece for piece, _, _ in far_pieces],
        [(part, starts[part] + offset - far_start) for _, part, offset in far_pieces],
        carried, far_start, zero_at - far_start, row_count, slot_count, width,
    )
    return purified.reshape(density.shape)


def solution(mesh):
    in_specs = (P("gx", "gy", None, None, None, None), P(), P(("gx", "gy"), None, None), P(), P())
    out_specs = P("gx", "gy", None, None, None, None)
    return jax.shard_map(
        per_device, mesh=mesh, in_specs=in_specs, out_specs=out_specs, check_vma=False
    )
```

```python
import functools

import jax
import jax.numpy as jnp
from jax import lax
from jax.experimental import pallas as pl
from jax.experimental.pallas import tpu as pltpu
from jax.sharding import PartitionSpec as P

C = 2


def pack_kernel(base_ref, owner_ref, ent_ref, out_ref, staged, seen, load_sems, store_sem):
    count = ent_ref.shape[0]
    parts = load_sems.shape[0]
    size = count // parts
    loads = []
    for p in range(parts):
        rows = pl.ds(p * size, size)
        loads.append(pltpu.make_async_copy(ent_ref.at[rows], staged.at[rows], load_sems.at[p]))
        loads[-1].start()

    def clear(i, carry):
        seen[i] = 0
        return carry

    def issue(i, carry):
        owner = owner_ref[base_ref[0] + i]
        rank = seen[owner]
        seen[owner] = rank + 1
        slot = owner * C + rank
        pltpu.make_async_copy(staged.at[i], out_ref.at[slot], store_sem).start()
        return carry

    lax.fori_loop(0, seen.shape[0], clear, 0, unroll=8)
    for p in range(parts):
        loads[p].wait()
        lax.fori_loop(p * size, (p + 1) * size, issue, 0)
    pltpu.make_async_copy(staged, out_ref.at[pl.ds(0, count)], store_sem).wait()


def pack(ent_blocks, ent_owner, base, device_count):
    return pl.pallas_call(
        pack_kernel,
        out_shape=jax.ShapeDtypeStruct(
            (device_count * C,) + ent_blocks.shape[1:], ent_blocks.dtype
        ),
        in_specs=[
            pl.BlockSpec(memory_space=pltpu.SMEM),
            pl.BlockSpec(memory_space=pltpu.SMEM),
            pl.BlockSpec(memory_space=pl.ANY),
        ],
        out_specs=pl.BlockSpec(memory_space=pl.ANY),
        scratch_shapes=[
            pltpu.VMEM(ent_blocks.shape, ent_blocks.dtype),
            pltpu.SMEM((device_count,), jnp.int32),
            pltpu.SemaphoreType.DMA((4,)),
            pltpu.SemaphoreType.DMA,
        ],
        name="pack",
    )(base, ent_owner, ent_blocks)


def admit_kernel(spans, first_ref, order_ref, source_ref, density_ref, received_ref, *refs):
    part_refs, own, sems = refs[: len(spans)], refs[len(spans)], refs[len(spans) + 1]

    def add(j, total):
        return total + received_ref[order_ref[j]].astype(jnp.float32)

    def place(p, carry):
        t = source_ref[p]
        total = lax.fori_loop(
            first_ref[t], first_ref[t + 1], add, density_ref[t].astype(jnp.float32)
        )
        own[p] = total.astype(own.dtype)
        return carry

    copies = []
    done = 0
    for i, (low, high) in enumerate(spans):
        if high > done:
            lax.fori_loop(max(low, done), high, place, 0)
            done = high
        copies.append(pltpu.make_async_copy(own.at[pl.ds(low, high - low)], part_refs[i], sems.at[i]))
        copies[-1].start()
    for copy in copies:
        copy.wait()


def admit(density, received, first, order, source, spans):
    return pl.pallas_call(
        functools.partial(admit_kernel, spans),
        out_shape=[
            jax.ShapeDtypeStruct((high - low,) + density.shape[1:], density.dtype)
            for low, high in spans
        ],
        in_specs=[pl.BlockSpec(memory_space=pltpu.SMEM)] * 3
        + [pl.BlockSpec(memory_space=pltpu.VMEM)] * 2,
        out_specs=[pl.BlockSpec(memory_space=pl.ANY)] * len(spans),
        scratch_shapes=[
            pltpu.VMEM(density.shape, density.dtype),
            pltpu.SemaphoreType.DMA((len(spans),)),
        ],
        compiler_params=pltpu.CompilerParams(vmem_limit_bytes=16 << 20),
        name="admit",
    )(first, order, source, density, received)


def reach(part):
    wide, narrow = divmod(part, 3)
    wides = (0, 1, 2) if wide == 0 else (0, wide)
    narrows = (0, 1, 2) if narrow == 0 else (0, narrow)
    return [w * 3 + n for w in wides for n in narrows]


NEAR_PARTS = 6


def near_count(part):
    return len([q for q in reach(part) if q < NEAR_PARTS])


def far_count(part):
    return len(reach(part)) - near_count(part)


def load_pieces(pieces, piece_starts, table, sems):
    copies = []
    for i, (piece, start) in enumerate(zip(pieces, piece_starts)):
        copies.append(
            pltpu.make_async_copy(piece, table.at[pl.ds(start, piece.shape[0])], sems.at[i])
        )
        copies[-1].start()
    return copies


def lanes_of(ref, parts, group):
    return jnp.concatenate([ref[:, q * group:(q + 1) * group] for q in parts], axis=1)


def near_kernel(row_count, width, piece_starts, table_size, pos_ref, *refs):
    pieces = refs[: len(piece_starts)]
    outs = refs[len(piece_starts):]
    grids, (square, left_far, table, left, sems) = outs[:9], outs[9:]
    near = 9 * row_count
    group = row_count * width
    copies = load_pieces(pieces, piece_starts, table, sems)
    table[table_size] = jnp.zeros((width, width), table.dtype)
    for copy in copies:
        copy.wait()

    def block(m, k):
        return table[jnp.minimum(pos_ref[m * near + k], table_size)]

    for r in range(row_count):
        for k in range(near):
            left[r * width:(r + 1) * width, k * width:(k + 1) * width] = block(r, k)
    left_far[...] = left[:, NEAR_PARTS * group:]
    for part in range(9):
        parts = [q for q in reach(part) if q < NEAR_PARTS]
        for i, q in enumerate(parts):
            for r in range(row_count):
                for k in range(row_count):
                    low = (i * row_count + r) * width
                    grids[part][low:low + width, k * width:(k + 1) * width] = block(
                        q * row_count + r, part * row_count + k
                    )
        square[part] = jnp.dot(
            lanes_of(left, parts, group), grids[part][...], preferred_element_type=jnp.float32
        )


def square_near(positions, pieces, piece_starts, table_size, row_count, width):
    group = row_count * width
    span = 9 * group
    return pl.pallas_call(
        functools.partial(near_kernel, row_count, width, piece_starts, table_size),
        out_shape=[
            pltpu.VMEM((near_count(part) * group, group), jnp.bfloat16) for part in range(9)
        ] + [
            pltpu.VMEM((9, group, group), jnp.float32),
            pltpu.VMEM((group, (9 - NEAR_PARTS) * group), jnp.bfloat16),
        ],
        in_specs=[pl.BlockSpec(memory_space=pltpu.SMEM)]
        + [pl.BlockSpec(memory_space=pl.ANY)] * len(pieces),
        out_specs=[pl.BlockSpec(memory_space=pltpu.VMEM)] * 11,
        scratch_shapes=[
            pltpu.VMEM((table_size + 1, width, width), jnp.bfloat16),
            pltpu.VMEM((group, span), jnp.bfloat16),
            pltpu.SemaphoreType.DMA((len(pieces),)),
        ],
        compiler_params=pltpu.CompilerParams(vmem_limit_bytes=20 << 20),
        name="square_near",
    )(positions, *pieces)


def far_kernel(row_count, width, piece_starts, table_start, table_size, pos_ref, slot_ref, *refs):
    pieces = refs[: len(piece_starts)]
    outs = refs[len(piece_starts):]
    near_grids = outs[:9]
    square_in, left, out_ref, table, grid, square, square_b, staged, sems, out_sem = outs[9:]
    near = 9 * row_count
    group = row_count * width
    zero_at = table_start + table_size
    copies = load_pieces(pieces, piece_starts, table, sems)
    table[table_size] = jnp.zeros((width, width), table.dtype)
    for copy in copies:
        copy.wait()

    for part in range(9):
        parts = reach(part)
        base = near_count(part)
        far_base = sum(far_count(q) for q in range(part)) * group
        for i, q in enumerate(parts[base:]):
            for r in range(row_count):
                for k in range(row_count):
                    low = far_base + (i * row_count + r) * width
                    grid[low:low + width, k * width:(k + 1) * width] = table[
                        pos_ref[(q * row_count + r) * near + part * row_count + k] - table_start
                    ]
        product = square_in[part]
        if base < len(parts):
            product = product + jnp.dot(
                lanes_of(left, [q - NEAR_PARTS for q in parts[base:]], group),
                grid[far_base:far_base + far_count(part) * group],
                preferred_element_type=jnp.float32,
            )
        square[part] = product
        for r in range(row_count):
            for k in range(row_count):
                listed = pos_ref[r * near + part * row_count + k] != zero_at
                low = part * group + k * width
                square_b[r * width:(r + 1) * width, low:low + width] = jnp.where(
                    listed, product[r * width:(r + 1) * width, k * width:(k + 1) * width], 0.0
                ).astype(jnp.bfloat16)

    blocks = out_ref.shape[0]
    for part in range(9):
        parts = reach(part)
        base = near_count(part)
        far_base = sum(far_count(q) for q in range(part)) * group
        product = jnp.dot(
            lanes_of(square_b, parts[:base], group), near_grids[part][...],
            preferred_element_type=jnp.float32,
        )
        if base < len(parts):
            product = product + jnp.dot(
                lanes_of(square_b, parts[base:], group),
                grid[far_base:far_base + far_count(part) * group],
                preferred_element_type=jnp.float32,
            )
        result = 3.0 * square[part] - 2.0 * product
        for r in range(row_count):
            for k in range(row_count):
                slot = slot_ref[r * near + part * row_count + k]
                staged[slot] = result[r * width:(r + 1) * width, k * width:(k + 1) * width]

                @pl.when(slot < blocks)
                def _():
                    pltpu.make_async_copy(staged.at[slot], out_ref.at[slot], out_sem).start()

    pltpu.make_async_copy(staged.at[pl.ds(0, blocks)], out_ref, out_sem).wait()


def purify_far(
    positions, out_slots, pieces, piece_starts, carried, table_start, table_size,
    row_count, slot_count, width,
):
    group = row_count * width
    span = 9 * group
    blocks = row_count * slot_count
    return pl.pallas_call(
        functools.partial(
            far_kernel, row_count, width, piece_starts, table_start, table_size
        ),
        out_shape=jax.ShapeDtypeStruct((blocks, width, width), jnp.float32),
        in_specs=[pl.BlockSpec(memory_space=pltpu.SMEM)] * 2
        + [pl.BlockSpec(memory_space=pl.ANY)] * len(pieces)
        + [pl.BlockSpec(memory_space=pltpu.VMEM)] * len(carried),
        out_specs=pl.BlockSpec(memory_space=pl.ANY),
        scratch_shapes=[
            pltpu.VMEM((table_size + 1, width, width), jnp.bfloat16),
            pltpu.VMEM((sum(far_count(part) for part in range(9)) * group, group), jnp.bfloat16),
            pltpu.VMEM((9, group, group), jnp.float32),
            pltpu.VMEM((group, span), jnp.bfloat16),
            pltpu.VMEM((blocks + 1, width, width), jnp.float32),
            pltpu.SemaphoreType.DMA((len(pieces),)),
            pltpu.SemaphoreType.DMA,
        ],
        compiler_params=pltpu.CompilerParams(vmem_limit_bytes=28 << 20),
        name="purify_far",
    )(
        positions, out_slots, *pieces,
        *[pltpu.with_memory_space_constraint(array, pltpu.VMEM) for array in carried],
    )


def block_positions(neighbours, here_x, here_y, starts, zero_at):
    wide_count, narrow_count, row_count, slot_count = neighbours.shape
    total_rows = wide_count * narrow_count * row_count
    listing = neighbours.reshape(total_rows, slot_count)
    ids = jnp.arange(9 * row_count, dtype=jnp.int32)
    wide, narrow, inner = ids // (3 * row_count), ids // row_count % 3, ids % row_count
    beyond = jnp.where(here_x % 2 == 0, here_x + wide_count - 1, here_x + 1) % wide_count
    near_x = jnp.where(wide == 0, here_x, jnp.where(wide == 1, here_x ^ 1, beyond))
    near_y = jnp.where(
        narrow == 0, here_y, jnp.where(narrow == 1, here_y ^ 1, narrow_count - 1 - here_y)
    )
    rows = (near_x * narrow_count + near_y) * row_count + inner
    lists = jnp.take(listing, rows, axis=0)
    list_x = lists // (narrow_count * row_count)
    list_y = lists // row_count % narrow_count
    aside = list_y == (near_y ^ 1)[:, None]
    kind = jnp.where(
        list_x == (near_x ^ 1)[:, None], jnp.where(aside, 2, 3), jnp.where(aside, 1, 0)
    )
    slot_ids = jnp.arange(slot_count, dtype=jnp.int32)
    key = kind * slot_count + slot_ids
    place = jnp.sum((key[:, :, None] > key[:, None, :]).astype(jnp.int32), axis=2)
    part = wide * 3 + narrow
    start = jnp.zeros_like(part)
    for i, value in enumerate(starts):
        start = jnp.where(part == i, value, start)
    held_at = (start + inner)[:, None] + place * row_count
    matches = lists[:, None, :] == rows[None, :, None]
    positions = jnp.min(jnp.where(matches, held_at[:, None, :], zero_at), axis=2)
    own_matches = matches[:row_count]
    own_slots = slot_ids + slot_count * jnp.arange(row_count, dtype=jnp.int32)[:, None, None]
    out_slots = jnp.min(jnp.where(own_matches, own_slots, row_count * slot_count), axis=2)
    order = (place[:row_count] * row_count + inner[:row_count, None]).reshape(-1)
    flat_ids = jnp.arange(row_count * slot_count, dtype=jnp.int32)
    source = jnp.sum(jnp.where(order[None, :] == flat_ids[:, None], flat_ids[None, :], 0), axis=1)
    return (
        positions.astype(jnp.int32).reshape(-1),
        out_slots.astype(jnp.int32).reshape(-1),
        source.astype(jnp.int32),
    )


def per_device(density, neighbours, ent_blocks, ent_owner, ent_place):
    wide_count = lax.axis_size("gx")
    narrow_count = lax.axis_size("gy")
    device_count = wide_count * narrow_count
    here_x = lax.axis_index("gx")
    here_y = lax.axis_index("gy")
    self_index = here_x * narrow_count + here_y
    row_count = density.shape[2]
    slot_count = density.shape[3]
    width = density.shape[4]
    blocks = row_count * slot_count
    held = ent_blocks.shape[0]
    owners = ent_owner.reshape(device_count, held)
    places = ent_place.reshape(device_count, held)

    base = (self_index * held).astype(jnp.int32).reshape(1)
    outgoing = pack(ent_blocks, ent_owner, base, device_count)
    received = lax.all_to_all(
        outgoing.reshape(device_count, C, width, width),
        ("gx", "gy"), split_axis=0, concat_axis=0, tiled=True,
    ).reshape(device_count * C, width, width)

    for_me = (owners == self_index).astype(jnp.int32)
    rank = jnp.cumsum(for_me, axis=1) - for_me
    picked = (for_me[:, :, None] == 1) & (
        rank[:, :, None] == jnp.arange(C, dtype=jnp.int32)[None, None, :]
    )
    slot_place = jnp.sum(jnp.where(picked, places[:, :, None], 0), axis=1).reshape(-1)
    slot_used = jnp.any(picked, axis=1).reshape(-1)
    slot_place = jnp.where(slot_used, slot_place, blocks)
    slot_ids = jnp.arange(device_count * C, dtype=jnp.int32)
    ahead = (slot_place[:, None] > slot_place[None, :]) | (
        (slot_place[:, None] == slot_place[None, :]) & (slot_ids[:, None] > slot_ids[None, :])
    )
    sorted_at = jnp.sum(ahead, axis=1)
    order = jnp.sum(
        jnp.where(sorted_at[None, :] == slot_ids[:, None], slot_ids[None, :], 0), axis=1
    ).astype(jnp.int32)
    target_ids = jnp.arange(blocks + 1, dtype=jnp.int32)
    first = jnp.sum(slot_place[None, :] < target_ids[:, None], axis=1).astype(jnp.int32)

    near_blocks = row_count * min(slot_count, 6 * row_count)
    corner_blocks = row_count * min(slot_count, 4 * row_count)
    sizes = [blocks] * 6 + [near_blocks, near_blocks, corner_blocks]
    starts = [sum(sizes[:i]) for i in range(9)]
    zero_at = sum(sizes)
    positions, out_slots, source = block_positions(neighbours, here_x, here_y, starts, zero_at)

    cut = corner_blocks // 2
    tail = blocks - 6 * row_count
    received, first, order, source, positions, out_slots = lax.optimization_barrier(
        (received, first, order, source, positions, out_slots)
    )
    flat_density = density.reshape(blocks, width, width)
    own_1, own_3, own_t = admit(
        flat_density, received, first, order, source,
        ((0, cut), (2 * cut, blocks), (tail, blocks)),
    )
    (own_2,) = admit(flat_density, received, first, order, source, ((cut, 2 * cut),))

    axes = ("gx", "gy")
    devices = [(x, y) for x in range(wide_count) for y in range(narrow_count)]

    def send(array, target):
        pairs = []
        for x, y in devices:
            to_x, to_y = target(x, y)
            pairs.append((x * narrow_count + y, to_x % wide_count * narrow_count + to_y))
        return lax.ppermute(array, axes, pairs)

    def across(x, y):
        return x, narrow_count - 1 - y

    def chip(x, y):
        return x, y ^ 1

    def ring(x, y):
        return x ^ 1, narrow_count - 1 - y

    def onward(x, y):
        return (x + 2 if x % 2 == 0 else x - 2), y

    ring_across_1 = send(own_1, ring)
    own_across_1 = send(own_1, across)
    ring_across_2 = send(own_2, ring)
    own_across_3 = send(own_3, across)
    far_across_1 = send(ring_across_1, onward)
    ring_same_1 = send(ring_across_1, across)
    own_chip_1 = send(own_1, chip)
    far_across_2 = send(ring_across_2[:cut // 2], onward)
    ring_same_2 = send(ring_across_2, across)
    ring_same_3 = send(own_across_3, ring)
    ring_across_t = send(own_t, ring)
    own_across_2 = send(own_2, across)
    own_chip_2 = send(own_2, chip)
    own_chip_3 = send(own_3, chip)
    far_same_1 = send(ring_same_1, onward)
    ring_chip_1 = send(ring_same_1, chip)
    far_same_3 = send(ring_same_3[:near_blocks - 2 * cut], onward)
    ring_chip_3 = send(ring_same_3, chip)
    far_same_2 = send(ring_same_2, onward)
    ring_chip_2 = send(ring_same_2, chip)
    far_across_3 = send(far_same_2[cut // 2:], across)
    far_chip_1 = send(far_same_1, chip)
    far_chip_3 = send(far_same_3, chip)
    far_chip_2 = send(far_same_2, chip)

    near_pieces = [
        (own_1, 0, 0), (own_2, 0, cut), (own_3, 0, 2 * cut),
        (own_chip_1, 1, 0), (own_chip_2, 1, cut), (own_chip_3, 1, 2 * cut),
        (own_across_1, 2, 0), (own_across_2, 2, cut), (own_across_3, 2, 2 * cut),
        (ring_same_1, 3, 0), (ring_same_2, 3, cut), (ring_same_3, 3, 2 * cut),
        (ring_chip_1, 4, 0), (ring_chip_2, 4, cut), (ring_chip_3, 4, 2 * cut),
        (ring_across_1, 5, 0), (ring_across_2, 5, cut), (ring_across_t, 5, tail),
    ]
    far_pieces = [
        (far_same_1, 6, 0), (far_same_2, 6, cut), (far_same_3, 6, 2 * cut),
        (far_chip_1, 7, 0), (far_chip_2, 7, cut), (far_chip_3, 7, 2 * cut),
        (far_across_1, 8, 0), (far_across_2, 8, cut), (far_across_3, 8, cut + cut // 2),
    ]
    far_start = starts[NEAR_PARTS]
    carried = square_near(
        positions, [piece for piece, _, _ in near_pieces],
        [starts[part] + offset for _, part, offset in near_pieces],
        far_start, row_count, width,
    )
    purified = purify_far(
        positions, out_slots, [piece for piece, _, _ in far_pieces],
        [starts[part] + offset - far_start for _, part, offset in far_pieces],
        carried, far_start, zero_at - far_start, row_count, slot_count, width,
    )
    return purified.reshape(density.shape)


def solution(mesh):
    in_specs = (P("gx", "gy", None, None, None, None), P(), P(("gx", "gy"), None, None), P(), P())
    out_specs = P("gx", "gy", None, None, None, None)
    return jax.shard_map(
        per_device, mesh=mesh, in_specs=in_specs, out_specs=out_specs, check_vma=False
    )
```
